32 devices in a mesh: dp: 8 (over z, y), seq: 4 (over x, core).
Axes of the slice: x: 2, y: 2, z: 4, core: 2. Of those that a mesh axis runs over, the one named last changes fastest.
Arguments:
- mel_frames: bfloat16 [8, 3072, 80], P('dp', 'seq'), may hold values from -6 to 6
- token_ids: int32 [8, 448], P('dp', 'seq'), may hold values from 0 to 26111
- token_counts: int32 [8], P('dp'), may hold values from 1 to 448, as said below
- conv1_weight: bfloat16 [3, 80, 768], P(None, 'seq', 'dp'), may hold values from -0.375 to 0.375
- conv2_weight: bfloat16 [3, 768, 768], P(None, 'dp', 'seq'), may hold values from -0.125 to 0.125
- encoder_attn_gain: bfloat16 [768], P(('dp', 'seq')), may hold values from 0.099609375 to 1.8984375
- encoder_attn_bias: bfloat16 [768], P(('dp', 'seq')), may hold values from -1.5 to 1.5
- encoder_query: bfloat16 [768, 768], P('dp', 'seq'), may hold values from -0.21875 to 0.21875
- encoder_key: bfloat16 [768, 768], P('dp', 'seq'), may hold values from -0.21875 to 0.21875
- encoder_value: bfloat16 [768, 768], P('dp', 'seq'), may hold values from -0.21875 to 0.21875
- encoder_output: bfloat16 [768, 768], P('dp', 'seq'), may hold values from -0.875 to 0.875
- encoder_mlp_gain: bfloat16 [768], P(('dp', 'seq')), may hold values from 0.099609375 to 1.8984375
- encoder_mlp_bias: bfloat16 [768], P(('dp', 'seq')), may hold values from -1.5 to 1.5
- encoder_expand: bfloat16 [768, 3072], P('dp', 'seq'), may hold values from -0.21875 to 0.21875
- encoder_contract: bfloat16 [3072, 768], P('dp', 'seq'), may hold values from -0.109375 to 0.109375
- encoder_final_gain: bfloat16 [768], P(('dp', 'seq')), may hold values from 0.099609375 to 1.8984375
- encoder_final_bias: bfloat16 [768], P(('dp', 'seq')), may hold values from -1.5 to 1.5
- token_table: bfloat16 [26112, 768], P('dp', 'seq'), may hold values from -5 to 5
- position_table: bfloat16 [448, 768], P('dp', 'seq'), may hold values from -2.5 to 2.5
- decoder_attn_gain: bfloat16 [768], P(('dp', 'seq')), may hold values from 0.099609375 to 1.8984375
- decoder_attn_bias: bfloat16 [768], P(('dp', 'seq')), may hold values from -1.5 to 1.5
- decoder_query: bfloat16 [768, 768], P('dp', 'seq'), may hold values from -0.21875 to 0.21875
- decoder_key: bfloat16 [768, 768], P('dp', 'seq'), may hold values from -0.21875 to 0.21875
- decoder_value: bfloat16 [768, 768], P('dp', 'seq'), may hold values from -0.21875 to 0.21875
- decoder_output: bfloat16 [768, 768], P('dp', 'seq'), may hold values from -0.625 to 0.625
- cross_attn_gain: bfloat16 [768], P(('dp', 'seq')), may hold values from 0.099609375 to 1.8984375
- cross_attn_bias: bfloat16 [768], P(('dp', 'seq')), may hold values from -1.5 to 1.5
- cross_query: bfloat16 [768, 768], P('dp', 'seq'), may hold values from -0.21875 to 0.21875
- cross_key: bfloat16 [768, 768], P('dp', 'seq'), may hold values from -0.21875 to 0.21875
- cross_value: bfloat16 [768, 768], P('dp', 'seq'), may hold values from -0.21875 to 0.21875
- cross_output: bfloat16 [768, 768], P('dp', 'seq'), may hold values from -0.875 to 0.875
- decoder_mlp_gain: bfloat16 [768], P(('dp', 'seq')), may hold values from 0.099609375 to 1.8984375
- decoder_mlp_bias: bfloat16 [768], P(('dp', 'seq')), may hold values from -1.5 to 1.5
- decoder_expand: bfloat16 [768, 3072], P('dp', 'seq'), may hold values from -0.21875 to 0.21875
- decoder_contract: bfloat16 [3072, 768], P('dp', 'seq'), may hold values from -0.109375 to 0.109375
- cotangent: bfloat16 [8, 448, 768], P('dp', 'seq'), may hold values from -6 to 6
Outputs:
- decoded: bfloat16 [8, 448, 768], P('dp', 'seq')
- mel_grad: float32 [8, 3072, 80], P('dp', 'seq')
- grad_conv1_weight: float32 [3, 80, 768], P(None, 'seq', 'dp')
- grad_conv2_weight: float32 [3, 768, 768], P(None, 'dp', 'seq')
- grad_encoder_attn_gain: float32 [768], P(('dp', 'seq'))
- grad_encoder_attn_bias: float32 [768], P(('dp', 'seq'))
- grad_encoder_query: float32 [768, 768], P('dp', 'seq')
- grad_encoder_key: float32 [768, 768], P('dp', 'seq')
- grad_encoder_value: float32 [768, 768], P('dp', 'seq')
- grad_encoder_output: float32 [768, 768], P('dp', 'seq')
- grad_encoder_mlp_gain: float32 [768], P(('dp', 'seq'))
- grad_encoder_mlp_bias: float32 [768], P(('dp', 'seq'))
- grad_encoder_expand: float32 [768, 3072], P('dp', 'seq')
- grad_encoder_contract: float32 [3072, 768], P('dp', 'seq')
- grad_encoder_final_gain: float32 [768], P(('dp', 'seq'))
- grad_encoder_final_bias: float32 [768], P(('dp', 'seq'))
- grad_token_table: float32 [26112, 768], P('dp', 'seq')
- grad_position_table: float32 [448, 768], P('dp', 'seq')
- grad_decoder_attn_gain: float32 [768], P(('dp', 'seq'))
- grad_decoder_attn_bias: float32 [768], P(('dp', 'seq'))
- grad_decoder_query: float32 [768, 768], P('dp', 'seq')
- grad_decoder_key: float32 [768, 768], P('dp', 'seq')
- grad_decoder_value: float32 [768, 768], P('dp', 'seq')
- grad_decoder_output: float32 [768, 768], P('dp', 'seq')
- grad_cross_attn_gain: float32 [768], P(('dp', 'seq'))
- grad_cross_attn_bias: float32 [768], P(('dp', 'seq'))
- grad_cross_query: float32 [768, 768], P('dp', 'seq')
- grad_cross_key: float32 [768, 768], P('dp', 'seq')
- grad_cross_value: float32 [768, 768], P('dp', 'seq')
- grad_cross_output: float32 [768, 768], P('dp', 'seq')
- grad_decoder_mlp_gain: float32 [768], P(('dp', 'seq'))
- grad_decoder_mlp_bias: float32 [768], P(('dp', 'seq'))
- grad_decoder_expand: float32 [768, 3072], P('dp', 'seq')
- grad_decoder_contract: float32 [3072, 768], P('dp', 'seq')
The draws below stay inside these ranges and needn't reach their ends.
Inputs may be any that keep to these rules, and one draw needn't show every extreme that they name: `token_counts`: each clip's number of live decoder slots; in every draw some clip has 448.
All inputs are finite; a program needn't handle non-finite values.
Results may differ from the reference program's by a relative error of at most 0.03.
Values may be sent and summed in bfloat16 or wider, within the bound.
A program may use at most 576 MiB of HBM per device.

```python
import math
import jax
import jax.numpy as jnp
import numpy as np
from jax import lax

D = 768
HEADS = 12
HEAD = 64
FF = 3072
MELS = 80
DEC = 448
VOCAB = 26112
FRAMES = 1536
MEL = 3072
CLIPS = 8


def draw_token_counts(key, part):
    key_low = jax.random.fold_in(key, 11)
    key_high = jax.random.fold_in(key, 12)
    key_pick = jax.random.fold_in(key, 13)
    lower_draw = jax.random.randint(key_low, (CLIPS,), 1, DEC + 1)
    upper_draw = jax.random.randint(key_high, (CLIPS,), 1, DEC + 1)
    chosen = jax.random.randint(key_pick, (), 0, CLIPS)
    larger = jnp.maximum(lower_draw, upper_draw)
    return jnp.where(jnp.arange(CLIPS) == chosen, DEC, larger).astype(jnp.int32)


def touch_ends(values, own_key, least, largest):
    longest = values.shape.index(max(values.shape))
    spots = []
    for shift in (0, 1):
        where = [jax.random.randint(jax.random.fold_in(own_key, axis), (), 0, length) for axis, length in enumerate(values.shape)]
        where[longest] = (where[longest] + shift) % values.shape[longest]
        spots.append(tuple(where))
    return values.at[spots[0]].set(least).at[spots[1]].set(largest)


def level_of(stream_key, extent, shards, smallest, high):
    def one(position, blocks):
        draws = jax.random.uniform(jax.random.fold_in(jax.random.fold_in(stream_key, 6), position), (blocks,), jnp.float32, smallest / len(shards), high / len(shards))
        return jnp.repeat(jnp.exp(draws), extent[position] // blocks).reshape((-1,) + (1,) * (len(extent) - position - 1))

    factor_of = one(*shards[0])
    for cut in shards[1:]:
        factor_of = factor_of * one(*cut)
    return factor_of


def rank_table(count, lean):
    weights = [(1 << 20) // math.isqrt(standing ** lean) + 1 for standing in range(1, count + 1)]
    scale = 1 + sum(weights) // (1 << 30)
    return np.cumsum(np.array([max(1, weight // scale) for weight in weights]))


def ranked(rng, shape, count, skew):
    grid = rank_table(count, skew)
    lot = jax.random.randint(jax.random.fold_in(rng, 1), shape, 0, int(grid[count - 1]))
    rank = jnp.searchsorted(jnp.asarray(grid, jnp.int32), lot, side="right")
    return jax.random.permutation(jax.random.fold_in(rng, 2), count)[rank].astype(jnp.int32)


def scatter_about(rng, extent, width, limit, split=(), dtype=jnp.bfloat16):
    values = jax.random.normal(rng, extent, jnp.float32) * width
    if len(split) > 0:
        values = level_of(rng, extent, split, -0.22, 0.18) * values
    return jnp.clip(values, min=-limit, max=limit).astype(dtype)


def setup_inputs(seed: int = 0) -> dict:
    arg_keys = jax.random.split(jax.random.key(seed), 37)
    mel_frames = scatter_about(arg_keys[0], (CLIPS, MEL, MELS), 1.0, 6.0, ((0, 8), (1, 4)))
    token_ids = touch_ends(ranked(arg_keys[1], (CLIPS, DEC), VOCAB, 2), jax.random.fold_in(arg_keys[1], 3), 0, VOCAB - 1).astype(jnp.int32)
    token_counts = draw_token_counts(jax.random.fold_in(arg_keys[36], 71), 0)
    conv1_weight = scatter_about(arg_keys[3], (3, MELS, D), (3 * MELS) ** -0.5, 0.375, ((1, 4), (2, 8)))
    conv2_weight = scatter_about(arg_keys[4], (3, D, D), (3 * D) ** -0.5, 0.125, ((1, 8), (2, 4)))
    encoder_attn_gain = jnp.clip(1.0 + 0.18 * jax.random.normal(arg_keys[5], (D,), jnp.float32), 0.099609375, 1.8984375).astype(jnp.bfloat16)
    encoder_attn_bias = scatter_about(arg_keys[6], (D,), 0.3, 1.5, ((0, 32),))
    encoder_query = scatter_about(arg_keys[7], (D, D), D ** -0.5, 0.21875, ((0, 8), (1, 4)))
    encoder_key = scatter_about(arg_keys[8], (D, D), D ** -0.5, 0.21875, ((0, 8), (1, 4)))
    encoder_value = scatter_about(arg_keys[9], (D, D), D ** -0.5, 0.21875, ((0, 8), (1, 4)))
    encoder_output = scatter_about(arg_keys[10], (D, D), (D // 16) ** -0.5, 0.875, ((0, 8), (1, 4)))
    encoder_mlp_gain = jnp.clip(1.0 + 0.18 * jax.random.normal(arg_keys[11], (D,), jnp.float32), 0.099609375, 1.8984375).astype(jnp.bfloat16)
    encoder_mlp_bias = scatter_about(arg_keys[12], (D,), 0.3, 1.5, ((0, 32),))
    encoder_expand = scatter_about(arg_keys[13], (D, FF), D ** -0.5, 0.21875, ((0, 8), (1, 4)))
    encoder_contract = scatter_about(arg_keys[14], (FF, D), FF ** -0.5, 0.109375, ((0, 8), (1, 4)))
    encoder_final_gain = jnp.clip(1.0 + 0.18 * jax.random.normal(arg_keys[15], (D,), jnp.float32), 0.099609375, 1.8984375).astype(jnp.bfloat16)
    encoder_final_bias = scatter_about(arg_keys[16], (D,), 0.3, 1.5, ((0, 32),))
    token_table = scatter_about(arg_keys[17], (VOCAB, D), 1.0, 5.0, ((0, 8), (1, 4)))
    position_table = scatter_about(arg_keys[18], (DEC, D), 0.5, 2.5, ((0, 8), (1, 4)))
    decoder_attn_gain = jnp.clip(1.0 + 0.18 * jax.random.normal(arg_keys[19], (D,), jnp.float32), 0.099609375, 1.8984375).astype(jnp.bfloat16)
    decoder_attn_bias = scatter_about(arg_keys[20], (D,), 0.3, 1.5, ((0, 32),))
    decoder_query = scatter_about(arg_keys[21], (D, D), D ** -0.5, 0.21875, ((0, 8), (1, 4)))
    decoder_key = scatter_about(arg_keys[22], (D, D), D ** -0.5, 0.21875, ((0, 8), (1, 4)))
    decoder_value = scatter_about(arg_keys[23], (D, D), D ** -0.5, 0.21875, ((0, 8), (1, 4)))
    decoder_output = scatter_about(arg_keys[24], (D, D), (D // 8) ** -0.5, 0.625, ((0, 8), (1, 4)))
    cross_attn_gain = jnp.clip(1.0 + 0.18 * jax.random.normal(arg_keys[25], (D,), jnp.float32), 0.099609375, 1.8984375).astype(jnp.bfloat16)
    cross_attn_bias = scatter_about(arg_keys[26], (D,), 0.3, 1.5, ((0, 32),))
    cross_query = scatter_about(arg_keys[27], (D, D), D ** -0.5, 0.21875, ((0, 8), (1, 4)))
    cross_key = scatter_about(arg_keys[28], (D, D), D ** -0.5, 0.21875, ((0, 8), (1, 4)))
    cross_value = scatter_about(arg_keys[29], (D, D), D ** -0.5, 0.21875, ((0, 8), (1, 4)))
    cross_output = scatter_about(arg_keys[30], (D, D), (D // 16) ** -0.5, 0.875, ((0, 8), (1, 4)))
    decoder_mlp_gain = jnp.clip(1.0 + 0.18 * jax.random.normal(arg_keys[31], (D,), jnp.float32), 0.099609375, 1.8984375).astype(jnp.bfloat16)
    decoder_mlp_bias = scatter_about(arg_keys[32], (D,), 0.3, 1.5, ((0, 32),))
    decoder_expand = scatter_about(arg_keys[33], (D, FF), D ** -0.5, 0.21875, ((0, 8), (1, 4)))
    decoder_contract = scatter_about(arg_keys[34], (FF, D), FF ** -0.5, 0.109375, ((0, 8), (1, 4)))
    cotangent = scatter_about(arg_keys[35], (CLIPS, DEC, D), 1.0, 6.0, ((0, 8), (1, 4)))
    return dict(mel_frames=mel_frames, token_ids=token_ids, token_counts=token_counts, conv1_weight=conv1_weight, conv2_weight=conv2_weight, encoder_attn_gain=encoder_attn_gain, encoder_attn_bias=encoder_attn_bias, encoder_query=encoder_query, encoder_key=encoder_key, encoder_value=encoder_value, encoder_output=encoder_output, encoder_mlp_gain=encoder_mlp_gain, encoder_mlp_bias=encoder_mlp_bias, encoder_expand=encoder_expand, encoder_contract=encoder_contract, encoder_final_gain=encoder_final_gain, encoder_final_bias=encoder_final_bias, token_table=token_table, position_table=position_table, decoder_attn_gain=decoder_attn_gain, decoder_attn_bias=decoder_attn_bias, decoder_query=decoder_query, decoder_key=decoder_key, decoder_value=decoder_value, decoder_output=decoder_output, cross_attn_gain=cross_attn_gain, cross_attn_bias=cross_attn_bias, cross_query=cross_query, cross_key=cross_key, cross_value=cross_value, cross_output=cross_output, decoder_mlp_gain=decoder_mlp_gain, decoder_mlp_bias=decoder_mlp_bias, decoder_expand=decoder_expand, decoder_contract=decoder_contract, cotangent=cotangent)


EPSILON = 1e-05
NEGATIVE = -1e+30

@jax.custom_vjp
def low(v):
    return lax.optimization_barrier(v.astype(jnp.bfloat16)).astype(jnp.float32)

@jax.custom_vjp
def low_back(v):
    return v

def low_keep(v):
    return (low(v), None)

def low_pass(kept, grad):
    return (grad,)

def back_keep(v):
    return (v, None)

def back_low(kept, grad):
    return (low(grad),)
low.defvjp(low_keep, low_pass)
low_back.defvjp(back_keep, back_low)

def round_both(values):
    return low_back(low(values))

def product(left_side, right_side):
    return jnp.dot(left_side, right_side, precision=lax.Precision.HIGHEST, preferred_element_type=jnp.float32)

def layer_norm(values, norm_gain, norm_bias):
    center = values - lax.optimization_barrier(jnp.mean(values, axis=-1, keepdims=True))
    spread = lax.optimization_barrier(jnp.mean(center * center, axis=-1, keepdims=True))
    return center * lax.rsqrt(spread + EPSILON) * norm_gain + norm_bias

def gelu_exact(values):
    return jax.nn.gelu(values, approximate=False)

def sinusoid(first_frame, frame_count):
    half_width = D // 2
    frequency = jnp.exp(jnp.arange(half_width).astype(jnp.float32) * (-math.log(10000.0) / (half_width - 1)))
    places = (first_frame + jnp.arange(frame_count)).astype(jnp.float32)
    angles = places[:, None] * frequency[None, :]
    return jnp.concatenate([jnp.sin(angles), jnp.cos(angles)], axis=1)

def attention(queries, key_rows, value_rows, allowed, out_weight):
    query_count = queries.shape[0]
    key_count = key_rows.shape[0]
    scores = jnp.einsum('qhd,khd->hqk', queries.reshape(query_count, HEADS, HEAD), key_rows.reshape(key_count, HEADS, HEAD), precision=lax.Precision.HIGHEST)
    scores = low_back(scores)
    if allowed is not None:
        scores = jnp.where(allowed[None], scores, NEGATIVE)
    lifted = jnp.exp(scores - lax.optimization_barrier(jnp.max(scores, axis=-1, keepdims=True)))
    probability = low(lifted / lax.optimization_barrier(jnp.sum(lifted, axis=-1, keepdims=True)))
    mixture = jnp.einsum('hqk,khd->qhd', probability, value_rows.reshape(key_count, HEADS, HEAD), precision=lax.Precision.HIGHEST)
    mixture = round_both(mixture.reshape(query_count, HEADS * HEAD))
    return low_back(product(mixture, out_weight))

def feed_forward(normed, expand, contract):
    pre_act = low_back(product(normed, expand))
    hidden = round_both(gelu_exact(pre_act))
    return low_back(product(hidden, contract))

def clip_forward(weight_list, mel_clip, ids_clip, count_clip):
    conv1_weight, conv2_weight, encoder_attn_gain, encoder_attn_bias, encoder_query, encoder_key, encoder_value, encoder_output, encoder_mlp_gain, encoder_mlp_bias, encoder_expand, encoder_contract, encoder_final_gain, encoder_final_bias, token_table, position_table, decoder_attn_gain, decoder_attn_bias, decoder_query, decoder_key, decoder_value, decoder_output, cross_attn_gain, cross_attn_bias, cross_query, cross_key, cross_value, cross_output, decoder_mlp_gain, decoder_mlp_bias, decoder_expand, decoder_contract = weight_list
    query_scale = 1.0 / math.sqrt(HEAD)
    mel_padded = jnp.pad(mel_clip, ((1, 1), (0, 0)))
    first_pre = low_back(sum((product(mel_padded[offset:offset + MEL], conv1_weight[offset]) for offset in range(3))))
    first_act = round_both(gelu_exact(first_pre))
    act_padded = jnp.pad(first_act, ((1, 1), (0, 0)))
    second_pre = low_back(sum((product(act_padded[offset:offset + 2 * FRAMES:2], conv2_weight[offset]) for offset in range(3))))
    stream0 = gelu_exact(second_pre) + sinusoid(0, FRAMES)
    normed = low(layer_norm(stream0, encoder_attn_gain, encoder_attn_bias))
    queries = round_both(product(normed, encoder_query) * query_scale)
    key_rows = round_both(product(normed, encoder_key))
    value_rows = round_both(product(normed, encoder_value))
    stream1 = stream0 + attention(queries, key_rows, value_rows, None, encoder_output)
    stream2 = stream1 + feed_forward(low(layer_norm(stream1, encoder_mlp_gain, encoder_mlp_bias)), encoder_expand, encoder_contract)
    memory = low(layer_norm(stream2, encoder_final_gain, encoder_final_bias))
    memory_keys = round_both(product(memory, cross_key))
    memory_values = round_both(product(memory, cross_value))
    slot_index = jnp.arange(DEC)
    live_slots = slot_index < count_clip
    allowed = (slot_index[None, :] <= slot_index[:, None]) & live_slots[None, :]
    embedded = token_table[ids_clip] + position_table
    normed = low(layer_norm(embedded, decoder_attn_gain, decoder_attn_bias))
    queries = round_both(product(normed, decoder_query) * query_scale)
    key_rows = round_both(product(normed, decoder_key))
    value_rows = round_both(product(normed, decoder_value))
    stream4 = embedded + attention(queries, key_rows, value_rows, allowed, decoder_output)
    normed = low(layer_norm(stream4, cross_attn_gain, cross_attn_bias))
    queries = round_both(product(normed, cross_query) * query_scale)
    stream5 = stream4 + attention(queries, memory_keys, memory_values, None, cross_output)
    stream6 = stream5 + feed_forward(low(layer_norm(stream5, decoder_mlp_gain, decoder_mlp_bias)), decoder_expand, decoder_contract)
    return jnp.where(live_slots[:, None], stream6, 0.0)

def reference(mel_frames, token_ids, token_counts, conv1_weight, conv2_weight, encoder_attn_gain, encoder_attn_bias, encoder_query, encoder_key, encoder_value, encoder_output, encoder_mlp_gain, encoder_mlp_bias, encoder_expand, encoder_contract, encoder_final_gain, encoder_final_bias, token_table, position_table, decoder_attn_gain, decoder_attn_bias, decoder_query, decoder_key, decoder_value, decoder_output, cross_attn_gain, cross_attn_bias, cross_query, cross_key, cross_value, cross_output, decoder_mlp_gain, decoder_mlp_bias, decoder_expand, decoder_contract, cotangent):
    weight_list = [entry.astype(jnp.float32) for entry in (conv1_weight, conv2_weight, encoder_attn_gain, encoder_attn_bias, encoder_query, encoder_key, encoder_value, encoder_output, encoder_mlp_gain, encoder_mlp_bias, encoder_expand, encoder_contract, encoder_final_gain, encoder_final_bias, token_table, position_table, decoder_attn_gain, decoder_attn_bias, decoder_query, decoder_key, decoder_value, decoder_output, cross_attn_gain, cross_attn_bias, cross_query, cross_key, cross_value, cross_output, decoder_mlp_gain, decoder_mlp_bias, decoder_expand, decoder_contract)]

    def one_clip(running, clip_inputs):
        mel_clip, ids_clip, count_clip, cot_clip = clip_inputs

        def closed(weights_in, mel_in):
            return clip_forward(weights_in, mel_in, ids_clip, count_clip)
        output, puller = jax.vjp(closed, weight_list, mel_clip.astype(jnp.float32))
        weight_grads, mel_grad = puller(cot_clip.astype(jnp.float32))
        running = [previous + current for previous, current in zip(running, weight_grads)]
        return (running, (output.astype(jnp.bfloat16), mel_grad))
    start_sums = [jnp.zeros_like(entry) for entry in weight_list]
    totals, (decoded, mel_grad) = lax.scan(one_clip, start_sums, (mel_frames, token_ids, token_counts, cotangent))
    return (decoded, mel_grad, totals[0], totals[1], totals[2], totals[3], totals[4], totals[5], totals[6], totals[7], totals[8], totals[9], totals[10], totals[11], totals[12], totals[13], totals[14], totals[15], totals[16], totals[17], totals[18], totals[19], totals[20], totals[21], totals[22], totals[23], totals[24], totals[25], totals[26], totals[27], totals[28], totals[29], totals[30], totals[31])
```

```python
import functools
import math

import jax
import jax.numpy as jnp
from jax import lax
from jax.experimental import pallas as pl
from jax.experimental.pallas import tpu as pltpu
from jax.sharding import PartitionSpec as P

D = 768
HEADS = 12
HEAD = 64
EPSILON = 1e-05
NEGATIVE = -1e30
SCALE = 1.0 / math.sqrt(HEAD)
BF = jnp.bfloat16
F32 = jnp.float32
BOTH = ("dp", "seq")

KINDS = "12vvmmmmvvmmvvtmvvmmmmvvmmmmvvmm"


def dot(a, b, ca, cb, out=F32):
    return lax.dot_general(a, b, (((ca,), (cb,)), ((), ())), preferred_element_type=F32).astype(out)


def mm(a, b, out=F32):
    return dot(a, b, 1, 0, out)


def mm_t(a, b, out=F32):
    return dot(a, b, 1, 1, out)


def outer(a, b, out=BF):
    return dot(a, b, 0, 0, out)


def norm_parts(values):
    center = values - jnp.mean(values, axis=-1, keepdims=True)
    spread = jnp.mean(center * center, axis=-1, keepdims=True)
    inv = lax.rsqrt(spread + EPSILON)
    return center * inv, inv


def norm(values, gain, bias):
    return (norm_parts(values)[0] * gain + bias).astype(BF)


def norm_back(values, gain, up):
    hat, inv = norm_parts(values)
    g = up * gain
    back = inv * (
        g - jnp.mean(g, axis=-1, keepdims=True) - hat * jnp.mean(g * hat, axis=-1, keepdims=True)
    )
    return back, jnp.sum(up * hat, axis=0), jnp.sum(up, axis=0)


def gelu(v):
    return v * (0.5 + 0.5 * lax.erf(v * math.sqrt(0.5)))


def gelu_slope(v):
    return (0.5 + 0.5 * lax.erf(v * math.sqrt(0.5))) + v * jnp.exp(-0.5 * v * v) * (
        1.0 / math.sqrt(2.0 * math.pi)
    )


def mlp(normed, expand, contract):
    wide = expand.shape[2]
    pre, hidden, out = [], [], 0.0
    for s in range(expand.shape[0]):
        pre.append(mm(normed, expand[s]))
        hidden.append(gelu(pre[s]).astype(BF))
        out = out + mm(hidden[s], contract[s * wide : (s + 1) * wide])
    return pre, hidden, out


def low(v):
    return lax.reduce_precision(v, 8, 7)


def heads(v):
    return v.reshape(v.shape[0], HEADS, HEAD)


def bdot(a, b, ca, cb, ba, bb):
    return lax.dot_general(a, b, (((ca,), (cb,)), ((ba,), (bb,))), preferred_element_type=F32)


def scores_of(q, k, allowed):
    s = bdot(heads(q), heads(k), 2, 2, 1, 1)
    return s if allowed is None else jnp.where(allowed, s, NEGATIVE)


def attend(q, k, v, allowed=None):
    s = scores_of(q, k, allowed)
    top = jnp.max(s, axis=-1, keepdims=True)
    e = jnp.exp(s - top)
    total = jnp.sum(e, axis=-1, keepdims=True)
    o = bdot((e / total).astype(BF), heads(v), 2, 0, 0, 1)
    o = o.transpose(1, 0, 2).reshape(q.shape)
    return o, (top + jnp.log(total))[..., 0].T


def attend_back(q, k, v, allowed, lse, up, total=lambda v: v):
    s = scores_of(q, k, allowed)
    p = jnp.exp(s - lse.T[:, :, None])
    dv = bdot(p.astype(BF), heads(up), 1, 0, 0, 1)
    dp = bdot(heads(up), heads(v), 2, 2, 1, 1)
    mass = total(jnp.sum(p, axis=-1, keepdims=True))
    inner = total(jnp.sum(p * dp, axis=-1, keepdims=True)) / mass
    ds = (p * (dp - inner)).astype(BF)
    dq = bdot(ds, heads(k), 2, 0, 0, 1)
    dk = bdot(ds, heads(q), 1, 0, 0, 1)
    flat = lambda a, like: a.transpose(1, 0, 2).reshape(like.shape)
    return flat(dq, q), flat(dk, k), flat(dv, v)


def pack(rows, extras):
    cols = [rows.astype(F32)] + extras
    wide = sum(c.shape[1] for c in cols)
    return jnp.concatenate(cols + [jnp.zeros((rows.shape[0], -wide % 128), F32)], axis=1)


def unpack(packed, count):
    return packed[..., :D], [
        packed[..., D + i * HEADS : D + (i + 1) * HEADS] for i in range(count)
    ]


def shift(v, axis, step):
    n = lax.axis_size(axis)
    return lax.ppermute(v, axis, [(i, i + step) for i in range(n) if 0 <= i + step < n])


def extended(x, width):
    before = shift(x[-width:], "seq", 1)
    after = shift(x[:width], "seq", -1)
    return jnp.concatenate([before, x, after], axis=0)


def exchange(v):
    n = lax.axis_size("seq")
    got = lax.all_to_all(v, "seq", split_axis=0, concat_axis=0, tiled=True)
    return got.reshape(n, v.shape[0] // n, v.shape[1])


def sinusoid(first_frame, frame_count):
    half = D // 2
    frequency = jnp.exp(jnp.arange(half).astype(F32) * (-math.log(10000.0) / (half - 1)))
    places = (first_frame + jnp.arange(frame_count)).astype(F32)
    angles = places[:, None] * frequency[None, :]
    return jnp.concatenate([jnp.sin(angles), jnp.cos(angles)], axis=1)


def to_whole(flat, shape, kind, dps, seqs):
    if kind == "v":
        return flat.reshape(-1)
    if kind == "1":
        t, i, o = shape
        return (
            flat.reshape(dps, seqs, t, i, o)
            .transpose(2, 1, 3, 0, 4)
            .reshape(t, seqs * i, dps * o)
        )
    if kind == "2":
        t, i, o = shape
        return (
            flat.reshape(dps, seqs, t, i, o)
            .transpose(2, 0, 3, 1, 4)
            .reshape(t, dps * i, seqs * o)
        )
    r, c = shape
    return flat.reshape(dps, seqs, r, c).transpose(0, 2, 1, 3).reshape(dps * r, seqs * c)


def to_owner(g, kind, dps, seqs):
    n = dps * seqs
    if kind == "v":
        return g.reshape(n, -1)
    if kind == "1":
        t, i, o = g.shape
        g = g.reshape(t, seqs, i // seqs, dps, o // dps).transpose(3, 1, 0, 2, 4)
    elif kind == "2":
        t, i, o = g.shape
        g = g.reshape(t, dps, i // dps, seqs, o // seqs).transpose(1, 3, 0, 2, 4)
    else:
        r, c = g.shape
        g = g.reshape(dps, r // dps, seqs, c // seqs).transpose(0, 2, 1, 3)
    return g.reshape(n, -1)


def gather_plain(shards):
    dps, seqs = lax.axis_size("dp"), lax.axis_size("seq")
    flat = jnp.concatenate([w.reshape(-1) for w in shards if w is not None])
    got = lax.all_gather(flat[None], BOTH, axis=0, tiled=True)
    out, at = [], 0
    for w, kind in zip(shards, KINDS):
        if w is None:
            out.append(None)
            continue
        out.append(to_whole(got[:, at : at + w.size], w.shape, kind, dps, seqs))
        at += w.size
    for i in BROAD:
        out[i] = out[i].reshape(D, seqs, -1).transpose(1, 0, 2)
    return out


def reduce_plain(grads, shards):
    dps, seqs = lax.axis_size("dp"), lax.axis_size("seq")
    grads = list(grads)
    for i in BROAD:
        grads[i] = grads[i].transpose(1, 0, 2).reshape(D, -1)
    flat = jnp.concatenate(
        [to_owner(g.astype(BF), k, dps, seqs) for g, k in zip(grads, KINDS) if g is not None], axis=1
    )
    own = lax.psum_scatter(flat, BOTH, scatter_dimension=0, tiled=True).astype(F32)[0]
    out, at = [], 0
    for w, g in zip(shards, grads):
        if g is None:
            out.append(None)
            continue
        out.append(own[at : at + w.size].reshape(w.shape))
        at += w.size
    return out


MESH = pl.DeviceIdType.MESH
LANES = 384


def where_am_i():
    d, s = lax.axis_index("dp"), lax.axis_index("seq")
    return d // 2, d % 2, s // 2, s % 2


def partners(z, y, x, c):
    at = lambda z, y, x, c: (z * 2 + y, x * 2 + c)
    zs = [at((z + j) % 4, y, x, c) for j in (1, 2, 3)]
    return zs, at(z, 1 - y, x, c), at(z, y, 1 - x, c), at(z, y, x, 1 - c)


def greet(zs, yp, xp, cp):
    barrier = pltpu.get_barrier_semaphore()
    everyone = zs + [yp, xp, cp]
    for dev in everyone:
        pl.semaphore_signal(barrier, inc=1, device_id=dev, device_id_type=MESH)
    pl.semaphore_wait(barrier, len(everyone))


def remote(src, dst, send, recv, dev):
    return pltpu.make_async_remote_copy(
        src_ref=src, dst_ref=dst, send_sem=send, recv_sem=recv, device_id=dev, device_id_type=MESH
    )


def split_at(i, rows):
    return rows // 2 if rows % 32 == 0 else 16 + 16 * (i % 2)


def lanes(x):
    return pl.ds(pl.multiple_of(x * LANES, LANES), LANES)


def spot(ref, wide, zs, ys, xs, c, rs):
    full = lambda v: slice(None) if v is None else v
    if wide:
        return ref.at[full(xs), c, full(zs), full(ys), rs, :]
    return ref.at[full(zs), full(ys), c, rs, slice(None) if xs is None else lanes(xs)]


def gather_kernel(plan, *refs):
    inputs = 1 + max(p[0] for p in plan)
    outputs = 1 + max(p[3] for p in plan)
    ins, outs = refs[:inputs], refs[inputs : inputs + outputs]
    lsem, zsend, zrecv, xsend, xrecv, ysend, yrecv, csend, crecv = refs[inputs + outputs :]
    z, y, x, c = where_am_i()
    zs, yp, xp, cp = partners(z, y, x, c)
    greet(zs, yp, xp, cp)
    n = len(plan)
    started = [[] for _ in range(n)]
    dst = []
    for src, first, rows, out, tap, wide in plan:
        dst.append(outs[out] if tap is None else outs[out].at[tap])

    def item(i):
        _, _, rows, _, _, wide = plan[i]
        h = split_at(i, rows)
        return rows, wide, slice(0, h), slice(h, rows)

    stages = {}

    def start(i, key, copies):
        for cpy in copies:
            cpy.start()
        stages[i, key] = copies

    def send_z(i):
        src, first, rows, _, _, wide = plan[i]
        block = ins[src].at[first : first + rows]
        here = spot(dst[i], wide, z, y, x, c, slice(None))
        start(i, 0, [remote(block, here, zsend.at[i, j], zrecv.at[i, j], zs[j]) for j in range(3)])
        start(i, 4, [pltpu.make_async_copy(block, here, lsem.at[i])])

    def send_1(i):
        rows, wide, a, b = item(i)
        for cpy in stages[i, 0]:
            cpy.wait_recv()
        stages[i, 4][0].wait()
        ax = spot(dst[i], wide, None, y, x, c, a)
        by = spot(dst[i], wide, None, y, x, c, b)
        start(
            i,
            1,
            [
                remote(ax, ax, xsend.at[i, 0], xrecv.at[i, 0], xp),
                remote(by, by, ysend.at[i, 0], yrecv.at[i, 0], yp),
            ],
        )

    def send_2(i):
        rows, wide, a, b = item(i)
        for cpy in stages[i, 1]:
            cpy.wait_recv()
        ay = spot(dst[i], wide, None, y, None, c, a)
        bx = spot(dst[i], wide, None, None, x, c, b)
        start(
            i,
            2,
            [
                remote(ay, ay, ysend.at[i, 1], yrecv.at[i, 1], yp),
                remote(bx, bx, xsend.at[i, 1], xrecv.at[i, 1], xp),
            ],
        )

    def send_core(i):
        rows, wide, a, b = item(i)
        for cpy in stages[i, 2]:
            cpy.wait_recv()
        half = spot(dst[i], wide, None, None, None, c, slice(None))
        start(i, 3, [remote(half, half, csend.at[i], crecv.at[i], cp)])

    for t in range(n + AHEAD[2]):
        if t == 0:
            for i in range(min(n, AHEAD[3])):
                send_z(i)
        if t + AHEAD[3] < n:
            send_z(t + AHEAD[3])
        if 0 <= t - AHEAD[0] < n:
            send_1(t - AHEAD[0])
        if 0 <= t - AHEAD[1] < n:
            send_2(t - AHEAD[1])
        if 0 <= t - AHEAD[2] < n:
            send_core(t - AHEAD[2])
    for i in range(n):
        stages[i, 3][0].wait_recv()
        for key in range(4):
            for cpy in stages[i, key]:
                cpy.wait_send()


AHEAD = (0, 1, 2, 4)


def gather_fast(plan, ins, out_shapes):
    n = len(plan)
    sem = pltpu.SemaphoreType.DMA
    hbm = pl.BlockSpec(memory_space=pl.ANY)
    return pl.pallas_call(
        functools.partial(gather_kernel, plan),
        out_shape=[jax.ShapeDtypeStruct(s, BF) for s in out_shapes],
        in_specs=[hbm] * len(ins),
        out_specs=[hbm] * len(out_shapes),
        scratch_shapes=[
            sem((n,)),
            sem((n, 3)),
            sem((n, 3)),
            sem((n, 2)),
            sem((n, 2)),
            sem((n, 2)),
            sem((n, 2)),
            sem((n,)),
            sem((n,)),
        ],
        compiler_params=pltpu.CompilerParams(collective_id=1, has_side_effects=True),
    )(*ins)


def add_into(dst, *srcs):
    lead = srcs[0].shape[:-2]
    total = math.prod(lead)

    def one(k, _):
        at = []
        for size in reversed(lead):
            at.append(lax.rem(k, size))
            k = lax.div(k, size)
        at = tuple(reversed(at))
        acc = srcs[0][at].astype(F32)
        for s in srcs[1:]:
            acc = acc + s[at].astype(F32)
        dst[at] = acc.astype(dst.dtype)
        return 0

    lax.fori_loop(0, total, one, 0)


def reduce_kernel(plan, *refs):
    inputs = 1 + max(p[0] for p in plan)
    outputs = 1 + max(p[4] for p in plan)
    n = len(plan)
    ins, refs = refs[:inputs], refs[inputs:]
    outs, refs = refs[:outputs], refs[outputs:]
    rc, refs = refs[:n], refs[n:]
    r1a, refs = refs[:n], refs[n:]
    r1b, refs = refs[:n], refs[n:]
    r2a, refs = refs[:n], refs[n:]
    r2b, refs = refs[:n], refs[n:]
    s3, refs = refs[:n], refs[n:]
    rz, refs = refs[:n], refs[n:]
    ring = {False: refs[0:2], True: refs[2:4]}
    refs = refs[4:]
    lsem, csend, crecv, xsend, xrecv, ysend, yrecv, zsend, zrecv = refs
    z, y, x, c = where_am_i()
    zs, yp, xp, cp = partners(z, y, x, c)
    greet(zs, yp, xp, cp)
    stages = {}

    def start(i, key, copies):
        for cpy in copies:
            cpy.start()
        stages[i, key] = copies

    def src(i):
        k, tap = plan[i][0], plan[i][1]
        return ins[k] if tap is None else ins[k].at[tap]

    def rows_of(i):
        r = plan[i][2]
        h = split_at(i, r)
        return plan[i][3], slice(0, h), slice(h, r), h, r

    kinds = {False: 0, True: 0}
    slot = []
    for p in plan:
        slot.append(kinds[p[3]] % 2)
        kinds[p[3]] += 1

    def own(i):
        wide, _, _, _, r = rows_of(i)
        buf = ring[wide][slot[i]]
        if wide:
            return buf.at[:, :, :, 0:r, :]
        return buf.at[:, :, 0:r, :]

    def send_core(i):
        wide, _, _, _, _ = rows_of(i)
        theirs = spot(src(i), wide, None, None, None, 1 - c, slice(None))
        start(i, 0, [remote(theirs, rc[i], csend.at[i], crecv.at[i], cp)])

    def load(i):
        wide, _, _, _, _ = rows_of(i)
        mine = spot(src(i), wide, None, None, None, c, slice(None))
        start(i, 5, [pltpu.make_async_copy(mine, own(i), lsem.at[i])])

    def send_1(i):
        wide, a, b, h, r = rows_of(i)
        stages[i, 5][0].wait()
        stages[i, 0][0].wait_recv()
        add_into(rc[i], own(i), rc[i])
        if wide:
            pa, pb = rc[i].at[:, :, 1 - y, a, :], rc[i].at[1 - x, :, :, b, :]
        else:
            pa, pb = rc[i].at[:, 1 - y, a, :], rc[i].at[:, :, b, lanes(1 - x)]
        start(
            i,
            1,
            [
                remote(pa, r1a[i], ysend.at[i, 0], yrecv.at[i, 0], yp),
                remote(pb, r1b[i], xsend.at[i, 0], xrecv.at[i, 0], xp),
            ],
        )

    def send_2(i):
        wide, a, b, h, r = rows_of(i)
        for cpy in stages[i, 1]:
            cpy.wait_recv()
        if wide:
            add_into(r1a[i], rc[i].at[:, :, y, a, :], r1a[i])
            add_into(r1b[i], rc[i].at[x, :, :, b, :], r1b[i])
            pa, pb = r1a[i].at[1 - x], r1b[i].at[:, 1 - y]
        else:
            add_into(r1a[i], rc[i].at[:, y, a, :], r1a[i])
            add_into(r1b[i], rc[i].at[:, :, b, lanes(x)], r1b[i])
            pa, pb = r1a[i].at[:, :, lanes(1 - x)], r1b[i].at[:, 1 - y]
        start(
            i,
            2,
            [
                remote(pa, r2a[i], xsend.at[i, 1], xrecv.at[i, 1], xp),
                remote(pb, r2b[i], ysend.at[i, 1], yrecv.at[i, 1], yp),
            ],
        )

    def send_z(i):
        wide, a, b, h, r = rows_of(i)
        for cpy in stages[i, 2]:
            cpy.wait_recv()
        keep = r1a[i].at[x] if wide else r1a[i].at[:, :, lanes(x)]
        add_into(s3[i].at[:, a, :], keep, r2a[i])
        add_into(s3[i].at[:, b, :], r1b[i].at[:, y], r2b[i])
        start(
            i,
            3,
            [
                remote(s3[i].at[(z + j + 1) % 4], rz[i].at[j], zsend.at[i, j], zrecv.at[i, j], zs[j])
                for j in range(3)
            ],
        )

    def finish(i):
        for cpy in stages[i, 3]:
            cpy.wait_recv()
        out, first, r = plan[i][4], plan[i][5], plan[i][2]
        acc = s3[i][z].astype(F32)
        for j in range(3):
            acc = acc + rz[i][j].astype(F32)
        outs[out][first : first + r, :] = acc

    for i in range(n):
        send_core(i)
    seen = {False: [], True: []}
    for i, p in enumerate(plan):
        seen[p[3]].append(i)
    for kind in (False, True):
        for i in seen[kind][:2]:
            load(i)
    for t in range(n + 3):
        if t < n:
            send_1(t)
            order = seen[plan[t][3]]
            k = order.index(t)
            if k + 2 < len(order):
                load(order[k + 2])
        if 0 <= t - 1 < n:
            send_2(t - 1)
        if 0 <= t - 2 < n:
            send_z(t - 2)
        if 0 <= t - 3 < n:
            finish(t - 3)
    for i in range(n):
        for key in range(4):
            for cpy in stages[i, key]:
                cpy.wait_send()


def reduce_fast(plan, ins, out_shapes):
    n = len(plan)
    sem = pltpu.SemaphoreType.DMA
    scratch = [[] for _ in range(7)]
    most = {False: 0, True: 0}
    for i, (_, _, r, wide, _, _) in enumerate(plan):
        h = split_at(i, r)
        most[wide] = max(most[wide], r)
        if wide:
            shapes = [
                (2, 4, 2, r, D),
                (2, 4, h, D),
                (4, 2, r - h, D),
                (4, h, D),
                (4, r - h, D),
                (4, r, D),
                (3, r, D),
            ]
        else:
            shapes = [
                (4, 2, r, D),
                (4, h, D),
                (4, 2, r - h, LANES),
                (4, h, LANES),
                (4, r - h, LANES),
                (4, r, LANES),
                (3, r, LANES),
            ]
        for group, shape in zip(scratch, shapes):
            group.append(pltpu.VMEM(shape, BF))
    scratch = [s for group in scratch for s in group]
    scratch += [pltpu.VMEM((4, 2, most[False], D), BF)] * 2
    scratch += [pltpu.VMEM((2, 4, 2, most[True], D), BF)] * 2
    scratch += [sem((n,)), sem((n,)), sem((n,))]
    scratch += [sem((n, 2)), sem((n, 2)), sem((n, 2)), sem((n, 2)), sem((n, 3)), sem((n, 3))]
    return pl.pallas_call(
        functools.partial(reduce_kernel, plan),
        out_shape=[jax.ShapeDtypeStruct(s, F32) for s in out_shapes],
        in_specs=[pl.BlockSpec(memory_space=pl.ANY)] * len(ins),
        out_specs=[pl.BlockSpec(memory_space=pltpu.VMEM)] * len(out_shapes),
        scratch_shapes=scratch,
        compiler_params=pltpu.CompilerParams(
            collective_id=2, has_side_effects=True, vmem_limit_bytes=60 << 20
        ),
    )(*ins)

SQUARE = (4, 5, 6, 7, 18, 19, 20, 21, 24, 25, 26, 27)
TALL = (11, 31)
BROAD = (10, 30)
VECTORS = tuple(i for i in range(32) if KINDS[i] == "v")
MISC_ROWS = 32
SWAP = ((0, 1), (1, 0), (2, 3), (3, 2))


def plans(shards):
    g, r, shapes, first = [], [], [], 0
    for i in SQUARE + (1,) + TALL:
        w = shards[i]
        rows = w.shape[-2] // 2
        one = (4, 2, 2, rows, D)
        for tap in range(w.shape[0]) if w.ndim == 3 else (None,):
            g.append((0, first, rows, len(shapes), tap, False))
            r.append((len(shapes), tap, rows, False, 0, first))
            first += rows
        shapes.append(one if w.ndim == 2 else (w.shape[0],) + one)
    at = 0
    for i in BROAD:
        rows = shards[i].shape[0]
        g.append((1, at, rows, len(shapes), None, True))
        r.append((len(shapes), None, rows, True, 1, at))
        at += rows
        shapes.append((2, 2, 4, 2, rows, D))
    g.append((2, 0, MISC_ROWS, len(shapes), None, True))
    r.append((len(shapes), None, MISC_ROWS, True, 2, 0))
    shapes.append((2, 2, 4, 2, MISC_ROWS, D))
    return g, r, shapes, first, at


def by_core(c, zero, one):
    return jnp.where(c == 0, zero, one)


def narrow_halves(shards):
    parts = []
    for i in SQUARE + (1,) + TALL:
        w = shards[i].reshape(-1, 2, shards[i].shape[-2] // 2, shards[i].shape[-1])
        parts += [w[t] for t in range(w.shape[0])]
    return jnp.concatenate(parts, axis=1)


def gather_weights(shards):
    c = lax.axis_index("seq") % 2
    g, _, shapes, _, _ = plans(shards)
    halves = narrow_halves(shards)
    mine = by_core(c, halves[0], halves[1])
    got = lax.ppermute(by_core(c, halves[1], halves[0]), "seq", SWAP)
    narrow = by_core(
        c, jnp.concatenate([mine, got], axis=1), jnp.concatenate([got, mine], axis=1)
    )
    broad = jnp.concatenate([shards[i] for i in BROAD], axis=0)
    flat = [shards[i].reshape(-1) for i in (0,) + VECTORS + (15,)]
    size = sum(f.size for f in flat)
    flat.append(jnp.zeros((MISC_ROWS * D - size,), BF))
    misc = jnp.concatenate(flat).reshape(MISC_ROWS, D)
    outs = gather_fast(g, [narrow, broad, misc], shapes)
    full = [None] * 32
    for k, i in enumerate(SQUARE + (1,) + TALL):
        full[i] = outs[k].reshape(shards[i].shape[:-2] + (8 * shards[i].shape[-2], D))
    for k, i in enumerate(BROAD):
        full[i] = outs[15 + k].reshape(4, D, D)
    misc = outs[17].reshape(2, 2, 4, 2, MISC_ROWS * D)
    at = 0
    t, a, b = shards[0].shape
    full[0] = (
        misc[..., : shards[0].size]
        .reshape(2, 2, 4, 2, t, a, b)
        .transpose(4, 0, 1, 5, 2, 3, 6)
        .reshape(t, 4 * a, 8 * b)
    )
    at += shards[0].size
    n = shards[VECTORS[0]].size
    vecs = misc[..., at : at + n * len(VECTORS)].reshape(2, 2, 4, 2, len(VECTORS), n)
    vecs = vecs.transpose(4, 2, 3, 0, 1, 5).reshape(len(VECTORS), D)
    for k, i in enumerate(VECTORS):
        full[i] = vecs[k]
    at += n * len(VECTORS)
    r, w = shards[15].shape
    full[15] = (
        misc[..., at : at + r * w]
        .reshape(2, 2, 4, 2, r, w)
        .transpose(2, 3, 4, 0, 1, 5)
        .reshape(8 * r, 4 * w)
    )
    return full


def reduce_grads(grads, shards):
    c = lax.axis_index("seq") % 2
    _, r, shapes, narrow_rows, broad_rows = plans(shards)
    ins = [grads[i].reshape(shapes[k]) for k, i in enumerate(SQUARE + (1,) + TALL + BROAD)]
    t, a, b = shards[0].shape
    conv1 = grads[0].reshape(t, 2, 2, a, 4, 2, b).transpose(1, 2, 4, 5, 0, 3, 6)
    n = shards[VECTORS[0]].size
    vecs = jnp.stack([grads[i] for i in VECTORS]).reshape(-1, 4, 2, 2, 2, n)
    flat = [conv1.reshape(2, 2, 4, 2, -1), vecs.transpose(3, 4, 1, 2, 0, 5).reshape(2, 2, 4, 2, -1)]
    size = sum(f.shape[-1] for f in flat)
    flat.append(jnp.zeros((2, 2, 4, 2, MISC_ROWS * D - size), F32))
    ins.append(jnp.concatenate(flat, axis=-1).astype(BF).reshape(shapes[-1]))
    narrow, broad, misc = reduce_fast(
        r, ins, [(narrow_rows, LANES), (broad_rows, D), (MISC_ROWS, D)]
    )
    half = LANES // 2
    mine = by_core(c, narrow[:, :half], narrow[:, half:])
    got = lax.ppermute(by_core(c, narrow[:, half:], narrow[:, :half]), "seq", SWAP)
    out, at = [None] * 32, 0
    for i in SQUARE + (1,) + TALL:
        w = shards[i]
        rows, taps = w.shape[-2] // 2, []
        for _ in range(w.shape[0] if w.ndim == 3 else 1):
            m, o = mine[at : at + rows], got[at : at + rows]
            taps.append(by_core(c, jnp.concatenate([m, o]), jnp.concatenate([o, m])))
            at += rows
        out[i] = taps[0] if w.ndim == 2 else jnp.stack(taps)
    at = 0
    for i in BROAD:
        out[i] = broad[at : at + shards[i].shape[0]]
        at += shards[i].shape[0]
    misc = misc.reshape(-1)
    out[0] = misc[: shards[0].size].reshape(shards[0].shape)
    at = shards[0].size
    for i in VECTORS:
        out[i] = misc[at : at + n]
        at += n
    return out


def one_hot(ids, table):
    first = lax.axis_index("dp") * table.shape[0]
    return ((ids - first)[:, None] == jnp.arange(table.shape[0])[None, :]).astype(BF)


def body(mel_frames, token_ids, token_counts, *rest):
    shards, cotangent = list(rest[:32]), rest[32][0]
    table = shards[14]
    dps, seqs = lax.axis_size("dp"), lax.axis_size("seq")
    me = lax.axis_index("seq")
    slots = token_ids.shape[1]
    all_slots = slots * seqs
    frames = mel_frames.shape[1] // 2

    ids = lax.all_gather(token_ids[0], BOTH, axis=0, tiled=True)
    hot = one_hot(ids, table)
    looked = mm(hot, table, BF)
    mine = lax.psum_scatter(looked, "dp", scatter_dimension=0, tiled=True)
    looked = lax.all_gather(mine, "seq", axis=0, tiled=True)
    looked = looked.reshape(seqs, all_slots, D // seqs).transpose(1, 0, 2).reshape(all_slots, D)

    weights = shards[:14] + [None] + shards[15:]
    fast = dps == 8 and seqs == 4
    full = gather_weights(weights) if fast else gather_plain(weights)
    vec = {i: full[i].astype(F32) for i in range(32) if KINDS[i] == "v"}
    conv1, conv2, position = full[0].reshape(-1, D), full[1], full[15]
    eq, ek, ev, eo = full[4:8]
    ee, ec = full[10:12]
    dq_w, dk_w, dv_w, do_w = full[18:22]
    cq_w, ck_w, cv_w, co_w = full[24:28]
    de, dc = full[30:32]

    pairs = extended(mel_frames[0], 2).reshape(frames + 2, -1)
    mels = mel_frames.shape[2]
    n = frames + 1
    even_in = jnp.concatenate([pairs[:n], pairs[1:, :mels]], axis=1)
    odd_in = jnp.concatenate([pairs[:n, mels:], pairs[1:]], axis=1)
    even_pre, odd_pre = mm(even_in, conv1), mm(odd_in, conv1)
    row = jnp.arange(n)[:, None]
    even_keep = (row > 0) | (me > 0)
    odd_keep = (row < n - 1) | (me < seqs - 1)
    even = jnp.where(even_keep, gelu(even_pre), 0.0).astype(BF)
    odd = jnp.where(odd_keep, gelu(odd_pre), 0.0).astype(BF)
    second_pre = mm(even[:frames], conv2[0]) + mm(odd[:frames], conv2[1]) + mm(even[1:], conv2[2])
    stream0 = gelu(second_pre) + sinusoid(me * frames, frames)

    enc_normed = norm(stream0, vec[2], vec[3])
    q = (mm(enc_normed, eq) * SCALE).astype(BF)
    k = mm(enc_normed, ek, BF)
    v = mm(enc_normed, ev, BF)
    kv = lax.all_gather(jnp.concatenate([k, v], axis=1), "seq", axis=0, tiled=True)
    k_all, v_all = kv[:, :D], kv[:, D:]
    enc_mixed, enc_lse = attend(q, k_all, v_all)
    enc_wide, enc_mixed = enc_mixed, enc_mixed.astype(BF)
    stream1 = stream0 + mm(enc_mixed, eo)
    enc_mlp_normed = norm(stream1, vec[8], vec[9])
    enc_pre, enc_hidden, out = mlp(enc_mlp_normed, ee, ec)
    stream2 = stream1 + out
    memory = norm(stream2, vec[12], vec[13])
    mk = mm(memory, ck_w, BF)
    mv = mm(memory, cv_w, BF)

    place = jnp.arange(all_slots)
    causal = (place[None, :] <= place[:, None]) & (place[None, :] < token_counts[0])
    embedded = looked.astype(F32) + position.astype(F32)
    dec_normed = norm(embedded, vec[16], vec[17])
    sq = (mm(dec_normed, dq_w) * SCALE).astype(BF)
    sk = mm(dec_normed, dk_w, BF)
    sv = mm(dec_normed, dv_w, BF)
    dec_mixed, dec_lse = attend(sq, sk, sv, causal)
    dec_wide, dec_mixed = dec_mixed, dec_mixed.astype(BF)
    stream4 = embedded + mm(dec_mixed, do_w)
    cross_normed = norm(stream4, vec[22], vec[23])
    xq = (mm(cross_normed, cq_w) * SCALE).astype(BF)

    part, part_lse = attend(xq, mk, mv)
    got = exchange(pack(part, [part_lse]))
    parts, (lses,) = unpack(got, 1)
    top = jnp.max(lses, axis=0)
    share = jnp.exp(lses - top)
    total = jnp.sum(share, axis=0)
    cross_lse = top + jnp.log(total)
    share = share / total
    cross_wide = jnp.sum(
        parts.reshape(seqs, slots, HEADS, HEAD) * share[..., None], axis=0
    ).reshape(slots, D)
    cross_mixed = cross_wide.astype(BF)

    own = lambda a: lax.dynamic_slice_in_dim(a, me * slots, slots, 0)
    stream4 = own(stream4)
    stream5 = stream4 + mm(cross_mixed, co_w)
    dec_mlp_normed = norm(stream5, vec[28], vec[29])
    dec_pre, dec_hidden, out = mlp(dec_mlp_normed, de, dc)
    stream6 = stream5 + out
    live = (own(place) < token_counts[0])[:, None]
    decoded = jnp.where(live, stream6, 0.0).astype(BF)

    grads = [None] * 32

    def mlp_back(ex, co, gain, normed, pre, hidden, stream, up):
        d_low = up.astype(BF)
        wide = normed.shape[1]
        first, second, total = [], [], 0.0
        for s in range(seqs):
            contract = full[co][s * wide : (s + 1) * wide]
            second.append(outer(hidden[s], d_low))
            d_pre = (gelu_slope(pre[s]) * low(mm_t(d_low, contract))).astype(BF)
            first.append(outer(normed, d_pre))
            total = total + mm_t(d_pre, full[ex][s])
        grads[co] = jnp.concatenate(second, axis=0)
        grads[ex] = jnp.stack(first)
        back, grads[gain], grads[gain + 1] = norm_back(stream, vec[gain], total)
        return up + back

    up = jnp.where(live, cotangent.astype(F32), 0.0)
    up = mlp_back(30, 31, 28, dec_mlp_normed, dec_pre, dec_hidden, stream5, up)
    d_low = up.astype(BF)
    grads[27] = outer(cross_mixed, d_low)
    d_mixed = mm_t(d_low, co_w, BF)
    sent = pack(d_mixed, [cross_lse])
    d_mixed, (lse_all,) = unpack(lax.all_gather(sent, "seq", axis=0, tiled=True), 1)
    dxq, dmk, dmv = attend_back(xq, mk, mv, None, lse_all, d_mixed.astype(BF), lambda v: lax.psum(v, "seq"))
    dxq = jnp.sum(exchange(dxq), axis=0)
    dxq = (low(dxq) * SCALE).astype(BF)
    grads[24] = outer(own(cross_normed), dxq)
    back, grads[22], grads[23] = norm_back(stream4, vec[22], mm_t(dxq, cq_w))
    up = up + back
    d_low = up.astype(BF)
    grads[21] = outer(own(dec_mixed), d_low)
    d_mixed = lax.all_gather(mm_t(d_low, do_w, BF), "seq", axis=0, tiled=True)
    dsq, dsk, dsv = attend_back(sq, sk, sv, causal, dec_lse, d_mixed)

    def inputs_back(first, gain, normed, stream, dq, dk, dv, up):
        dq = (low(dq) * SCALE).astype(BF)
        dk, dv = dk.astype(BF), dv.astype(BF)
        total = 0.0
        for i, g in enumerate((dq, dk, dv)):
            grads[first + i] = outer(normed, g)
            total = total + mm_t(g, full[first + i])
        back, grads[gain], grads[gain + 1] = norm_back(stream, vec[gain], total)
        return up + back

    up = inputs_back(18, 16, own(dec_normed), own(embedded), own(dsq), own(dsk), own(dsv), up)

    cols = exchange_columns(up.astype(BF))
    every = lax.all_gather(cols, "dp", axis=0, tiled=True)
    grad_table = dot(hot, every, 0, 0)
    per_clip = every.reshape(dps, dps, -1, D // seqs)
    grad_position = jnp.sum(
        lax.dynamic_index_in_dim(per_clip, lax.axis_index("dp"), 1, False).astype(F32), axis=0
    )

    dmk, dmv = dmk.astype(BF), dmv.astype(BF)
    grads[25] = outer(memory, dmk)
    grads[26] = outer(memory, dmv)
    up, grads[12], grads[13] = norm_back(stream2, vec[12], mm_t(dmk, ck_w) + mm_t(dmv, cv_w))
    up = mlp_back(10, 11, 8, enc_mlp_normed, enc_pre, enc_hidden, stream1, up)
    d_low = up.astype(BF)
    grads[7] = outer(enc_mixed, d_low)
    d_mixed = mm_t(d_low, eo, BF)
    dq, dk, dv = attend_back(q, k_all, v_all, None, enc_lse, d_mixed)
    dkv = jnp.concatenate([dk, dv], axis=1).astype(BF)
    dkv = lax.psum_scatter(dkv, "seq", scatter_dimension=0, tiled=True)
    up = inputs_back(4, 2, enc_normed, stream0, dq, dkv[:, :D], dkv[:, D:], up)

    d_second = (gelu_slope(second_pre) * up).astype(BF)
    grads[1] = jnp.stack(
        [outer(even[:frames], d_second), outer(odd[:frames], d_second), outer(even[1:], d_second)]
    )
    rim = extended(d_second, 1)
    d_even = mm_t(rim[1:], conv2[0]) + mm_t(rim[:n], conv2[2])
    d_odd = mm_t(rim[1:], conv2[1])
    d_even = jnp.where(even_keep, gelu_slope(even_pre) * low(d_even), 0.0).astype(BF)
    d_odd = jnp.where(odd_keep, gelu_slope(odd_pre) * low(d_odd), 0.0).astype(BF)
    grads[0] = (outer(odd_in[:frames], d_odd[:frames], F32) + outer(even_in[1:], d_even[1:], F32)).reshape(
        3, mels, D
    )
    me_g, mo_g = mm_t(d_even, conv1), mm_t(d_odd, conv1)
    mel_grad = jnp.concatenate(
        [
            me_g[1:, :mels] + me_g[:-1, 2 * mels :] + mo_g[:-1, mels : 2 * mels],
            me_g[1:, mels : 2 * mels] + mo_g[1:, :mels] + mo_g[:-1, 2 * mels :],
        ],
        axis=1,
    ).reshape(1, 2 * frames, mels)

    done = (reduce_grads if fast else reduce_plain)(grads, shards)
    done[14], done[15] = grad_table, grad_position
    return tuple([decoded[None], mel_grad] + done)


def exchange_columns(v):
    n = lax.axis_size("seq")
    wide = v.shape[1] // n
    v = v.reshape(v.shape[0], n, wide).transpose(1, 0, 2)
    return lax.all_to_all(v, "seq", split_axis=0, concat_axis=0, tiled=True).reshape(-1, wide)


def solution(mesh):
    place = {
        "1": P(None, "seq", "dp"),
        "2": P(None, "dp", "seq"),
        "v": P(BOTH),
        "m": P("dp", "seq"),
        "t": P("dp", "seq"),
    }
    rows = P("dp", "seq", None)
    weights = tuple(place[k] for k in KINDS)
    return jax.shard_map(
        body,
        mesh=mesh,
        in_specs=(rows, P("dp", "seq"), P("dp")) + weights + (rows,),
        out_specs=(rows, rows) + weights,
        check_vma=False,
    )
```

```python
import functools
import math

import jax
import jax.numpy as jnp
from jax import lax
from jax.experimental import pallas as pl
from jax.experimental.pallas import tpu as pltpu
from jax.sharding import PartitionSpec as P

D = 768
HEADS = 12
HEAD = 64
EPSILON = 1e-05
NEGATIVE = -1e30
SCALE = 1.0 / math.sqrt(HEAD)
BF = jnp.bfloat16
F32 = jnp.float32
BOTH = ("dp", "seq")

KINDS = "12vvmmmmvvmmvvtmvvmmmmvvmmmmvvmm"


def dot(a, b, ca, cb, out=F32):
    return lax.dot_general(a, b, (((ca,), (cb,)), ((), ())), preferred_element_type=F32).astype(out)


def mm(a, b, out=F32):
    return dot(a, b, 1, 0, out)


def mm_t(a, b, out=F32):
    return dot(a, b, 1, 1, out)


def outer(a, b, out=BF):
    return dot(a, b, 0, 0, out)


def norm_parts(values):
    center = values - jnp.mean(values, axis=-1, keepdims=True)
    spread = jnp.mean(center * center, axis=-1, keepdims=True)
    inv = lax.rsqrt(spread + EPSILON)
    return center * inv, inv


def norm(values, gain, bias):
    return (norm_parts(values)[0] * gain + bias).astype(BF)


def norm_back(values, gain, up):
    hat, inv = norm_parts(values)
    g = up * gain
    back = inv * (
        g - jnp.mean(g, axis=-1, keepdims=True) - hat * jnp.mean(g * hat, axis=-1, keepdims=True)
    )
    return back, jnp.sum(up * hat, axis=0), jnp.sum(up, axis=0)


def gelu(v):
    return v * (0.5 + 0.5 * lax.erf(v * math.sqrt(0.5)))


def gelu_slope(v):
    return (0.5 + 0.5 * lax.erf(v * math.sqrt(0.5))) + v * jnp.exp(-0.5 * v * v) * (
        1.0 / math.sqrt(2.0 * math.pi)
    )


def low(v):
    return lax.reduce_precision(v, 8, 7)


PAIR = 2 * HEAD


def tdot(a, b, ca, cb):
    return lax.dot_general(a, b, (((ca,), (cb,)), ((), ())), preferred_element_type=F32)


def one_head(rows, half):
    lane = lax.broadcasted_iota(jnp.int32, rows.shape, 1)
    return jnp.where((lane < HEAD) == (half == 0), rows, jnp.zeros_like(rows))


def masked(s, count_ref):
    if count_ref is None:
        return s
    key = lax.broadcasted_iota(jnp.int32, s.shape, 0)
    query = lax.broadcasted_iota(jnp.int32, s.shape, 1)
    return jnp.where((key <= query) & (key < count_ref[0]), s, NEGATIVE)


def pack(rows, log_sums):
    cols, rest = [rows], log_sums.T
    for _ in range(3):
        term = low(rest)
        cols.append(term.astype(BF))
        rest = rest - term
    wide = sum(c.shape[1] for c in cols)
    return jnp.concatenate(cols + [jnp.zeros((rows.shape[0], -wide % 128), BF)], axis=1)


def unpack(packed):
    terms = [packed[..., D + i * HEADS : D + (i + 1) * HEADS].astype(F32) for i in range(3)]
    return packed[..., :D], terms[0] + terms[1] + terms[2]


SWAP = ((0, 1), (1, 0), (2, 3), (3, 2))


def shift(v, axis, step):
    n = lax.axis_size(axis)
    return lax.ppermute(v, axis, [(i, i + step) for i in range(n) if 0 <= i + step < n])


def extended(x, width):
    before = shift(x[-width:], "seq", 1)
    after = shift(x[:width], "seq", -1)
    return jnp.concatenate([before, x, after], axis=0)


def exchange(v):
    n = lax.axis_size("seq")
    got = lax.all_to_all(v, "seq", split_axis=0, concat_axis=0, tiled=True)
    return got.reshape(n, v.shape[0] // n, v.shape[1])


def sinusoid(first_frame, frame_count):
    half = D // 2
    frequency = jnp.exp(jnp.arange(half).astype(F32) * (-math.log(10000.0) / (half - 1)))
    places = (first_frame + jnp.arange(frame_count)).astype(F32)
    angles = places[:, None] * frequency[None, :]
    return jnp.concatenate([jnp.sin(angles), jnp.cos(angles)], axis=1)


def to_whole(flat, shape, kind, dps, seqs):
    if kind == "v":
        return flat.reshape(-1)
    if kind == "1":
        t, i, o = shape
        return (
            flat.reshape(dps, seqs, t, i, o)
            .transpose(2, 1, 3, 0, 4)
            .reshape(t, seqs * i, dps * o)
        )
    if kind == "2":
        t, i, o = shape
        return (
            flat.reshape(dps, seqs, t, i, o)
            .transpose(2, 0, 3, 1, 4)
            .reshape(t, dps * i, seqs * o)
        )
    r, c = shape
    return flat.reshape(dps, seqs, r, c).transpose(0, 2, 1, 3).reshape(dps * r, seqs * c)


def to_owner(g, kind, dps, seqs):
    n = dps * seqs
    if kind == "v":
        return g.reshape(n, -1)
    if kind == "1":
        t, i, o = g.shape
        g = g.reshape(t, seqs, i // seqs, dps, o // dps).transpose(3, 1, 0, 2, 4)
    elif kind == "2":
        t, i, o = g.shape
        g = g.reshape(t, dps, i // dps, seqs, o // seqs).transpose(1, 3, 0, 2, 4)
    else:
        r, c = g.shape
        g = g.reshape(dps, r // dps, seqs, c // seqs).transpose(0, 2, 1, 3)
    return g.reshape(n, -1)


def gather_plain(shards):
    dps, seqs = lax.axis_size("dp"), lax.axis_size("seq")
    flat = jnp.concatenate([w.reshape(-1) for w in shards if w is not None])
    got = lax.all_gather(flat[None], BOTH, axis=0, tiled=True)
    out, at = [], 0
    for w, kind in zip(shards, KINDS):
        if w is None:
            out.append(None)
            continue
        out.append(to_whole(got[:, at : at + w.size], w.shape, kind, dps, seqs))
        at += w.size
    for i in BROAD:
        out[i] = out[i].reshape(D, seqs, -1).transpose(1, 0, 2)
    return out


def product(factors):
    left, right = factors
    if right.ndim == 3:
        return jnp.concatenate([outer(left, r) for r in right], axis=1)
    if isinstance(left, list) or left.ndim == 3:
        return jnp.stack([outer(l, right) for l in left])
    return outer(left, right)


def reduce_plain(grads, shards):
    dps, seqs = lax.axis_size("dp"), lax.axis_size("seq")
    grads = [product(g) if isinstance(g, tuple) else g for g in grads]
    for i in TALL:
        grads[i] = grads[i].reshape(-1, D)
    flat = jnp.concatenate(
        [to_owner(g.astype(BF), k, dps, seqs) for g, k in zip(grads, KINDS) if g is not None], axis=1
    )
    own = lax.psum_scatter(flat, BOTH, scatter_dimension=0, tiled=True).astype(F32)[0]
    out, at = [], 0
    for w, g in zip(shards, grads):
        if g is None:
            out.append(None)
            continue
        out.append(own[at : at + w.size].reshape(w.shape))
        at += w.size
    return out


MESH = pl.DeviceIdType.MESH
LANES = 384


def where_am_i():
    d, s = lax.axis_index("dp"), lax.axis_index("seq")
    return d // 2, d % 2, s // 2, s % 2


def partners(z, y, x, c):
    at = lambda z, y, x, c: (z * 2 + y, x * 2 + c)
    zs = [at((z + j) % 4, y, x, c) for j in (1, 2, 3)]
    return zs, at(z, 1 - y, x, c), at(z, y, 1 - x, c), at(z, y, x, 1 - c)


def greet(zs, yp, xp, cp):
    barrier = pltpu.get_barrier_semaphore()
    everyone = zs + [yp, xp, cp]
    for dev in everyone:
        pl.semaphore_signal(barrier, inc=1, device_id=dev, device_id_type=MESH)
    pl.semaphore_wait(barrier, len(everyone))


def remote(src, dst, send, recv, dev):
    return pltpu.make_async_remote_copy(
        src_ref=src, dst_ref=dst, send_sem=send, recv_sem=recv, device_id=dev, device_id_type=MESH
    )


def split_at(i, rows):
    return rows // 2 if rows % 32 == 0 else 16 + 16 * (i % 2)


def lanes(x):
    return pl.ds(pl.multiple_of(x * LANES, LANES), LANES)


def spot(ref, wide, zs, ys, xs, c, rs):
    full = lambda v: slice(None) if v is None else v
    if wide:
        return ref.at[full(xs), c, full(zs), full(ys), rs, :]
    return ref.at[full(zs), full(ys), c, rs, slice(None) if xs is None else lanes(xs)]


def gather_kernel(plan, *refs):
    inputs = 1 + max(p[0] for p in plan)
    outputs = 1 + max(p[3] for p in plan)
    ins, outs = refs[:inputs], refs[inputs : inputs + outputs]
    lsem, zsend, zrecv, xsend, xrecv, ysend, yrecv, csend, crecv = refs[inputs + outputs :]
    z, y, x, c = where_am_i()
    zs, yp, xp, cp = partners(z, y, x, c)
    greet(zs, yp, xp, cp)
    n = len(plan)
    started = [[] for _ in range(n)]
    dst = []
    for src, first, rows, out, tap, wide in plan:
        dst.append(outs[out] if tap is None else outs[out].at[tap])

    def item(i):
        _, _, rows, _, _, wide = plan[i]
        h = split_at(i, rows)
        return rows, wide, slice(0, h), slice(h, rows)

    stages = {}

    def start(i, key, copies):
        for cpy in copies:
            cpy.start()
        stages[i, key] = copies

    def send_z(i):
        src, first, rows, _, _, wide = plan[i]
        block = ins[src].at[first : first + rows]
        here = spot(dst[i], wide, z, y, x, c, slice(None))
        start(i, 0, [remote(block, here, zsend.at[i, j], zrecv.at[i, j], zs[j]) for j in range(3)])
        start(i, 4, [pltpu.make_async_copy(block, here, lsem.at[i])])

    def send_1(i):
        rows, wide, a, b = item(i)
        for cpy in stages[i, 0]:
            cpy.wait_recv()
        stages[i, 4][0].wait()
        ax = spot(dst[i], wide, None, y, x, c, a)
        by = spot(dst[i], wide, None, y, x, c, b)
        start(
            i,
            1,
            [
                remote(ax, ax, xsend.at[i, 0], xrecv.at[i, 0], xp),
                remote(by, by, ysend.at[i, 0], yrecv.at[i, 0], yp),
            ],
        )

    def send_2(i):
        rows, wide, a, b = item(i)
        for cpy in stages[i, 1]:
            cpy.wait_recv()
        ay = spot(dst[i], wide, None, y, None, c, a)
        bx = spot(dst[i], wide, None, None, x, c, b)
        start(
            i,
            2,
            [
                remote(ay, ay, ysend.at[i, 1], yrecv.at[i, 1], yp),
                remote(bx, bx, xsend.at[i, 1], xrecv.at[i, 1], xp),
            ],
        )

    def send_core(i):
        rows, wide, a, b = item(i)
        for cpy in stages[i, 2]:
            cpy.wait_recv()
        half = spot(dst[i], wide, None, None, None, c, slice(None))
        start(i, 3, [remote(half, half, csend.at[i], crecv.at[i], cp)])

    for t in range(n + AHEAD[2]):
        if t == 0:
            for i in range(min(n, AHEAD[3])):
                send_z(i)
        if t + AHEAD[3] < n:
            send_z(t + AHEAD[3])
        if 0 <= t - AHEAD[0] < n:
            send_1(t - AHEAD[0])
        if 0 <= t - AHEAD[1] < n:
            send_2(t - AHEAD[1])
        if 0 <= t - AHEAD[2] < n:
            send_core(t - AHEAD[2])
    for i in range(n):
        stages[i, 3][0].wait_recv()
        for key in range(4):
            for cpy in stages[i, key]:
                cpy.wait_send()


AHEAD = (0, 1, 2, 4)


def gather_fast(plan, ins, out_shapes):
    n = len(plan)
    sem = pltpu.SemaphoreType.DMA
    hbm = pl.BlockSpec(memory_space=pl.ANY)
    return pl.pallas_call(
        functools.partial(gather_kernel, plan),
        out_shape=[jax.ShapeDtypeStruct(s, BF) for s in out_shapes],
        in_specs=[hbm] * len(ins),
        out_specs=[hbm] * len(out_shapes),
        scratch_shapes=[
            sem((n,)),
            sem((n, 3)),
            sem((n, 3)),
            sem((n, 2)),
            sem((n, 2)),
            sem((n, 2)),
            sem((n, 2)),
            sem((n,)),
            sem((n,)),
        ],
        compiler_params=pltpu.CompilerParams(collective_id=1, has_side_effects=True),
    )(*ins)


def add_into(dst, *srcs):
    lead = srcs[0].shape[:-2]
    total = math.prod(lead)

    def one(k, _):
        at = []
        for size in reversed(lead):
            at.append(lax.rem(k, size))
            k = lax.div(k, size)
        at = tuple(reversed(at))
        acc = srcs[0][at].astype(F32)
        for s in srcs[1:]:
            acc = acc + s[at].astype(F32)
        dst[at] = acc.astype(dst.dtype)
        return 0

    lax.fori_loop(0, total, one, 0)


RB = 48


def item_shapes(kind, h):
    if kind == "n":
        g = RB - h
        return [
            (4, 2, RB, D),
            (4, h, D),
            (4, 2, g, LANES),
            (4, h, LANES),
            (4, g, LANES),
            (4, RB, LANES),
            (3, RB, LANES),
        ]
    if kind == "t":
        return [
            (4, 4, 2, RB, D),
            (4, 2, RB, D),
            (4, 4, RB, LANES),
            (4, 2, RB, LANES),
            (4, 2, RB, LANES),
            (4, 2, 2, RB, LANES),
            (3, 2, 2, RB, LANES),
        ]
    r = RB if kind == "w" else MISC_ROWS // 2
    return [
        (2, 4, 2, 2, r, D),
        (2, 4, r, D),
        (4, 2, r, D),
        (4, r, D),
        (4, r, D),
        (4, 2, r, D),
        (3, 2, r, D),
    ]


def halves_of(k):
    return 16 + 16 * (k % 2)


def reduce_kernel(items, jobs, inputs, outputs, *refs):
    n = len(items)
    take = lambda count: (refs[:count], refs[count:])
    ins, refs = take(inputs)
    outs, refs = take(outputs)
    rc, refs = take(n)
    r1a, refs = take(n)
    r1b, refs = take(n)
    r2a, refs = take(n)
    r2b, refs = take(n)
    s3, refs = take(n)
    rz, refs = take(n)
    sbuf, refs = take(n)
    ring, wide_ring, given, xbuf, ybuf = refs[:5]
    loads, csend, crecv, xsend, xrecv, ysend, yrecv, zsend, zrecv, fsend, frecv = refs[5:]
    z, y, x, c = where_am_i()
    zs, yp, xp, cp = partners(z, y, x, c)
    greet(zs, yp, xp, cp)
    started = []

    def start(copy):
        copy.start()
        started.append(copy)
        return copy

    cores, ones, twos, threes, loaded = {}, {}, {}, {}, {}
    half = lambda i: halves_of(i)

    def load(t):
        _, part, xi, yi, rows = jobs[t]
        xsrc, ysrc = ins[xi], ins[yi]
        if len(xsrc.shape) == 3:
            xsrc = xsrc.at[part]
        if len(ysrc.shape) == 3:
            ysrc = ysrc.at[2 * (part // 2) + (c if part % 2 else 1 - c)]
        pair = []
        for k, (src, buf) in enumerate(((xsrc, xbuf), (ysrc, ybuf))):
            copy = pltpu.make_async_copy(src, buf.at[t % 2, 0:rows], loads.at[t % 2, k])
            copy.start()
            pair.append(copy)
        loaded[t] = pair

    def room(t):
        return wide_ring if items[jobs[t][0]][1] == F32 else ring.at[t % RING]

    def compute(t):
        i, part, _, _, rows = jobs[t]
        if t >= RING and t - RING in cores and items[jobs[t - RING][0]][1] == BF:
            cores[t - RING].wait_send()
        for copy in loaded[t]:
            copy.wait()
        room_t = room(t)
        left = xbuf[t % 2, 0:rows, :]

        def column(k, _):
            at = pl.ds(pl.multiple_of(k * 256, 256), 256)
            product = tdot(left, ybuf[t % 2, 0:rows, at], 0, 0)
            room_t[:, :, :, :, at] = product.reshape(4, 2, 2, RB, 256).astype(room_t.dtype)
            return 0

        lax.fori_loop(0, D // 256, column, 0)
        if t + 2 < len(jobs):
            load(t + 2)
        kind = items[i][0]
        if kind == "n":
            cores[t] = remote(room_t.at[:, :, 1 - c], rc[i], csend.at[t], crecv.at[t], cp)
        elif kind == "t":
            cores[t] = remote(room_t.at[:, :, 1 - c], rc[i].at[part], csend.at[t], crecv.at[t], cp)
        elif part % 2 == 0:
            cores[t] = remote(room_t, rc[i].at[part // 2], csend.at[t], crecv.at[t], cp)
        if t in cores:
            cores[t].start()

    def add_own(t):
        i, part, _, _, _ = jobs[t]
        kind, mine = items[i][0], room(t)
        if kind == "w":
            if part % 2 == 0:
                return False
            cores[t - 1].wait_recv()
            add_into(rc[i].at[part // 2], mine, rc[i].at[part // 2])
            return part == 3
        cores[t].wait_recv()
        dst = rc[i] if kind == "n" else rc[i].at[part]
        add_into(dst, mine.at[:, :, c], dst)
        return kind == "n" or part == 3

    def views(i):
        kind, h = items[i][0], half(i)
        r, a, b = rc[i], r1a[i], r1b[i]
        here, there = lanes(x), lanes(1 - x)
        if kind == "n":
            one = (r.at[:, 1 - y, 0:h, :], r.at[:, :, h:RB, there], r.at[:, y, 0:h, :], r.at[:, :, h:RB, here])
            two = (a.at[:, :, there], b.at[:, 1 - y], a.at[:, :, here], b.at[:, y])
            parts = (s3[i].at[:, 0:h, :], s3[i].at[:, h:RB, :])
        elif kind == "t":
            up, down = pl.ds(2 * y, 2), pl.ds(2 * (1 - y), 2)
            one = (r.at[:, down, 0], r.at[:, :, 1, :, there], r.at[:, up, 0], r.at[:, :, 1, :, here])
            two = (a.at[:, :, :, there], b.at[:, down], a.at[:, :, :, here], b.at[:, up])
            parts = (s3[i].at[:, 0], s3[i].at[:, 1])
        else:
            one = (r.at[:, :, 1 - y, 0], r.at[1 - x, :, :, 1], r.at[:, :, y, 0], r.at[x, :, :, 1])
            two = (a.at[1 - x], b.at[:, 1 - y], a.at[x], b.at[:, y])
            parts = (s3[i].at[:, 0], s3[i].at[:, 1])
        return one, two, parts

    def send_1(i):
        (over_y, over_x, _, _), _, _ = views(i)
        ones[i] = [
            start(remote(over_y, r1a[i], ysend.at[i, 0], yrecv.at[i, 0], yp)),
            start(remote(over_x, r1b[i], xsend.at[i, 0], xrecv.at[i, 0], xp)),
        ]

    def send_2(i):
        (_, _, stay_a, stay_b), (over_x, over_y, _, _), _ = views(i)
        ones[i][0].wait_recv()
        add_into(r1a[i], stay_a, r1a[i])
        first = start(remote(over_x, r2a[i], xsend.at[i, 1], xrecv.at[i, 1], xp))
        ones[i][1].wait_recv()
        add_into(r1b[i], stay_b, r1b[i])
        twos[i] = [first, start(remote(over_y, r2b[i], ysend.at[i, 1], yrecv.at[i, 1], yp))]

    def send_z(i):
        _, (_, _, stay_a, stay_b), (part_a, part_b) = views(i)
        twos[i][0].wait_recv()
        add_into(part_a, stay_a, r2a[i])
        twos[i][1].wait_recv()
        add_into(part_b, stay_b, r2b[i])
        threes[i] = [
            start(remote(s3[i].at[(z + j + 1) % 4], rz[i].at[j], zsend.at[i, j], zrecv.at[i, j], zs[j]))
            for j in range(3)
        ]

    finals = []

    def finish(i):
        kind, _, out, tap = items[i]
        for copy in threes[i]:
            copy.wait_recv()
        acc = s3[i][z].astype(F32)
        for j in range(3):
            acc = acc + rz[i][j].astype(F32)
        dst = outs[out] if tap is None else outs[out].at[tap]
        if kind in "wm":
            dst[...] = acc
            return
        mine = acc[..., : LANES // 2]
        theirs = acc[..., LANES // 2 :]
        keep = jnp.where(c == 0, mine, theirs)
        other = jnp.where(c == 0, theirs, mine)
        if kind == "n":
            sbuf[i][...] = other
            dst[c] = keep
            finals.append(start(remote(sbuf[i], dst.at[c], fsend.at[i], frecv.at[i], cp)))
            return
        for a in (0, 1):
            for b in (0, 1):
                dst[b, a, c] = keep[a, b]
                sbuf[i][b, a] = other[a, b]
        finals.append(start(remote(sbuf[i], dst.at[:, :, c], fsend.at[i], frecv.at[i], cp)))

    g = [i for i in range(n) if items[i][0] == "m"][0]
    last = len(jobs)
    theirs = start(remote(ins[-1].at[:, 1 - c], rc[g], csend.at[last], crecv.at[last], cp))
    mine = pltpu.make_async_copy(ins[-1].at[:, c], given, loads.at[0, 2])
    mine.start()
    load(0)
    load(1)
    queue = [[], [], []]
    steps = (send_2, send_z, finish)

    def advance(keep):
        for k in (2, 1, 0):
            while len(queue[k]) > keep:
                i = queue[k].pop(0)
                steps[k](i)
                if k < 2:
                    queue[k + 1].append(i)

    mine.wait()
    for t in range(last + 1):
        if t < last:
            compute(t)
        if t == 1:
            theirs.wait_recv()
            add_into(rc[g], given, rc[g])
            send_1(g)
            queue[0].append(g)
        if t >= 1 and add_own(t - 1):
            i = jobs[t - 1][0]
            send_1(i)
            queue[0].append(i)
        advance(LAG)
    for keep in range(LAG - 1, -1, -1):
        advance(keep)
    while queue[0] or queue[1] or queue[2]:
        advance(0)
    for copy in finals:
        copy.wait_recv()
    for copy in started:
        copy.wait_send()
    for t in cores:
        if t + RING >= last or items[jobs[t][0]][1] == F32:
            cores[t].wait_send()


RING = 3
LAG = 1


def reduce_fast(items, jobs, ins, out_shapes):
    n, m = len(items), len(jobs)
    sem = pltpu.SemaphoreType.DMA
    groups = [[] for _ in range(8)]
    for i, (kind, dtype, _, _) in enumerate(items):
        for group, shape in zip(groups, item_shapes(kind, halves_of(i))):
            group.append(pltpu.VMEM(shape, dtype))
        last = {"n": (RB, LANES // 2), "t": (2, 2, RB, LANES // 2)}.get(kind, (8, 128))
        groups[7].append(pltpu.VMEM(last, F32))
    scratch = [s for group in groups for s in group]
    scratch += [
        pltpu.VMEM((RING, 4, 2, 2, RB, D), BF),
        pltpu.VMEM((4, 2, 2, RB, D), F32),
        pltpu.VMEM((2, 4, 2, 2, MISC_ROWS // 2, D), BF),
    ]
    most = max(j[4] for j in jobs)
    scratch += [pltpu.VMEM((2, most, D), BF)] * 2
    scratch += [sem((2, 3)), sem((m + 1,)), sem((m + 1,))]
    scratch += [sem((n, 2))] * 4 + [sem((n, 3))] * 2 + [sem((n,))] * 2
    return pl.pallas_call(
        functools.partial(reduce_kernel, items, jobs, len(ins), len(out_shapes)),
        out_shape=[jax.ShapeDtypeStruct(s, F32) for s in out_shapes],
        in_specs=[pl.BlockSpec(memory_space=pl.ANY)] * len(ins),
        out_specs=[pl.BlockSpec(memory_space=pltpu.VMEM)] * len(out_shapes),
        scratch_shapes=scratch,
        compiler_params=pltpu.CompilerParams(
            collective_id=2, has_side_effects=True, vmem_limit_bytes=62 << 20
        ),
    )(*ins)


def lanes_of(pair):
    return pl.ds(pl.multiple_of(pair * PAIR, PAIR), PAIR)


def clip_partners():
    d, s = lax.axis_index("dp"), lax.axis_index("seq")
    x, c = s // 2, s % 2
    return (d, (1 - x) * 2 + c), (d, x * 2 + 1 - c)


def greet_pair(xp, cp):
    barrier = pltpu.get_barrier_semaphore()
    for dev in (xp, cp):
        pl.semaphore_signal(barrier, inc=1, device_id=dev, device_id_type=MESH)
    pl.semaphore_wait(barrier, 2)


def forward_head(q_one, k_slab, v_slab, half, count):
    s = masked(tdot(k_slab, q_one, 1, 1), count)
    top = jnp.max(s, axis=0, keepdims=True)
    e = jnp.exp(s - top)
    total = jnp.sum(e, axis=0, keepdims=True)
    mixed = tdot(v_slab, e.astype(BF), 0, 0)[half * HEAD : (half + 1) * HEAD]
    return mixed / total, top + jnp.log(total)


def forward_pair(pair, q, k, v, o, lse, count):
    at = lanes_of(pair)
    q_slab, k_slab, v_slab = q[:, at], k[:, at], v[:, at]
    both = []
    for half in (0, 1):
        mixed, log_sum = forward_head(one_head(q_slab, half), k_slab, v_slab, half, count)
        both.append(mixed)
        lse[pl.ds(2 * pair + half, 1), :] = log_sum
    o[:, at] = jnp.concatenate(both, axis=0).T.astype(o.dtype)


def backward_pair(pair, q, k, v, up, lse, dq, dk, dv, count, known):
    at = lanes_of(pair)
    q_slab, k_slab, v_slab, u_slab = q[:, at], k[:, at], v[:, at], up[:, at]
    both, dk_sum, dv_sum = [], 0.0, 0.0
    for half in (0, 1):
        row = pl.ds(2 * pair + half, 1)
        q_one, u_one = one_head(q_slab, half), one_head(u_slab, half)
        p = jnp.exp(masked(tdot(k_slab, q_one, 1, 1), count) - lse[row, :])
        dp = tdot(v_slab, u_one, 1, 1)
        if known is None:
            mass = jnp.sum(p, axis=0, keepdims=True)
            inner = jnp.sum(p * dp, axis=0, keepdims=True) / mass
        else:
            inner = known[row, :]
        ds = (p * (dp - inner)).astype(BF)
        dv_sum = dv_sum + tdot(p.astype(BF), u_one, 1, 0)
        dk_sum = dk_sum + tdot(ds, q_one, 1, 0)
        both.append(tdot(k_slab, ds, 0, 0)[half * HEAD : (half + 1) * HEAD])
    dq[:, at] = jnp.concatenate(both, axis=0).T.astype(dq.dtype)
    dk[:, at] = dk_sum.astype(dk.dtype)
    dv[:, at] = dv_sum.astype(dv.dtype)


def attend_kernel(causal, *refs):
    count = refs[0] if causal else None
    q, k, v, o, lse = refs[1:] if causal else refs

    def step(pair, _):
        forward_pair(pair, q, k, v, o, lse, count)
        return 0

    lax.fori_loop(0, HEADS // 2, step, 0)


def sums_kernel(q, k, v, up, lse, mass, inner):
    def step(pair, _):
        at = lanes_of(pair)
        q_slab, k_slab, v_slab, u_slab = q[:, at], k[:, at], v[:, at], up[:, at]
        for half in (0, 1):
            row = pl.ds(2 * pair + half, 1)
            p = jnp.exp(tdot(k_slab, one_head(q_slab, half), 1, 1) - lse[row, :])
            dp = tdot(v_slab, one_head(u_slab, half), 1, 1)
            mass[row, :] = jnp.sum(p, axis=0, keepdims=True)
            inner[row, :] = jnp.sum(p * dp, axis=0, keepdims=True)
        return 0

    lax.fori_loop(0, HEADS // 2, step, 0)


def back_kernel(causal, given, *refs):
    count, known = None, None
    if causal:
        count, refs = refs[0], refs[1:]
    q, k, v, up, lse = refs[:5]
    refs = refs[5:]
    if given:
        known, refs = refs[0], refs[1:]
    dq, dk, dv = refs

    def step(pair, _):
        backward_pair(pair, q, k, v, up, lse, dq, dk, dv, count, known)
        return 0

    lax.fori_loop(0, HEADS // 2, step, 0)


def clip_attend_kernel(q, k, v, o, lse, k_all, v_all, xsend, xrecv, csend, crecv):
    xp, cp = clip_partners()
    r = q.shape[0]
    greet_pair(xp, cp)
    pairs = HEADS // 2

    def across(pair):
        at = lanes_of(pair)
        return [
            remote(src.at[:, at], dst.at[r : 2 * r, at], xsend.at[j, pair], xrecv.at[j, pair], xp)
            for j, (src, dst) in enumerate(((k, k_all), (v, v_all)))
        ]

    def beside(pair):
        at = lanes_of(pair)
        return [
            remote(a.at[0 : 2 * r, at], a.at[2 * r : 4 * r, at], csend.at[j, pair], crecv.at[j, pair], cp)
            for j, a in enumerate((k_all, v_all))
        ]

    for pair in range(pairs):
        for copy in across(pair):
            copy.start()
    k_all[0:r, :] = k[...]
    v_all[0:r, :] = v[...]

    def pass_on(pair):
        for copy in across(pair):
            copy.wait_recv()
        for copy in beside(pair):
            copy.start()

    pass_on(0)

    def step(pair, _):
        @pl.when(pair + 1 < pairs)
        def _():
            pass_on(pair + 1)

        for copy in beside(pair):
            copy.wait_recv()
        forward_pair(pair, q, k_all, v_all, o, lse, None)
        return 0

    lax.fori_loop(0, pairs, step, 0)
    for pair in range(pairs):
        for copy in across(pair) + beside(pair):
            copy.wait_send()


def clip_back_kernel(q, k, v, up, lse, dq, dk, dv, *refs):
    k_sum, v_sum, k_near, v_near, k_far, v_far, xsend, xrecv, csend, crecv = refs
    xp, cp = clip_partners()
    r = q.shape[0]
    greet_pair(xp, cp)
    pairs = HEADS // 2
    sums, nears, fars, outs = (k_sum, v_sum), (k_near, v_near), (k_far, v_far), (dk, dv)

    def beside(pair):
        at = lanes_of(pair)
        return [
            remote(sums[j].at[2 * r : 4 * r, at], nears[j].at[:, at], csend.at[j, pair], crecv.at[j, pair], cp)
            for j in (0, 1)
        ]

    def across(pair):
        at = lanes_of(pair)
        return [
            remote(sums[j].at[r : 2 * r, at], fars[j].at[:, at], xsend.at[j, pair], xrecv.at[j, pair], xp)
            for j in (0, 1)
        ]

    def step(t, _):
        @pl.when(t < pairs)
        def _():
            backward_pair(t, q, k, v, up, lse, dq, k_sum, v_sum, None, None)
            for copy in beside(t):
                copy.start()

        @pl.when((t >= 1) & (t <= pairs))
        def _():
            pair = t - 1
            at = lanes_of(pair)
            for copy in beside(pair):
                copy.wait_recv()
            for j in (0, 1):
                near = sums[j][0 : 2 * r, at].astype(F32) + nears[j][:, at].astype(F32)
                sums[j][0 : 2 * r, at] = near.astype(BF)
            for copy in across(pair):
                copy.start()

        @pl.when(t >= 2)
        def _():
            pair = t - 2
            at = lanes_of(pair)
            for copy in across(pair):
                copy.wait_recv()
            for j in (0, 1):
                total = sums[j][0:r, at].astype(F32) + fars[j][:, at].astype(F32)
                outs[j][:, at] = total.astype(BF)

        return 0

    lax.fori_loop(0, pairs + 2, step, 0)
    for pair in range(pairs):
        for copy in across(pair) + beside(pair):
            copy.wait_send()


def local_call(kernel, out_shape, args, cost, count=None, scratch=(), barrier=None):
    vmem = pl.BlockSpec(memory_space=pltpu.VMEM)
    specs = [vmem] * len(args)
    if count is not None:
        specs, args = [pl.BlockSpec(memory_space=pltpu.SMEM)] + specs, [count] + args
    params = dict(vmem_limit_bytes=56 << 20)
    if barrier is not None:
        params.update(collective_id=barrier, has_side_effects=True)
    return pl.pallas_call(
        kernel,
        out_shape=[jax.ShapeDtypeStruct(s, t) for s, t in out_shape],
        in_specs=specs,
        out_specs=[vmem] * len(out_shape),
        scratch_shapes=list(scratch),
        cost_estimate=pl.CostEstimate(flops=cost, bytes_accessed=8 << 20, transcendentals=0),
        compiler_params=pltpu.CompilerParams(**params),
    )(*args)


def rows_cost(q, k):
    return 8 * q.shape[0] * k.shape[0] * D


def attend(q, k, v, count=None):
    shapes = [(q.shape, BF), ((HEADS, q.shape[0]), F32)]
    kernel = functools.partial(attend_kernel, count is not None)
    return local_call(kernel, shapes, [q, k, v], rows_cost(q, k), count)


def attend_sums(q, k, v, up, lse):
    return local_call(sums_kernel, [(lse.shape, F32)] * 2, [q, k, v, up, lse], rows_cost(q, k))


def attend_back(q, k, v, up, lse, count=None, inner=None, out=BF):
    shapes = [(q.shape, out), (k.shape, BF), (k.shape, BF)]
    kernel = functools.partial(back_kernel, count is not None, inner is not None)
    args = [q, k, v, up, lse] + ([] if inner is None else [inner])
    return local_call(kernel, shapes, args, 3 * rows_cost(q, k), count)


def clip_attend(q, k, v):
    r = k.shape[0]
    shapes = [(q.shape, BF), ((HEADS, r), F32), ((4 * r, D), BF), ((4 * r, D), BF)]
    sems = [pltpu.SemaphoreType.DMA((2, HEADS // 2))] * 4
    return local_call(clip_attend_kernel, shapes, [q, k, v], 4 * rows_cost(q, k), None, sems, 3)


def clip_attend_back(q, k_all, v_all, up, lse):
    r = q.shape[0]
    scratch = [pltpu.VMEM((4 * r, D), BF)] * 2 + [pltpu.VMEM((2 * r, D), BF)] * 2
    scratch += [pltpu.VMEM((r, D), BF)] * 2 + [pltpu.SemaphoreType.DMA((2, HEADS // 2))] * 4
    args = [q, k_all, v_all, up, lse]
    return local_call(clip_back_kernel, [(q.shape, BF)] * 3, args, 3 * rows_cost(q, k_all), None, scratch, 4)


def mlp_kernel(stream, gain, bias, expand, contract, normed, pre, hidden, out):
    @pl.when(pl.program_id(0) == 0)
    def _():
        normed[...] = norm(stream[...], gain[...], bias[...])
        out[...] = stream[...]

    before = tdot(normed[...], expand[0], 1, 0)
    pre[0] = before
    after = gelu(before).astype(BF)
    hidden[0] = after
    out[...] += tdot(after, contract[0], 1, 0)


def mlp_back_kernel(up, stream, gain, pre, expand, contract, out, d_low, d_pre, d_gain, d_bias, total):
    s = pl.program_id(0)

    @pl.when(s == 0)
    def _():
        d_low[...] = up[...].astype(BF)
        total[...] = jnp.zeros_like(total)

    d_hidden = low(tdot(d_low[...], contract[0], 1, 1))
    grad = (gelu_slope(pre[0]) * d_hidden).astype(BF)
    d_pre[0] = grad
    total[...] += tdot(grad, expand[0], 1, 1)

    @pl.when(s == pl.num_programs(0) - 1)
    def _():
        hat, inv = norm_parts(stream[...])
        g = total[...] * gain[...]
        mean = lambda v: jnp.mean(v, axis=-1, keepdims=True)
        out[...] = up[...] + inv * (g - mean(g) - hat * mean(g * hat))
        d_gain[...] = jnp.sum(total[...] * hat, axis=0, keepdims=True)
        d_bias[...] = jnp.sum(total[...], axis=0, keepdims=True)


def blocks(kernel, grid, ins, outs, args, cost, scratch=()):
    def spec(shape, cut):
        if cut:
            return pl.BlockSpec((1,) + shape[1:], lambda s: (s,) + (0,) * (len(shape) - 1))
        return pl.BlockSpec(shape, lambda s: (0,) * len(shape))

    return pl.pallas_call(
        kernel,
        grid=(grid,),
        out_shape=[jax.ShapeDtypeStruct(s, t) for s, t, _ in outs],
        in_specs=[spec(a.shape, cut) for a, cut in zip(args, ins)],
        out_specs=[spec(s, cut) for s, _, cut in outs],
        scratch_shapes=list(scratch),
        cost_estimate=pl.CostEstimate(flops=cost, bytes_accessed=16 << 20, transcendentals=0),
        compiler_params=pltpu.CompilerParams(vmem_limit_bytes=48 << 20),
    )(*args)


def mlp(stream, gain, bias, expand, contract):
    n, (r, _) = expand.shape[0], stream.shape
    outs = [((r, D), BF, False), ((n, r, D), F32, True), ((n, r, D), BF, True), ((r, D), F32, False)]
    args = [stream, gain[None], bias[None], expand, contract.reshape(n, D, D)]
    return blocks(mlp_kernel, n, [False] * 3 + [True] * 2, outs, args, 4 * n * r * D * D)


def mlp_backward(up, stream, gain, pre, expand, contract):
    n, (r, _) = expand.shape[0], stream.shape
    outs = [((r, D), F32, False), ((r, D), BF, False), ((n, r, D), BF, True)]
    outs += [((1, D), F32, False)] * 2
    args = [up, stream, gain[None], pre, expand, contract.reshape(n, D, D)]
    scratch = [pltpu.VMEM((r, D), F32)]
    return blocks(mlp_back_kernel, n, [False] * 3 + [True] * 3, outs, args, 4 * n * r * D * D, scratch)


SQUARE = (4, 5, 6, 7, 18, 19, 20, 21, 24, 25, 26, 27)
TALL = (11, 31)
BROAD = (10, 30)
VECTORS = tuple(i for i in range(32) if KINDS[i] == "v")
MISC_ROWS = 32


def plan_gather(shards):
    g, shapes, first, at = [], [], 0, 0
    for i in SQUARE + (1,) + TALL:
        w = shards[i]
        rows = w.shape[-2] // 2
        one = (4, 2, 2, rows, D)
        for tap in range(w.shape[0]) if w.ndim == 3 else (None,):
            g.append((0, first, rows, len(shapes), tap, False))
            first += rows
        shapes.append(one if w.ndim == 2 else (w.shape[0],) + one)
    for i in BROAD:
        rows = shards[i].shape[0]
        g.append((1, at, rows, len(shapes), None, True))
        at += rows
        shapes.append((2, 2, 4, 2, rows, D))
    g.append((2, 0, MISC_ROWS, len(shapes), None, True))
    shapes.append((2, 2, 4, 2, MISC_ROWS, D))
    return g, shapes


def by_core(c, zero, one):
    return jnp.where(c == 0, zero, one)


def narrow_halves(shards):
    parts = []
    for i in SQUARE + (1,) + TALL:
        w = shards[i].reshape(-1, 2, shards[i].shape[-2] // 2, shards[i].shape[-1])
        parts += [w[t] for t in range(w.shape[0])]
    return jnp.concatenate(parts, axis=1)


def gather_weights(shards, ids):
    c = lax.axis_index("seq") % 2
    g, shapes = plan_gather(shards)
    halves = narrow_halves(shards)
    mine = by_core(c, halves[0], halves[1])
    got = lax.ppermute(by_core(c, halves[1], halves[0]), "seq", SWAP)
    narrow = by_core(
        c, jnp.concatenate([mine, got], axis=1), jnp.concatenate([got, mine], axis=1)
    )
    broad = jnp.concatenate([shards[i] for i in BROAD], axis=0)
    flat = [shards[i].reshape(-1) for i in (0,) + VECTORS + (15,)]
    flat += [(ids // 256).astype(BF), (ids % 256).astype(BF)]
    size = sum(f.size for f in flat)
    flat.append(jnp.zeros((MISC_ROWS * D - size,), BF))
    misc = jnp.concatenate(flat).reshape(MISC_ROWS, D)
    outs = gather_fast(g, [narrow, broad, misc], shapes)
    full = [None] * 32
    for k, i in enumerate(SQUARE + (1,) + TALL):
        full[i] = outs[k].reshape(shards[i].shape[:-2] + (8 * shards[i].shape[-2], D))
    for k, i in enumerate(BROAD):
        full[i] = outs[15 + k].reshape(4, D, D)
    misc = outs[17].reshape(2, 2, 4, 2, MISC_ROWS * D)
    at = 0
    t, a, b = shards[0].shape
    full[0] = (
        misc[..., : shards[0].size]
        .reshape(2, 2, 4, 2, t, a, b)
        .transpose(4, 0, 1, 5, 2, 3, 6)
        .reshape(t, 4 * a, 8 * b)
    )
    at += shards[0].size
    n = shards[VECTORS[0]].size
    vecs = misc[..., at : at + n * len(VECTORS)].reshape(2, 2, 4, 2, len(VECTORS), n)
    vecs = vecs.transpose(4, 2, 3, 0, 1, 5).reshape(len(VECTORS), D)
    for k, i in enumerate(VECTORS):
        full[i] = vecs[k]
    at += n * len(VECTORS)
    r, w = shards[15].shape
    full[15] = (
        misc[..., at : at + r * w]
        .reshape(2, 2, 4, 2, r, w)
        .transpose(2, 3, 4, 0, 1, 5)
        .reshape(8 * r, 4 * w)
    )
    at += r * w
    both = misc[..., at : at + 2 * ids.size].reshape(2, 2, 4, 2, 2, ids.size).astype(jnp.int32)
    all_ids = (both[..., 0, :] * 256 + both[..., 1, :]).transpose(2, 3, 0, 1, 4).reshape(-1)
    return full, all_ids


ORDER = (31, 30, 27, 24, 21, 18, 19, 20, 11, 10, 25, 26, 7, 4, 5, 6, 1)
EXACT = 25


def reduce_grads(grads, shards):
    items, jobs, ins, shapes, seen = [], [], [], [], {}

    def place(v):
        if id(v) not in seen:
            seen[id(v)] = len(ins)
            ins.append(v)
        return seen[id(v)]

    for i in ORDER:
        left, right = grads[i]
        if i in TALL:
            jobs += [(len(items), s, place(left), place(right), left.shape[1]) for s in range(4)]
            items.append(("t", BF, len(shapes), None))
            shapes.append((2, 2, 2, RB, LANES // 2))
        elif i in BROAD:
            jobs += [(len(items), s, place(left), place(right), left.shape[0]) for s in range(4)]
            items.append(("w", BF, len(shapes), None))
            shapes.append((2, RB, D))
        elif i == 1:
            for tap, l in enumerate(left):
                jobs.append((len(items), 0, place(l), place(right), l.shape[0]))
                items.append(("n", BF, len(shapes), tap))
            shapes.append((3, 2, RB, LANES // 2))
        else:
            jobs.append((len(items), 0, place(left), place(right), left.shape[0]))
            items.append(("n", F32 if i == EXACT else BF, len(shapes), None))
            shapes.append((2, RB, LANES // 2))
    t, a, b = shards[0].shape
    conv1 = grads[0].reshape(t, 2, 2, a, 4, 2, b).transpose(1, 2, 4, 5, 0, 3, 6)
    n = shards[VECTORS[0]].size
    vecs = jnp.stack([grads[i] for i in VECTORS]).reshape(-1, 4, 2, 2, 2, n)
    flat = [conv1.reshape(2, 2, 4, 2, -1), vecs.transpose(3, 4, 1, 2, 0, 5).reshape(2, 2, 4, 2, -1)]
    size = sum(f.shape[-1] for f in flat)
    flat.append(jnp.zeros((2, 2, 4, 2, MISC_ROWS * D - size), F32))
    ins.append(jnp.concatenate(flat, axis=-1).astype(BF).reshape(2, 2, 4, 2, 2, MISC_ROWS // 2, D))
    items.append(("m", BF, len(shapes), None))
    shapes.append((2, MISC_ROWS // 2, D))
    got = reduce_fast(items, jobs, ins, shapes)
    out = [None] * 32
    for i, v in zip(ORDER, got):
        out[i] = v.reshape(shards[i].shape)
    misc = got[-1].reshape(-1)
    out[0] = misc[: shards[0].size].reshape(shards[0].shape)
    at = shards[0].size
    for i in VECTORS:
        out[i] = misc[at : at + n]
        at += n
    return out


def one_hot(ids, table):
    first = lax.axis_index("dp") * table.shape[0]
    return ((ids - first)[:, None] == jnp.arange(table.shape[0])[None, :]).astype(BF)


def body(mel_frames, token_ids, token_counts, *rest):
    shards, cotangent = list(rest[:32]), rest[32][0]
    table = shards[14]
    dps, seqs = lax.axis_size("dp"), lax.axis_size("seq")
    me = lax.axis_index("seq")
    slots = token_ids.shape[1]
    all_slots = slots * seqs
    frames = mel_frames.shape[1] // 2

    fast = dps == 8 and seqs == 4
    weights = shards[:14] + [None] + shards[15:]
    if fast:
        full, ids = gather_weights(weights, token_ids[0])
    else:
        full, ids = gather_plain(weights), lax.all_gather(token_ids[0], BOTH, axis=0, tiled=True)
    hot = one_hot(ids, table)
    looked = mm(hot, table, BF)
    mine = lax.psum_scatter(looked, "dp", scatter_dimension=0, tiled=True)

    vec = {i: full[i].astype(F32) for i in range(32) if KINDS[i] == "v"}
    conv1, conv2, position = full[0].reshape(-1, D), full[1], full[15]
    eq, ek, ev, eo = full[4:8]
    ee, ec = full[10:12]
    dq_w, dk_w, dv_w, do_w = full[18:22]
    cq_w, ck_w, cv_w, co_w = full[24:28]
    de, dc = full[30:32]

    pairs = extended(mel_frames[0], 2).reshape(frames + 2, -1)
    mels = mel_frames.shape[2]
    n = frames + 1
    even_in = jnp.concatenate([pairs[:n], pairs[1:, :mels]], axis=1)
    odd_in = jnp.concatenate([pairs[:n, mels:], pairs[1:]], axis=1)
    even_pre, odd_pre = mm(even_in, conv1), mm(odd_in, conv1)
    row = jnp.arange(n)[:, None]
    even_keep = (row > 0) | (me > 0)
    odd_keep = (row < n - 1) | (me < seqs - 1)
    even = jnp.where(even_keep, gelu(even_pre), 0.0).astype(BF)
    odd = jnp.where(odd_keep, gelu(odd_pre), 0.0).astype(BF)
    second_pre = mm(even[:frames], conv2[0]) + mm(odd[:frames], conv2[1]) + mm(even[1:], conv2[2])
    stream0 = gelu(second_pre) + sinusoid(me * frames, frames)

    enc_normed = norm(stream0, vec[2], vec[3])
    q = (mm(enc_normed, eq) * SCALE).astype(BF)
    k = mm(enc_normed, ek, BF)
    v = mm(enc_normed, ev, BF)
    enc_mixed, enc_lse, k_all, v_all = clip_attend(q, k, v)
    stream1 = stream0 + mm(enc_mixed, eo)
    enc_mlp_normed, enc_pre, enc_hidden, stream2 = mlp(stream1, vec[8], vec[9], ee, ec)
    memory = norm(stream2, vec[12], vec[13])
    mk = mm(memory, ck_w, BF)
    mv = mm(memory, cv_w, BF)

    mine, enc_mixed = lax.optimization_barrier((mine, enc_mixed))
    looked = lax.all_gather(mine, "seq", axis=0, tiled=True)
    looked = looked.reshape(seqs, all_slots, D // seqs).transpose(1, 0, 2).reshape(all_slots, D)
    place = jnp.arange(all_slots)
    embedded = looked.astype(F32) + position.astype(F32)
    dec_normed = norm(embedded, vec[16], vec[17])
    sq = (mm(dec_normed, dq_w) * SCALE).astype(BF)
    sk = mm(dec_normed, dk_w, BF)
    sv = mm(dec_normed, dv_w, BF)
    dec_mixed, dec_lse = attend(sq, sk, sv, token_counts)
    stream4 = embedded + mm(dec_mixed, do_w)
    cross_normed = norm(stream4, vec[22], vec[23])
    xq = (mm(cross_normed, cq_w) * SCALE).astype(BF)

    part, part_lse = attend(xq, mk, mv)
    parts, lses = unpack(exchange(pack(part, part_lse)))
    top = jnp.max(lses, axis=0)
    share = jnp.exp(lses - top)
    total = jnp.sum(share, axis=0)
    cross_lse = top + jnp.log(total)
    share = share / total
    cross_mixed = jnp.sum(
        parts.astype(F32).reshape(seqs, slots, HEADS, HEAD) * share[..., None], axis=0
    ).reshape(slots, D)
    cross_mixed = cross_mixed.astype(BF)

    own = lambda a: lax.dynamic_slice_in_dim(a, me * slots, slots, 0)
    stream4 = own(stream4)
    stream5 = stream4 + mm(cross_mixed, co_w)
    dec_mlp_normed, dec_pre, dec_hidden, stream6 = mlp(stream5, vec[28], vec[29], de, dc)
    live = (own(place) < token_counts[0])[:, None]
    decoded = jnp.where(live, stream6, 0.0).astype(BF)

    grads = [None] * 32

    def mlp_back(ex, co, gain, normed, pre, hidden, stream, up):
        up, d_low, d_pre, d_gain, d_bias = mlp_backward(up, stream, vec[gain], pre, full[ex], full[co])
        grads[co], grads[ex] = (hidden, d_low), (normed, d_pre)
        grads[gain], grads[gain + 1] = d_gain[0], d_bias[0]
        return up

    up = jnp.where(live, cotangent.astype(F32), 0.0)
    up = mlp_back(30, 31, 28, dec_mlp_normed, dec_pre, dec_hidden, stream5, up)
    d_low = up.astype(BF)
    grads[27] = (cross_mixed, d_low)
    d_mixed = mm_t(d_low, co_w, BF)
    d_mixed, lse_all = unpack(lax.all_gather(pack(d_mixed, cross_lse.T), "seq", axis=0, tiled=True))
    lse_all = lse_all.T
    sums = lax.psum(jnp.stack(attend_sums(xq, mk, mv, d_mixed, lse_all)), "seq")
    dxq, dmk, dmv = attend_back(xq, mk, mv, d_mixed, lse_all, inner=sums[1] / sums[0], out=F32)
    dxq = jnp.sum(exchange(dxq), axis=0)
    dxq = (low(dxq) * SCALE).astype(BF)
    grads[24] = (own(cross_normed), dxq)
    back, grads[22], grads[23] = norm_back(stream4, vec[22], mm_t(dxq, cq_w))
    up = up + back
    d_low = up.astype(BF)
    grads[21] = (own(dec_mixed), d_low)
    d_mixed = lax.all_gather(mm_t(d_low, do_w, BF), "seq", axis=0, tiled=True)
    dsq, dsk, dsv = attend_back(sq, sk, sv, d_mixed, dec_lse, token_counts)

    def inputs_back(first, gain, normed, stream, dq, dk, dv, up):
        dq = (dq.astype(F32) * SCALE).astype(BF)
        total = 0.0
        for i, g in enumerate((dq, dk, dv)):
            grads[first + i] = (normed, g)
            total = total + mm_t(g, full[first + i])
        back, grads[gain], grads[gain + 1] = norm_back(stream, vec[gain], total)
        return up + back

    up = inputs_back(18, 16, own(dec_normed), own(embedded), own(dsq), own(dsk), own(dsv), up)

    cols = exchange_columns(up.astype(BF))
    every = lax.all_gather(cols, "dp", axis=0, tiled=True)
    grad_table = dot(hot, every, 0, 0)
    per_clip = every.reshape(dps, dps, -1, D // seqs)
    grad_position = jnp.sum(
        lax.dynamic_index_in_dim(per_clip, lax.axis_index("dp"), 1, False).astype(F32), axis=0
    )

    grads[25] = (memory, dmk)
    grads[26] = (memory, dmv)
    up, grads[12], grads[13] = norm_back(stream2, vec[12], mm_t(dmk, ck_w) + mm_t(dmv, cv_w))
    up = mlp_back(10, 11, 8, enc_mlp_normed, enc_pre, enc_hidden, stream1, up)
    d_low = up.astype(BF)
    grads[7] = (enc_mixed, d_low)
    d_mixed = mm_t(d_low, eo, BF)
    dq, dk, dv = clip_attend_back(q, k_all, v_all, d_mixed, enc_lse)
    up = inputs_back(4, 2, enc_normed, stream0, dq, dk, dv, up)

    d_second = (gelu_slope(second_pre) * up).astype(BF)
    grads[1] = ([even[:frames], odd[:frames], even[1:]], d_second)
    rim = extended(d_second, 1)
    d_even = mm_t(rim[1:], conv2[0]) + mm_t(rim[:n], conv2[2])
    d_odd = mm_t(rim[1:], conv2[1])
    d_even = jnp.where(even_keep, gelu_slope(even_pre) * low(d_even), 0.0).astype(BF)
    d_odd = jnp.where(odd_keep, gelu_slope(odd_pre) * low(d_odd), 0.0).astype(BF)
    grads[0] = (outer(odd_in[:frames], d_odd[:frames], F32) + outer(even_in[1:], d_even[1:], F32)).reshape(
        3, mels, D
    )
    me_g, mo_g = mm_t(d_even, conv1), mm_t(d_odd, conv1)
    mel_grad = jnp.concatenate(
        [
            me_g[1:, :mels] + me_g[:-1, 2 * mels :] + mo_g[:-1, mels : 2 * mels],
            me_g[1:, mels : 2 * mels] + mo_g[1:, :mels] + mo_g[:-1, 2 * mels :],
        ],
        axis=1,
    ).reshape(1, 2 * frames, mels)

    done = (reduce_grads if fast else reduce_plain)(grads, shards)
    done[14], done[15] = grad_table, grad_position
    return tuple([decoded[None], mel_grad] + done)


def exchange_columns(v):
    n = lax.axis_size("seq")
    wide = v.shape[1] // n
    v = v.reshape(v.shape[0], n, wide).transpose(1, 0, 2)
    return lax.all_to_all(v, "seq", split_axis=0, concat_axis=0, tiled=True).reshape(-1, wide)


def solution(mesh):
    place = {
        "1": P(None, "seq", "dp"),
        "2": P(None, "dp", "seq"),
        "v": P(BOTH),
        "m": P("dp", "seq"),
        "t": P("dp", "seq"),
    }
    rows = P("dp", "seq", None)
    weights = tuple(place[k] for k in KINDS)
    return jax.shard_map(
        body,
        mesh=mesh,
        in_specs=(rows, P("dp", "seq"), P("dp")) + weights + (rows,),
        out_specs=(rows, rows) + weights,
        check_vma=False,
    )
```

```python
import functools
import math

import jax
import jax.numpy as jnp
from jax import lax
from jax.experimental import pallas as pl
from jax.experimental.pallas import tpu as pltpu
from jax.sharding import PartitionSpec as P

D = 768
HEADS = 12
HEAD = 64
EPSILON = 1e-05
NEGATIVE = -1e30
SCALE = 1.0 / math.sqrt(HEAD)
BF = jnp.bfloat16
F32 = jnp.float32
BOTH = ("dp", "seq")

KINDS = "12vvmmmmvvmmvvtmvvmmmmvvmmmmvvmm"


def dot(a, b, ca, cb, out=F32):
    return lax.dot_general(a, b, (((ca,), (cb,)), ((), ())), preferred_element_type=F32).astype(out)


def mm(a, b, out=F32):
    return dot(a, b, 1, 0, out)


def mm_t(a, b, out=F32):
    return dot(a, b, 1, 1, out)


def outer(a, b, out=BF):
    return dot(a, b, 0, 0, out)


def norm_parts(values):
    center = values - jnp.mean(values, axis=-1, keepdims=True)
    spread = jnp.mean(center * center, axis=-1, keepdims=True)
    inv = lax.rsqrt(spread + EPSILON)
    return center * inv, inv


def norm(values, gain, bias):
    return (norm_parts(values)[0] * gain + bias).astype(BF)


def norm_back(values, gain, up):
    hat, inv = norm_parts(values)
    g = up * gain
    back = inv * (
        g - jnp.mean(g, axis=-1, keepdims=True) - hat * jnp.mean(g * hat, axis=-1, keepdims=True)
    )
    return back, jnp.sum(up * hat, axis=0), jnp.sum(up, axis=0)


def gelu(v):
    return v * (0.5 + 0.5 * lax.erf(v * math.sqrt(0.5)))


def gelu_slope(v):
    return (0.5 + 0.5 * lax.erf(v * math.sqrt(0.5))) + v * jnp.exp(-0.5 * v * v) * (
        1.0 / math.sqrt(2.0 * math.pi)
    )


def low(v):
    return lax.reduce_precision(v, 8, 7)


PAIR = 2 * HEAD


def tdot(a, b, ca, cb):
    return lax.dot_general(a, b, (((ca,), (cb,)), ((), ())), preferred_element_type=F32)


def one_head(rows, half):
    lane = lax.broadcasted_iota(jnp.int32, rows.shape, 1)
    return jnp.where((lane < HEAD) == (half == 0), rows, jnp.zeros_like(rows))


def masked(s, count_ref):
    if count_ref is None:
        return s
    key = lax.broadcasted_iota(jnp.int32, s.shape, 0)
    query = lax.broadcasted_iota(jnp.int32, s.shape, 1)
    return jnp.where((key <= query) & (key < count_ref[0]), s, NEGATIVE)


def pack(rows, log_sums):
    cols, rest = [rows], log_sums.T
    for _ in range(3):
        term = low(rest)
        cols.append(term.astype(BF))
        rest = rest - term
    wide = sum(c.shape[1] for c in cols)
    return jnp.concatenate(cols + [jnp.zeros((rows.shape[0], -wide % 128), BF)], axis=1)


def unpack(packed):
    terms = [packed[..., D + i * HEADS : D + (i + 1) * HEADS].astype(F32) for i in range(3)]
    return packed[..., :D], terms[0] + terms[1] + terms[2]


def shift(v, axis, step):
    n = lax.axis_size(axis)
    return lax.ppermute(v, axis, [(i, i + step) for i in range(n) if 0 <= i + step < n])


def extended(x, width):
    before = shift(x[-width:], "seq", 1)
    after = shift(x[:width], "seq", -1)
    return jnp.concatenate([before, x, after], axis=0)


def exchange(v):
    n = lax.axis_size("seq")
    got = lax.all_to_all(v, "seq", split_axis=0, concat_axis=0, tiled=True)
    return got.reshape(n, v.shape[0] // n, v.shape[1])


def sinusoid(first_frame, frame_count):
    half = D // 2
    frequency = jnp.exp(jnp.arange(half).astype(F32) * (-math.log(10000.0) / (half - 1)))
    places = (first_frame + jnp.arange(frame_count)).astype(F32)
    angles = places[:, None] * frequency[None, :]
    return jnp.concatenate([jnp.sin(angles), jnp.cos(angles)], axis=1)


def to_whole(flat, shape, kind, dps, seqs):
    if kind == "v":
        return flat.reshape(-1)
    if kind == "1":
        t, i, o = shape
        return (
            flat.reshape(dps, seqs, t, i, o)
            .transpose(2, 1, 3, 0, 4)
            .reshape(t, seqs * i, dps * o)
        )
    if kind == "2":
        t, i, o = shape
        return (
            flat.reshape(dps, seqs, t, i, o)
            .transpose(2, 0, 3, 1, 4)
            .reshape(t, dps * i, seqs * o)
        )
    r, c = shape
    return flat.reshape(dps, seqs, r, c).transpose(0, 2, 1, 3).reshape(dps * r, seqs * c)


def to_owner(g, kind, dps, seqs):
    n = dps * seqs
    if kind == "v":
        return g.reshape(n, -1)
    if kind == "1":
        t, i, o = g.shape
        g = g.reshape(t, seqs, i // seqs, dps, o // dps).transpose(3, 1, 0, 2, 4)
    elif kind == "2":
        t, i, o = g.shape
        g = g.reshape(t, dps, i // dps, seqs, o // seqs).transpose(1, 3, 0, 2, 4)
    else:
        r, c = g.shape
        g = g.reshape(dps, r // dps, seqs, c // seqs).transpose(0, 2, 1, 3)
    return g.reshape(n, -1)


def gather_plain(shards):
    dps, seqs = lax.axis_size("dp"), lax.axis_size("seq")
    flat = jnp.concatenate([w.reshape(-1) for w in shards if w is not None])
    got = lax.all_gather(flat[None], BOTH, axis=0, tiled=True)
    out, at = [], 0
    for w, kind in zip(shards, KINDS):
        if w is None:
            out.append(None)
            continue
        out.append(to_whole(got[:, at : at + w.size], w.shape, kind, dps, seqs))
        at += w.size
    for i in BROAD:
        out[i] = out[i].reshape(D, seqs, -1).transpose(1, 0, 2)
    return out


def product(factors):
    left, right = factors
    if right.ndim == 3:
        return jnp.concatenate([outer(left, r) for r in right], axis=1)
    if isinstance(left, list) or left.ndim == 3:
        return jnp.stack([outer(l, right) for l in left])
    return outer(left, right)


def reduce_plain(grads, shards):
    dps, seqs = lax.axis_size("dp"), lax.axis_size("seq")
    grads = [product(g) if isinstance(g, tuple) else g for g in grads]
    for i in TALL:
        grads[i] = grads[i].reshape(-1, D)
    flat = jnp.concatenate(
        [to_owner(g.astype(BF), k, dps, seqs) for g, k in zip(grads, KINDS) if g is not None], axis=1
    )
    own = lax.psum_scatter(flat, BOTH, scatter_dimension=0, tiled=True).astype(F32)[0]
    out, at = [], 0
    for w, g in zip(shards, grads):
        if g is None:
            out.append(None)
            continue
        out.append(own[at : at + w.size].reshape(w.shape))
        at += w.size
    return out


MESH = pl.DeviceIdType.MESH
LANES = 384


def where_am_i():
    d, s = lax.axis_index("dp"), lax.axis_index("seq")
    return d // 2, d % 2, s // 2, s % 2


def partners(z, y, x, c):
    at = lambda z, y, x, c: (z * 2 + y, x * 2 + c)
    zs = [at((z + j) % 4, y, x, c) for j in (1, 2, 3)]
    return zs, at(z, 1 - y, x, c), at(z, y, 1 - x, c), at(z, y, x, 1 - c)


def greet(zs, yp, xp, cp):
    barrier = pltpu.get_barrier_semaphore()
    everyone = zs + [yp, xp, cp]
    for dev in everyone:
        pl.semaphore_signal(barrier, inc=1, device_id=dev, device_id_type=MESH)
    pl.semaphore_wait(barrier, len(everyone))


def remote(src, dst, send, recv, dev):
    return pltpu.make_async_remote_copy(
        src_ref=src, dst_ref=dst, send_sem=send, recv_sem=recv, device_id=dev, device_id_type=MESH
    )


def split_at(i, rows):
    return rows // 2 if rows % 32 == 0 else 16 + 16 * (i % 2)


def lanes(x):
    return pl.ds(pl.multiple_of(x * LANES, LANES), LANES)


def spot(ref, wide, zs, ys, xs, c, rs):
    full = lambda v: slice(None) if v is None else v
    if wide:
        return ref.at[full(xs), c, full(zs), full(ys), rs, :]
    return ref.at[full(zs), full(ys), c, rs, slice(None) if xs is None else lanes(xs)]


def add_into(dst, *srcs):
    lead = srcs[0].shape[:-2]
    total = math.prod(lead)

    def one(k, _):
        at = []
        for size in reversed(lead):
            at.append(lax.rem(k, size))
            k = lax.div(k, size)
        at = tuple(reversed(at))
        acc = srcs[0][at].astype(F32)
        for s in srcs[1:]:
            acc = acc + s[at].astype(F32)
        dst[at] = acc.astype(dst.dtype)
        return 0

    lax.fori_loop(0, total, one, 0)


RB = 48


def item_shapes(kind, h):
    if kind == "n":
        g = RB - h
        return [
            (4, 2, RB, D),
            (4, h, D),
            (4, 2, g, LANES),
            (4, h, LANES),
            (4, g, LANES),
            (4, RB, LANES),
            (3, RB, LANES),
        ]
    if kind == "t":
        return [
            (4, 4, 2, RB, D),
            (4, 2, RB, D),
            (4, 4, RB, LANES),
            (4, 2, RB, LANES),
            (4, 2, RB, LANES),
            (4, 2, 2, RB, LANES),
            (3, 2, 2, RB, LANES),
        ]
    r = RB if kind == "w" else MISC_ROWS // 2
    return [
        (2, 4, 2, 2, r, D),
        (2, 4, r, D),
        (4, 2, r, D),
        (4, r, D),
        (4, r, D),
        (4, 2, r, D),
        (3, 2, r, D),
    ]


def halves_of(k):
    return 16 + 16 * (k % 2)


def reduce_kernel(items, jobs, inputs, outputs, *refs):
    n = len(items)
    take = lambda count: (refs[:count], refs[count:])
    ins, refs = take(inputs)
    outs, refs = take(outputs)
    rc, refs = take(n)
    r1a, refs = take(n)
    r1b, refs = take(n)
    r2a, refs = take(n)
    r2b, refs = take(n)
    s3, refs = take(n)
    rz, refs = take(n)
    sbuf, refs = take(n)
    ring, wide_ring, given, xbuf, ybuf = refs[:5]
    loads, csend, crecv, xsend, xrecv, ysend, yrecv, zsend, zrecv, fsend, frecv = refs[5:]
    z, y, x, c = where_am_i()
    zs, yp, xp, cp = partners(z, y, x, c)
    greet(zs, yp, xp, cp)
    started = []

    def start(copy):
        copy.start()
        started.append(copy)
        return copy

    cores, ones, twos, threes, loaded = {}, {}, {}, {}, {}
    half = lambda i: halves_of(i)
    at = {(j[0], j[1]): t for t, j in enumerate(jobs)}

    def load(t):
        _, part, xi, yi, rows = jobs[t]
        xsrc, ysrc = ins[xi], ins[yi]
        if len(xsrc.shape) == 3:
            xsrc = xsrc.at[part]
        if len(ysrc.shape) == 3:
            ysrc = ysrc.at[2 * (part // 2) + (c if part % 2 else 1 - c)]
        pair = []
        for k, (src, buf) in enumerate(((xsrc, xbuf), (ysrc, ybuf))):
            copy = pltpu.make_async_copy(src, buf.at[t % 2, 0:rows], loads.at[t % 2, k])
            copy.start()
            pair.append(copy)
        loaded[t] = pair

    def room(t):
        return wide_ring if items[jobs[t][0]][1] == F32 else ring.at[t % RING]

    def compute(t):
        i, part, _, _, rows = jobs[t]
        if t >= RING and t - RING in cores and items[jobs[t - RING][0]][1] == BF:
            cores[t - RING].wait_send()
        for copy in loaded[t]:
            copy.wait()
        room_t = room(t)
        left = xbuf[t % 2, 0:rows, :]

        def column(k, _):
            cols = pl.ds(pl.multiple_of(k * 256, 256), 256)
            product = tdot(left, ybuf[t % 2, 0:rows, cols], 0, 0)
            room_t[:, :, :, :, cols] = product.reshape(4, 2, 2, RB, 256).astype(room_t.dtype)
            return 0

        lax.fori_loop(0, D // 256, column, 0)
        if t + 2 < len(jobs):
            load(t + 2)
        kind = items[i][0]
        if kind == "n":
            cores[t] = remote(room_t.at[:, :, 1 - c], rc[i], csend.at[t], crecv.at[t], cp)
        elif kind == "t":
            cores[t] = remote(room_t.at[:, :, 1 - c], rc[i].at[part], csend.at[t], crecv.at[t], cp)
        elif part % 2 == 0:
            cores[t] = remote(room_t, rc[i].at[part // 2], csend.at[t], crecv.at[t], cp)
        if t in cores:
            cores[t].start()

    def add_own(t):
        i, part, _, _, _ = jobs[t]
        kind, mine = items[i][0], room(t)
        if kind == "w":
            if part % 2 == 0:
                return False
            cores[at[i, part - 1]].wait_recv()
            add_into(rc[i].at[part // 2], mine, rc[i].at[part // 2])
            return part == 3
        cores[t].wait_recv()
        dst = rc[i] if kind == "n" else rc[i].at[part]
        add_into(dst, mine.at[:, :, c], dst)
        return kind == "n" or part == 3

    def views(i):
        kind, h = items[i][0], half(i)
        r, a, b = rc[i], r1a[i], r1b[i]
        here, there = lanes(x), lanes(1 - x)
        if kind == "n":
            one = (r.at[:, 1 - y, 0:h, :], r.at[:, :, h:RB, there], r.at[:, y, 0:h, :], r.at[:, :, h:RB, here])
            two = (a.at[:, :, there], b.at[:, 1 - y], a.at[:, :, here], b.at[:, y])
            parts = (s3[i].at[:, 0:h, :], s3[i].at[:, h:RB, :])
        elif kind == "t":
            up, down = pl.ds(2 * y, 2), pl.ds(2 * (1 - y), 2)
            one = (r.at[:, down, 0], r.at[:, :, 1, :, there], r.at[:, up, 0], r.at[:, :, 1, :, here])
            two = (a.at[:, :, :, there], b.at[:, down], a.at[:, :, :, here], b.at[:, up])
            parts = (s3[i].at[:, 0], s3[i].at[:, 1])
        else:
            one = (r.at[:, :, 1 - y, 0], r.at[1 - x, :, :, 1], r.at[:, :, y, 0], r.at[x, :, :, 1])
            two = (a.at[1 - x], b.at[:, 1 - y], a.at[x], b.at[:, y])
            parts = (s3[i].at[:, 0], s3[i].at[:, 1])
        return one, two, parts

    def send_1(i):
        (over_y, over_x, _, _), _, _ = views(i)
        ones[i] = [
            start(remote(over_y, r1a[i], ysend.at[i, 0], yrecv.at[i, 0], yp)),
            start(remote(over_x, r1b[i], xsend.at[i, 0], xrecv.at[i, 0], xp)),
        ]

    def send_2(i):
        (_, _, stay_a, stay_b), (over_x, over_y, _, _), _ = views(i)
        ones[i][0].wait_recv()
        add_into(r1a[i], stay_a, r1a[i])
        first = start(remote(over_x, r2a[i], xsend.at[i, 1], xrecv.at[i, 1], xp))
        ones[i][1].wait_recv()
        add_into(r1b[i], stay_b, r1b[i])
        twos[i] = [first, start(remote(over_y, r2b[i], ysend.at[i, 1], yrecv.at[i, 1], yp))]

    def send_z(i):
        _, (_, _, stay_a, stay_b), (part_a, part_b) = views(i)
        twos[i][0].wait_recv()
        add_into(part_a, stay_a, r2a[i])
        twos[i][1].wait_recv()
        add_into(part_b, stay_b, r2b[i])
        threes[i] = [
            start(remote(s3[i].at[(z + j + 1) % 4], rz[i].at[j], zsend.at[i, j], zrecv.at[i, j], zs[j]))
            for j in range(3)
        ]

    finals = []

    def finish(i):
        kind, _, out, tap = items[i]
        for copy in threes[i]:
            copy.wait_recv()
        acc = s3[i][z].astype(F32)
        for j in range(3):
            acc = acc + rz[i][j].astype(F32)
        dst = outs[out] if tap is None else outs[out].at[tap]
        if kind in "wm":
            dst[...] = acc
            return
        mine = acc[..., : LANES // 2]
        theirs = acc[..., LANES // 2 :]
        keep = jnp.where(c == 0, mine, theirs)
        other = jnp.where(c == 0, theirs, mine)
        if kind == "n":
            sbuf[i][...] = other
            dst[c] = keep
            finals.append(start(remote(sbuf[i], dst.at[c], fsend.at[i], frecv.at[i], cp)))
            return
        for a in (0, 1):
            for b in (0, 1):
                dst[b, a, c] = keep[a, b]
                sbuf[i][b, a] = other[a, b]
        finals.append(start(remote(sbuf[i], dst.at[:, :, c], fsend.at[i], frecv.at[i], cp)))

    g = [i for i in range(n) if items[i][0] == "m"][0]
    last = len(jobs)
    theirs = start(remote(ins[-1].at[:, 1 - c], rc[g], csend.at[last], crecv.at[last], cp))
    mine = pltpu.make_async_copy(ins[-1].at[:, c], given, loads.at[0, 2])
    mine.start()
    load(0)
    load(1)
    queue = [[], [], []]
    steps = (send_2, send_z, finish)

    def advance(keep):
        for k in (2, 1, 0):
            while len(queue[k]) > keep:
                i = queue[k].pop(0)
                steps[k](i)
                if k < 2:
                    queue[k + 1].append(i)

    mine.wait()
    for t in range(last + 1):
        if t < last:
            compute(t)
        if t == 1:
            theirs.wait_recv()
            add_into(rc[g], given, rc[g])
            send_1(g)
            queue[0].append(g)
        if t >= 1 and add_own(t - 1):
            i = jobs[t - 1][0]
            send_1(i)
            queue[0].append(i)
        advance(LAG)
    for keep in range(LAG - 1, -1, -1):
        advance(keep)
    while queue[0] or queue[1] or queue[2]:
        advance(0)
    for copy in finals:
        copy.wait_recv()
    for copy in started:
        copy.wait_send()
    for t in cores:
        if t + RING >= last or items[jobs[t][0]][1] == F32:
            cores[t].wait_send()


RING = 3
LAG = 1


def reduce_fast(items, jobs, ins, out_shapes):
    n, m = len(items), len(jobs)
    sem = pltpu.SemaphoreType.DMA
    groups = [[] for _ in range(8)]
    for i, (kind, dtype, _, _) in enumerate(items):
        for group, shape in zip(groups, item_shapes(kind, halves_of(i))):
            group.append(pltpu.VMEM(shape, dtype))
        last = {"n": (RB, LANES // 2), "t": (2, 2, RB, LANES // 2)}.get(kind, (8, 128))
        groups[7].append(pltpu.VMEM(last, F32))
    scratch = [s for group in groups for s in group]
    scratch += [
        pltpu.VMEM((RING, 4, 2, 2, RB, D), BF),
        pltpu.VMEM((4, 2, 2, RB, D), F32),
        pltpu.VMEM((2, 4, 2, 2, MISC_ROWS // 2, D), BF),
    ]
    most = max(j[4] for j in jobs)
    scratch += [pltpu.VMEM((2, most, D), BF)] * 2
    scratch += [sem((2, 3)), sem((m + 1,)), sem((m + 1,))]
    scratch += [sem((n, 2))] * 4 + [sem((n, 3))] * 2 + [sem((n,))] * 2
    return pl.pallas_call(
        functools.partial(reduce_kernel, items, jobs, len(ins), len(out_shapes)),
        out_shape=[jax.ShapeDtypeStruct(s, F32) for s in out_shapes],
        in_specs=[pl.BlockSpec(memory_space=pl.ANY)] * len(ins),
        out_specs=[pl.BlockSpec(memory_space=pltpu.VMEM)] * len(out_shapes),
        scratch_shapes=scratch,
        compiler_params=pltpu.CompilerParams(
            collective_id=2, has_side_effects=True, vmem_limit_bytes=62 << 20
        ),
    )(*ins)


def lanes_of(pair):
    return pl.ds(pl.multiple_of(pair * PAIR, PAIR), PAIR)


def clip_partners():
    d, s = lax.axis_index("dp"), lax.axis_index("seq")
    x, c = s // 2, s % 2
    return (d, (1 - x) * 2 + c), (d, x * 2 + 1 - c)


def greet_pair(xp, cp):
    barrier = pltpu.get_barrier_semaphore()
    for dev in (xp, cp):
        pl.semaphore_signal(barrier, inc=1, device_id=dev, device_id_type=MESH)
    pl.semaphore_wait(barrier, 2)


def forward_head(q_one, k_slab, v_slab, half, count):
    s = masked(tdot(k_slab, q_one, 1, 1), count)
    top = jnp.max(s, axis=0, keepdims=True)
    e = jnp.exp(s - top)
    total = jnp.sum(e, axis=0, keepdims=True)
    mixed = tdot(v_slab, e.astype(BF), 0, 0)[half * HEAD : (half + 1) * HEAD]
    return mixed / total, top + jnp.log(total)


def forward_pair(pair, q, k, v, o, lse, count):
    at = lanes_of(pair)
    q_slab, k_slab, v_slab = q[:, at], k[:, at], v[:, at]
    both = []
    for half in (0, 1):
        mixed, log_sum = forward_head(one_head(q_slab, half), k_slab, v_slab, half, count)
        both.append(mixed)
        lse[pl.ds(2 * pair + half, 1), :] = log_sum
    o[:, at] = jnp.concatenate(both, axis=0).T.astype(o.dtype)


def backward_pair(pair, q, k, v, up, lse, dq, dk, dv, count, known):
    at = lanes_of(pair)
    q_slab, k_slab, v_slab, u_slab = q[:, at], k[:, at], v[:, at], up[:, at]
    both, dk_sum, dv_sum = [], 0.0, 0.0
    for half in (0, 1):
        row = pl.ds(2 * pair + half, 1)
        q_one, u_one = one_head(q_slab, half), one_head(u_slab, half)
        p = jnp.exp(masked(tdot(k_slab, q_one, 1, 1), count) - lse[row, :])
        dp = tdot(v_slab, u_one, 1, 1)
        if known is None:
            mass = jnp.sum(p, axis=0, keepdims=True)
            inner = jnp.sum(p * dp, axis=0, keepdims=True) / mass
        else:
            inner = known[row, :]
        ds = (p * (dp - inner)).astype(BF)
        dv_sum = dv_sum + tdot(p.astype(BF), u_one, 1, 0)
        dk_sum = dk_sum + tdot(ds, q_one, 1, 0)
        both.append(tdot(k_slab, ds, 0, 0)[half * HEAD : (half + 1) * HEAD])
    dq[:, at] = jnp.concatenate(both, axis=0).T.astype(dq.dtype)
    dk[:, at] = dk_sum.astype(dk.dtype)
    dv[:, at] = dv_sum.astype(dv.dtype)


def attend_kernel(causal, *refs):
    count = refs[0] if causal else None
    q, k, v, o, lse = refs[1:] if causal else refs

    def step(pair, _):
        forward_pair(pair, q, k, v, o, lse, count)
        return 0

    lax.fori_loop(0, HEADS // 2, step, 0)


def sums_kernel(q, k, v, up, lse, mass, inner):
    def step(pair, _):
        at = lanes_of(pair)
        q_slab, k_slab, v_slab, u_slab = q[:, at], k[:, at], v[:, at], up[:, at]
        for half in (0, 1):
            row = pl.ds(2 * pair + half, 1)
            p = jnp.exp(tdot(k_slab, one_head(q_slab, half), 1, 1) - lse[row, :])
            dp = tdot(v_slab, one_head(u_slab, half), 1, 1)
            mass[row, :] = jnp.sum(p, axis=0, keepdims=True)
            inner[row, :] = jnp.sum(p * dp, axis=0, keepdims=True)
        return 0

    lax.fori_loop(0, HEADS // 2, step, 0)


def back_kernel(causal, given, *refs):
    count, known = None, None
    if causal:
        count, refs = refs[0], refs[1:]
    q, k, v, up, lse = refs[:5]
    refs = refs[5:]
    if given:
        known, refs = refs[0], refs[1:]
    dq, dk, dv = refs

    def step(pair, _):
        backward_pair(pair, q, k, v, up, lse, dq, dk, dv, count, known)
        return 0

    lax.fori_loop(0, HEADS // 2, step, 0)


def clip_attend_kernel(q, k, v, o, lse, k_all, v_all, xsend, xrecv, csend, crecv):
    xp, cp = clip_partners()
    r = q.shape[0]
    greet_pair(xp, cp)
    pairs = HEADS // 2

    def across(pair):
        at = lanes_of(pair)
        return [
            remote(src.at[:, at], dst.at[r : 2 * r, at], xsend.at[j, pair], xrecv.at[j, pair], xp)
            for j, (src, dst) in enumerate(((k, k_all), (v, v_all)))
        ]

    def beside(pair):
        at = lanes_of(pair)
        return [
            remote(a.at[0 : 2 * r, at], a.at[2 * r : 4 * r, at], csend.at[j, pair], crecv.at[j, pair], cp)
            for j, a in enumerate((k_all, v_all))
        ]

    for pair in range(pairs):
        for copy in across(pair):
            copy.start()
    k_all[0:r, :] = k[...]
    v_all[0:r, :] = v[...]

    def pass_on(pair):
        for copy in across(pair):
            copy.wait_recv()
        for copy in beside(pair):
            copy.start()

    pass_on(0)

    def step(pair, _):
        @pl.when(pair + 1 < pairs)
        def _():
            pass_on(pair + 1)

        for copy in beside(pair):
            copy.wait_recv()
        forward_pair(pair, q, k_all, v_all, o, lse, None)
        return 0

    lax.fori_loop(0, pairs, step, 0)
    for pair in range(pairs):
        for copy in across(pair) + beside(pair):
            copy.wait_send()


def clip_back_kernel(q, k, v, up, lse, dq, dk, dv, *refs):
    k_sum, v_sum, k_near, v_near, k_far, v_far, xsend, xrecv, csend, crecv = refs
    xp, cp = clip_partners()
    r = q.shape[0]
    greet_pair(xp, cp)
    pairs = HEADS // 2
    sums, nears, fars, outs = (k_sum, v_sum), (k_near, v_near), (k_far, v_far), (dk, dv)

    def beside(pair):
        at = lanes_of(pair)
        return [
            remote(sums[j].at[2 * r : 4 * r, at], nears[j].at[:, at], csend.at[j, pair], crecv.at[j, pair], cp)
            for j in (0, 1)
        ]

    def across(pair):
        at = lanes_of(pair)
        return [
            remote(sums[j].at[r : 2 * r, at], fars[j].at[:, at], xsend.at[j, pair], xrecv.at[j, pair], xp)
            for j in (0, 1)
        ]

    def step(t, _):
        @pl.when(t < pairs)
        def _():
            backward_pair(t, q, k, v, up, lse, dq, k_sum, v_sum, None, None)
            for copy in beside(t):
                copy.start()

        @pl.when((t >= 1) & (t <= pairs))
        def _():
            pair = t - 1
            at = lanes_of(pair)
            for copy in beside(pair):
                copy.wait_recv()
            for j in (0, 1):
                near = sums[j][0 : 2 * r, at].astype(F32) + nears[j][:, at].astype(F32)
                sums[j][0 : 2 * r, at] = near.astype(BF)
            for copy in across(pair):
                copy.start()

        @pl.when(t >= 2)
        def _():
            pair = t - 2
            at = lanes_of(pair)
            for copy in across(pair):
                copy.wait_recv()
            for j in (0, 1):
                total = sums[j][0:r, at].astype(F32) + fars[j][:, at].astype(F32)
                outs[j][:, at] = total.astype(BF)

        return 0

    lax.fori_loop(0, pairs + 2, step, 0)
    for pair in range(pairs):
        for copy in across(pair) + beside(pair):
            copy.wait_send()


def local_call(kernel, out_shape, args, cost, count=None, scratch=(), barrier=None):
    vmem = pl.BlockSpec(memory_space=pltpu.VMEM)
    specs = [vmem] * len(args)
    if count is not None:
        specs, args = [pl.BlockSpec(memory_space=pltpu.SMEM)] + specs, [count] + args
    params = dict(vmem_limit_bytes=56 << 20)
    if barrier is not None:
        params.update(collective_id=barrier, has_side_effects=True)
    return pl.pallas_call(
        kernel,
        out_shape=[jax.ShapeDtypeStruct(s, t) for s, t in out_shape],
        in_specs=specs,
        out_specs=[vmem] * len(out_shape),
        scratch_shapes=list(scratch),
        cost_estimate=pl.CostEstimate(flops=cost, bytes_accessed=8 << 20, transcendentals=0),
        compiler_params=pltpu.CompilerParams(**params),
    )(*args)


def rows_cost(q, k):
    return 8 * q.shape[0] * k.shape[0] * D


def attend(q, k, v, count=None):
    shapes = [(q.shape, BF), ((HEADS, q.shape[0]), F32)]
    kernel = functools.partial(attend_kernel, count is not None)
    return local_call(kernel, shapes, [q, k, v], rows_cost(q, k), count)


def attend_sums(q, k, v, up, lse):
    return local_call(sums_kernel, [(lse.shape, F32)] * 2, [q, k, v, up, lse], rows_cost(q, k))


def attend_back(q, k, v, up, lse, count=None, inner=None, out=BF):
    shapes = [(q.shape, out), (k.shape, BF), (k.shape, BF)]
    kernel = functools.partial(back_kernel, count is not None, inner is not None)
    args = [q, k, v, up, lse] + ([] if inner is None else [inner])
    return local_call(kernel, shapes, args, 3 * rows_cost(q, k), count)


def clip_attend(q, k, v):
    r = k.shape[0]
    shapes = [(q.shape, BF), ((HEADS, r), F32), ((4 * r, D), BF), ((4 * r, D), BF)]
    sems = [pltpu.SemaphoreType.DMA((2, HEADS // 2))] * 4
    return local_call(clip_attend_kernel, shapes, [q, k, v], 4 * rows_cost(q, k), None, sems, 3)


def clip_attend_back(q, k_all, v_all, up, lse):
    r = q.shape[0]
    scratch = [pltpu.VMEM((4 * r, D), BF)] * 2 + [pltpu.VMEM((2 * r, D), BF)] * 2
    scratch += [pltpu.VMEM((r, D), BF)] * 2 + [pltpu.SemaphoreType.DMA((2, HEADS // 2))] * 4
    args = [q, k_all, v_all, up, lse]
    return local_call(clip_back_kernel, [(q.shape, BF)] * 3, args, 3 * rows_cost(q, k_all), None, scratch, 4)


def mlp_kernel(stream, gain, bias, expand, contract, normed, pre, hidden, out):
    @pl.when(pl.program_id(0) == 0)
    def _():
        normed[...] = norm(stream[...], gain[...], bias[...])
        out[...] = stream[...]

    before = tdot(normed[...], expand[0], 1, 0)
    pre[0] = before
    after = gelu(before).astype(BF)
    hidden[0] = after
    out[...] += tdot(after, contract[0], 1, 0)


def mlp_back_kernel(up, stream, gain, pre, expand, contract, out, d_low, d_pre, d_gain, d_bias, total):
    s = pl.program_id(0)

    @pl.when(s == 0)
    def _():
        d_low[...] = up[...].astype(BF)
        total[...] = jnp.zeros_like(total)

    d_hidden = low(tdot(d_low[...], contract[0], 1, 1))
    grad = (gelu_slope(pre[0]) * d_hidden).astype(BF)
    d_pre[0] = grad
    total[...] += tdot(grad, expand[0], 1, 1)

    @pl.when(s == pl.num_programs(0) - 1)
    def _():
        hat, inv = norm_parts(stream[...])
        g = total[...] * gain[...]
        mean = lambda v: jnp.mean(v, axis=-1, keepdims=True)
        out[...] = up[...] + inv * (g - mean(g) - hat * mean(g * hat))
        d_gain[...] = jnp.sum(total[...] * hat, axis=0, keepdims=True)
        d_bias[...] = jnp.sum(total[...], axis=0, keepdims=True)


def blocks(kernel, grid, ins, outs, args, cost, scratch=()):
    def spec(shape, cut):
        if cut:
            return pl.BlockSpec((1,) + shape[1:], lambda s: (s,) + (0,) * (len(shape) - 1))
        return pl.BlockSpec(shape, lambda s: (0,) * len(shape))

    return pl.pallas_call(
        kernel,
        grid=(grid,),
        out_shape=[jax.ShapeDtypeStruct(s, t) for s, t, _ in outs],
        in_specs=[spec(a.shape, cut) for a, cut in zip(args, ins)],
        out_specs=[spec(s, cut) for s, _, cut in outs],
        scratch_shapes=list(scratch),
        cost_estimate=pl.CostEstimate(flops=cost, bytes_accessed=16 << 20, transcendentals=0),
        compiler_params=pltpu.CompilerParams(vmem_limit_bytes=48 << 20),
    )(*args)


def mlp(stream, gain, bias, expand, contract):
    n, (r, _) = expand.shape[0], stream.shape
    outs = [((r, D), BF, False), ((n, r, D), F32, True), ((n, r, D), BF, True), ((r, D), F32, False)]
    args = [stream, gain[None], bias[None], expand, contract.reshape(n, D, D)]
    return blocks(mlp_kernel, n, [False] * 3 + [True] * 2, outs, args, 4 * n * r * D * D)


def mlp_backward(up, stream, gain, pre, expand, contract):
    n, (r, _) = expand.shape[0], stream.shape
    outs = [((r, D), F32, False), ((r, D), BF, False), ((n, r, D), BF, True)]
    outs += [((1, D), F32, False)] * 2
    args = [up, stream, gain[None], pre, expand, contract.reshape(n, D, D)]
    scratch = [pltpu.VMEM((r, D), F32)]
    return blocks(mlp_back_kernel, n, [False] * 3 + [True] * 3, outs, args, 4 * n * r * D * D, scratch)


SQUARE = (4, 5, 6, 7, 18, 19, 20, 21, 24, 25, 26, 27)
TALL = (11, 31)
BROAD = (10, 30)
VECTORS = tuple(i for i in range(32) if KINDS[i] == "v")
MISC_ROWS = 32


ROW_PAD = 400
CHUNK = 80
SMALL_ROWS = 96


def gather_split(i, rows):
    return rows // 2 if rows % 32 == 0 else 16 + 16 * (i % 2)


def stem_kernel(plan, inputs, outputs, *refs):
    n = len(plan)
    ins, refs = refs[:inputs], refs[inputs:]
    patches, angles, refs = refs[:3], refs[3], refs[4:]
    outs, refs = refs[:outputs], refs[outputs:]
    even_pre, odd_pre, even, odd, even_next, second, stream, normed, q, k_all, v_all, o, lse, vec = refs[:14]
    got, stage, refs = refs[14 : 14 + n], refs[14 + n : 14 + 2 * n], refs[14 + 2 * n :]
    small, weights, k_own, v_own = refs[:4]
    lsem, zsend, zrecv, xsend, xrecv, ysend, yrecv, csend, crecv, psend, precv = refs[4:15]
    wsem, kxs, kxr, kcs, kcr = refs[15:]
    z, y, x, c = where_am_i()
    zs, yp, xp, cp = partners(z, y, x, c)
    greet(zs, yp, xp, cp)
    dst, src, swaps = [], [], []
    for i, (k, rows, out, tap, kind) in enumerate(plan):
        dst.append(outs[out] if tap is None else outs[out].at[tap])
        src.append(ins[k] if tap is None else ins[k].at[tap])
        swaps.append(None)
        if kind == "n":
            theirs = src[i].at[pl.ds(pl.multiple_of((1 - c) * rows, 16), rows), :]
            swaps[i] = remote(theirs, got[i], psend.at[i], precv.at[i], cp)
            swaps[i].start()

    def item(i):
        rows, wide = plan[i][1], plan[i][4] == "w"
        h = gather_split(i, rows)
        return rows, wide, slice(0, h), slice(h, rows)

    stages = {}

    def start(i, key, copies):
        for cpy in copies:
            cpy.start()
        stages[i, key] = copies

    def send_z(i):
        rows, wide, _, _ = item(i)
        block = src[i]
        if not wide:
            mine = src[i][pl.ds(pl.multiple_of(c * rows, 16), rows), :]
            swaps[i].wait_recv()
            theirs = got[i][...]
            stage[i][...] = jnp.concatenate(
                [jnp.where(c == 0, mine, theirs), jnp.where(c == 0, theirs, mine)], axis=1
            )
            block = stage[i]
        here = spot(dst[i], wide, z, y, x, c, slice(None))
        start(i, 0, [remote(block, here, zsend.at[i, j], zrecv.at[i, j], zs[j]) for j in range(3)])
        start(i, 4, [pltpu.make_async_copy(block, here, lsem.at[i])])

    def send_1(i):
        rows, wide, a, b = item(i)
        for cpy in stages[i, 0]:
            cpy.wait_recv()
        stages[i, 4][0].wait()
        ax = spot(dst[i], wide, None, y, x, c, a)
        by = spot(dst[i], wide, None, y, x, c, b)
        start(
            i,
            1,
            [
                remote(ax, ax, xsend.at[i, 0], xrecv.at[i, 0], xp),
                remote(by, by, ysend.at[i, 0], yrecv.at[i, 0], yp),
            ],
        )

    def send_2(i):
        rows, wide, a, b = item(i)
        for cpy in stages[i, 1]:
            cpy.wait_recv()
        ay = spot(dst[i], wide, None, y, None, c, a)
        bx = spot(dst[i], wide, None, None, x, c, b)
        start(
            i,
            2,
            [
                remote(ay, ay, ysend.at[i, 1], yrecv.at[i, 1], yp),
                remote(bx, bx, xsend.at[i, 1], xrecv.at[i, 1], xp),
            ],
        )

    def send_core(i):
        rows, wide, a, b = item(i)
        for cpy in stages[i, 2]:
            cpy.wait_recv()
        half = spot(dst[i], wide, None, None, None, c, slice(None))
        start(i, 3, [remote(half, half, csend.at[i], crecv.at[i], cp)])

    arrived = set()

    def arrive(i):
        if i not in arrived:
            stages[i, 3][0].wait_recv()
            arrived.add(i)

    r = q.shape[0]
    pairs = HEADS // 2

    def fetch(items, slots):
        copies = []
        for i, slot in zip(items, slots):
            arrive(i)
            copies.append(pltpu.make_async_copy(dst[i], weights.at[slot], wsem.at[slot]))
            copies[-1].start()
        for cpy in copies:
            cpy.wait()

    def weight(slot):
        return weights[slot].reshape(D, D)

    def open_small():
        arrive(0)
        copy = pltpu.make_async_copy(dst[0], small, wsem.at[3])
        copy.start()
        copy.wait()
        cells = []
        for zy in range(8):
            for s in range(4):
                cells.append(small[s // 2, s % 2, zy // 2, zy % 2, 64:80, 0:24].astype(F32))
        vec[...] = jnp.concatenate(cells, axis=1)

    def convolve(patch, pre, act, edge):
        def one(t, _):
            rows = pl.ds(pl.multiple_of(t * CHUNK, 16), CHUNK)
            left = patch[rows, :]
            cells = []
            for zy in range(8):
                taps = [small[s // 2, s % 2, zy // 2, zy % 2, 0:64, :] for s in range(4)]
                cells.append(tdot(left, jnp.concatenate(taps, axis=0), 1, 0)[:, 0:96])
            before = jnp.concatenate(cells, axis=1)
            if pre is not None:
                pre[rows, :] = before
            after = gelu(before)
            if edge is not None:
                row, outside = edge
                at = t * CHUNK + lax.broadcasted_iota(jnp.int32, after.shape, 0)
                after = jnp.where((at == row) & outside, 0.0, after)
            act[rows, :] = after.astype(BF)
            return 0

        lax.fori_loop(0, ROW_PAD // CHUNK, one, 0)

    me = 2 * x + c
    part = 128

    def convolve_second(t):
        rows = slice(t * part, (t + 1) * part)
        total = tdot(even[rows, :], weight(0), 1, 0)
        total = total + tdot(odd[rows, :], weight(1), 1, 0)
        total = total + tdot(even_next[rows, :], weight(2), 1, 0)
        second[rows, :] = total
        out = gelu(total) + angles[rows, :]
        stream[rows, :] = out
        normed[rows, :] = norm(out, vec[0:1, :], vec[1:2, :])

    def project():
        for t in range(r // part):
            rows = slice(t * part, (t + 1) * part)
            left = normed[rows, :]
            q[rows, :] = (tdot(left, weight(0), 1, 0) * SCALE).astype(BF)
            k_own[rows, :] = tdot(left, weight(1), 1, 0).astype(BF)
            v_own[rows, :] = tdot(left, weight(2), 1, 0).astype(BF)
        for pair in range(pairs):
            for cpy in across(pair):
                cpy.start()
        k_all[0:r, :] = k_own[...]
        v_all[0:r, :] = v_own[...]

    def across(pair):
        at = lanes_of(pair)
        return [
            remote(a.at[:, at], b.at[r : 2 * r, at], kxs.at[j, pair], kxr.at[j, pair], xp)
            for j, (a, b) in enumerate(((k_own, k_all), (v_own, v_all)))
        ]

    def beside(pair):
        at = lanes_of(pair)
        return [
            remote(a.at[0 : 2 * r, at], a.at[2 * r : 4 * r, at], kcs.at[j, pair], kcr.at[j, pair], cp)
            for j, a in enumerate((k_all, v_all))
        ]

    def pass_on(pair):
        for cpy in across(pair):
            cpy.wait_recv()
        for cpy in beside(pair):
            cpy.start()

    def attend_pair(pair):
        if pair + 1 < pairs:
            pass_on(pair + 1)
        for cpy in beside(pair):
            cpy.wait_recv()
        forward_pair(pair, q, k_all, v_all, o, lse, None)

    pieces = [
        open_small,
        lambda: convolve(patches[0], even_pre, even, (0, me == 0)),
        lambda: convolve(patches[1], odd_pre, odd, (r, me == 3)),
        lambda: convolve(patches[2], None, even_next, None),
        lambda: fetch((1, 2, 3), (0, 1, 2)),
    ]
    pieces += [functools.partial(convolve_second, t) for t in range(r // part)]
    pieces += [lambda: (fetch((4, 5, 6), (0, 1, 2)), project()), lambda: pass_on(0)]
    pieces += [functools.partial(attend_pair, pair) for pair in range(pairs)]

    for t in range(n + AHEAD[2]):
        if t == 0:
            for i in range(min(n, AHEAD[3])):
                send_z(i)
        if t + AHEAD[3] < n:
            send_z(t + AHEAD[3])
        if 0 <= t - AHEAD[0] < n:
            send_1(t - AHEAD[0])
        if 0 <= t - AHEAD[1] < n:
            send_2(t - AHEAD[1])
        if 0 <= t - AHEAD[2] < n:
            send_core(t - AHEAD[2])
        if t >= PIECES_FROM and pieces:
            pieces.pop(0)()
    while pieces:
        pieces.pop(0)()
    for i in range(n):
        if swaps[i] is not None:
            swaps[i].wait_send()
        arrive(i)
        for key in range(4):
            for cpy in stages[i, key]:
                cpy.wait_send()
    for pair in range(pairs):
        for cpy in across(pair) + beside(pair):
            cpy.wait_send()


AHEAD = (0, 1, 3, 6)
PIECES_FROM = 5


def gather_and_stem(plan, ins, out_shapes, patches, angles):
    n, r = len(plan), angles.shape[0]
    sem = pltpu.SemaphoreType.DMA
    hbm, vmem = pl.BlockSpec(memory_space=pl.ANY), pl.BlockSpec(memory_space=pltpu.VMEM)
    got, stage = [], []
    for _, rows, _, _, kind in plan:
        got.append(pltpu.VMEM((rows, LANES // 2) if kind == "n" else (16, 128), BF))
        stage.append(pltpu.VMEM((rows, LANES) if kind == "n" else (16, 128), BF))
    sems = [sem((n,)), sem((n, 3)), sem((n, 3))] + [sem((n, 2))] * 4 + [sem((n,))] * 4
    made = [((ROW_PAD, D), F32)] * 2 + [((ROW_PAD, D), BF)] * 3 + [((r, D), F32)] * 2
    made += [((r, D), BF)] * 2 + [((4 * r, D), BF)] * 2 + [((r, D), BF), ((HEADS, r), F32), ((16, D), F32)]
    held = [pltpu.VMEM((2, 2, 4, 2, SMALL_ROWS, 128), BF), pltpu.VMEM((3, 4, 2, 2, 48, D), BF)]
    held += [pltpu.VMEM((r, D), BF)] * 2
    return pl.pallas_call(
        functools.partial(stem_kernel, plan, len(ins), len(out_shapes)),
        out_shape=[jax.ShapeDtypeStruct(s, BF) for s in out_shapes]
        + [jax.ShapeDtypeStruct(s, t) for s, t in made],
        in_specs=[vmem] * (len(ins) + 4),
        out_specs=[hbm] * len(out_shapes) + [vmem] * len(made),
        scratch_shapes=got + stage + held + sems + [sem((4,))] + [sem((2, HEADS // 2))] * 4,
        compiler_params=pltpu.CompilerParams(
            collective_id=1, has_side_effects=True, vmem_limit_bytes=60 << 20
        ),
    )(*ins, *patches, angles)


def share_kernel(own, out, send, zrecv, xrecv, yrecv, crecv):
    z, y, x, c = where_am_i()
    zs, yp, xp, cp = partners(z, y, x, c)
    greet(zs, yp, xp, cp)
    here = out.at[x, c, z, y]
    here[...] = own[...]
    started = []

    def go(copies):
        for cpy in copies:
            cpy.start()
        for cpy in copies:
            cpy.wait_recv()
        started.extend(copies)

    go([remote(own, here, send.at[j], zrecv.at[j], zs[j]) for j in range(3)])
    line = out.at[x, c, :, y]
    go([remote(line, line, send.at[3], xrecv.at[0], xp)])
    plane = out.at[:, c, :, y]
    go([remote(plane, plane, send.at[4], yrecv.at[0], yp)])
    half = out.at[:, c]
    go([remote(half, half, send.at[5], crecv.at[0], cp)])
    for cpy in started:
        cpy.wait_send()


def share_ids(ids):
    own = jnp.pad(ids[None], ((0, 7), (0, 128 - ids.size)))
    sem, vmem = pltpu.SemaphoreType.DMA, pl.BlockSpec(memory_space=pltpu.VMEM)
    out = pl.pallas_call(
        share_kernel,
        out_shape=jax.ShapeDtypeStruct((2, 2, 4, 2, 8, 128), jnp.int32),
        in_specs=[vmem],
        out_specs=vmem,
        scratch_shapes=[sem((6,)), sem((3,)), sem((1,)), sem((1,)), sem((1,))],
        compiler_params=pltpu.CompilerParams(collective_id=5, has_side_effects=True),
    )(own)
    return out[..., 0, : ids.size].transpose(2, 3, 0, 1, 4).reshape(-1)


def small_block(shards):
    w = shards[0]
    t, i, o = w.shape
    top = jnp.pad(w.reshape(t * i, o), ((0, 64 - t * i), (0, 128 - o)))
    rows = jnp.stack([shards[k] for k in VECTORS])
    rows = jnp.pad(rows, ((0, SMALL_ROWS - 64 - rows.shape[0]), (0, 128 - rows.shape[1])))
    return jnp.concatenate([top, rows])


def patch_rows(patch, mels):
    p = patch.reshape(patch.shape[0], 3, 4, mels // 4).transpose(0, 2, 1, 3).reshape(patch.shape[0], 4, -1)
    p = jnp.pad(p, ((0, ROW_PAD - p.shape[0]), (0, 0), (0, 64 - p.shape[2])))
    return p.reshape(ROW_PAD, 256)


def gather_weights(shards, patches, angles):
    plan, ins, shapes, at = [], [], [], {}
    for i in SQUARE + (1,) + TALL + (15,):
        w = shards[i]
        if i == 15:
            w = jnp.concatenate([w, jnp.zeros((-w.shape[0] % 32, w.shape[1]), BF)])
        rows = w.shape[-2] // 2
        for tap in range(3) if w.ndim == 3 else (None,):
            at[i, tap] = len(plan)
            plan.append((len(ins), rows, len(shapes), None, "n"))
            ins.append(w if tap is None else w[tap])
            shapes.append((4, 2, 2, rows, D))
    for i in BROAD:
        at[i, None] = len(plan)
        plan.append((len(ins), shards[i].shape[0], len(shapes), None, "w"))
        ins.append(shards[i])
        shapes.append((2, 2, 4, 2) + shards[i].shape)
    at[0, None] = len(plan)
    plan.append((len(ins), SMALL_ROWS, len(shapes), None, "w"))
    ins.append(small_block(shards))
    shapes.append((2, 2, 4, 2, SMALL_ROWS, 128))
    first = [at[0, None], at[1, 0], at[1, 1], at[1, 2], at[4, None], at[5, None], at[6, None]]
    order = first + [k for k in range(len(plan)) if k not in first]
    outs = gather_and_stem([plan[k] for k in order], ins, shapes, patches, angles)
    outs, made = outs[: len(plan)], outs[len(plan) :]
    full = [None] * 32
    for i in SQUARE + TALL:
        full[i] = outs[at[i, None]].reshape(-1, D)
    full[1] = [outs[at[1, tap]].reshape(D, D) for tap in range(3)]
    r = shards[15].shape[0]
    full[15] = outs[at[15, None]].reshape(8, -1, D)[:, :r].reshape(8 * r, D)
    for i in BROAD:
        full[i] = outs[at[i, None]].reshape(4, D, D)
    t, a, b = shards[0].shape
    conv1 = outs[at[0, None]][..., : t * a, :b].reshape(2, 2, 4, 2, t, a, b)
    full[0] = conv1.transpose(4, 0, 1, 5, 2, 3, 6).reshape(t, 4 * a, 8 * b)
    for k, i in enumerate(VECTORS):
        full[i] = made[13][k]
    return full, made[:13]


ORDER = (31, 30, 27, 24, 21, 18, 19, 20, 11, 10, 25, 26, 7, 4, 5, 6, 1)
EXACT = 25
HEAD_START = 1
MIX = 2


def reduce_grads(grads, shards):
    items, jobs, ins, shapes, seen = [], [], [], [], {}

    def place(v):
        if id(v) not in seen:
            seen[id(v)] = len(ins)
            ins.append(v)
        return seen[id(v)]

    for i in ORDER:
        left, right = grads[i]
        if i in TALL:
            jobs += [(len(items), s, place(left), place(right), left.shape[1]) for s in range(4)]
            items.append(("t", BF, len(shapes), None))
            shapes.append((2, 2, 2, RB, LANES // 2))
        elif i in BROAD:
            jobs += [(len(items), s, place(left), place(right), left.shape[0]) for s in range(4)]
            items.append(("w", BF, len(shapes), None))
            shapes.append((2, RB, D))
        elif i == 1:
            for tap, l in enumerate(left):
                jobs.append((len(items), 0, place(l), place(right), l.shape[0]))
                items.append(("n", BF, len(shapes), tap))
            shapes.append((3, 2, RB, LANES // 2))
        else:
            jobs.append((len(items), 0, place(left), place(right), left.shape[0]))
            items.append(("n", F32 if i == EXACT else BF, len(shapes), None))
            shapes.append((2, RB, LANES // 2))
    t, a, b = shards[0].shape
    conv1 = grads[0].reshape(t, 2, 2, a, 4, 2, b).transpose(1, 2, 4, 5, 0, 3, 6)
    n = shards[VECTORS[0]].size
    vecs = jnp.stack([grads[i] for i in VECTORS]).reshape(-1, 4, 2, 2, 2, n)
    flat = [conv1.reshape(2, 2, 4, 2, -1), vecs.transpose(3, 4, 1, 2, 0, 5).reshape(2, 2, 4, 2, -1)]
    size = sum(f.shape[-1] for f in flat)
    flat.append(jnp.zeros((2, 2, 4, 2, MISC_ROWS * D - size), F32))
    ins.append(jnp.concatenate(flat, axis=-1).astype(BF).reshape(2, 2, 4, 2, 2, MISC_ROWS // 2, D))
    items.append(("m", BF, len(shapes), None))
    shapes.append((2, MISC_ROWS // 2, D))
    small = [j for j in jobs if items[j[0]][0] == "n"]
    large = [j for j in jobs if items[j[0]][0] != "n"]
    jobs, large = small[:HEAD_START], list(large)
    for j in small[HEAD_START:]:
        jobs += large[:MIX] + [j]
        large = large[MIX:]
    jobs = jobs[:-1] + large + jobs[-1:]
    got = reduce_fast(items, jobs, ins, shapes)
    out = [None] * 32
    for i, v in zip(ORDER, got):
        out[i] = v.reshape(shards[i].shape)
    misc = got[-1].reshape(-1)
    out[0] = misc[: shards[0].size].reshape(shards[0].shape)
    at = shards[0].size
    for i in VECTORS:
        out[i] = misc[at : at + n]
        at += n
    return out


def one_hot(ids, table):
    first = lax.axis_index("dp") * table.shape[0]
    return ((ids - first)[:, None] == jnp.arange(table.shape[0])[None, :]).astype(BF)


def body(mel_frames, token_ids, token_counts, *rest):
    shards, cotangent = list(rest[:32]), rest[32][0]
    table = shards[14]
    dps, seqs = lax.axis_size("dp"), lax.axis_size("seq")
    me = lax.axis_index("seq")
    slots = token_ids.shape[1]
    all_slots = slots * seqs
    frames = mel_frames.shape[1] // 2

    fast = dps == 8 and seqs == 4
    weights = shards[:14] + [None] + shards[15:]
    if fast:
        ids = share_ids(token_ids[0])
    else:
        ids = lax.all_gather(token_ids[0], BOTH, axis=0, tiled=True)
    hot = one_hot(ids, table)
    looked = mm(hot, table, BF)

    mine = lax.psum_scatter(looked, "dp", scatter_dimension=0, tiled=True)

    pairs = extended(mel_frames[0], 2).reshape(frames + 2, -1)
    mels = mel_frames.shape[2]
    n = frames + 1
    even_in = jnp.concatenate([pairs[:n], pairs[1:, :mels]], axis=1)
    odd_in = jnp.concatenate([pairs[:n, mels:], pairs[1:]], axis=1)
    angles = sinusoid(me * frames, frames)
    row = jnp.arange(n)[:, None]
    even_keep = (row > 0) | (me > 0)
    odd_keep = (row < n - 1) | (me < seqs - 1)
    if fast:
        patches = [patch_rows(p, mels) for p in (even_in, odd_in, even_in[1:])]
        patches[0], _ = lax.optimization_barrier((patches[0], looked))
        full, made = gather_weights(weights, patches, angles)
        even_pre, odd_pre, even0, odd0, even1, second_pre, stream0, enc_normed, q, k_all, v_all = made[:11]
        enc_mixed, enc_lse = made[11:]
        even_pre, odd_pre = even_pre[:n], odd_pre[:n]
        even0, odd0, even1 = even0[:frames], odd0[:frames], even1[:frames]
    else:
        full = gather_plain(weights)
        conv1, conv2 = full[0].reshape(-1, D), full[1]
        even_pre, odd_pre = mm(even_in, conv1), mm(odd_in, conv1)
        even = jnp.where(even_keep, gelu(even_pre), 0.0).astype(BF)
        odd0 = jnp.where(odd_keep, gelu(odd_pre), 0.0).astype(BF)[:frames]
        even0, even1 = even[:frames], even[1:]
        second_pre = mm(even0, conv2[0]) + mm(odd0, conv2[1]) + mm(even1, conv2[2])
        stream0 = gelu(second_pre) + angles
        enc_normed = norm(stream0, full[2].astype(F32), full[3].astype(F32))
        q = (mm(enc_normed, full[4]) * SCALE).astype(BF)
        k, v = mm(enc_normed, full[5], BF), mm(enc_normed, full[6], BF)
        enc_mixed, enc_lse, k_all, v_all = clip_attend(q, k, v)
    vec = {i: full[i].astype(F32) for i in range(32) if KINDS[i] == "v"}
    conv1, conv2, position = full[0].reshape(-1, D), full[1], full[15]
    eo = full[7]
    ee, ec = full[10:12]
    dq_w, dk_w, dv_w, do_w = full[18:22]
    cq_w, ck_w, cv_w, co_w = full[24:28]
    de, dc = full[30:32]


    stream1 = stream0 + mm(enc_mixed, eo)
    enc_mlp_normed, enc_pre, enc_hidden, stream2 = mlp(stream1, vec[8], vec[9], ee, ec)
    memory = norm(stream2, vec[12], vec[13])
    mk = mm(memory, ck_w, BF)
    mv = mm(memory, cv_w, BF)

    mine, enc_mixed = lax.optimization_barrier((mine, enc_mixed))
    looked = lax.all_gather(mine, "seq", axis=0, tiled=True)
    looked = looked.reshape(seqs, all_slots, D // seqs).transpose(1, 0, 2).reshape(all_slots, D)
    place = jnp.arange(all_slots)
    embedded = looked.astype(F32) + position.astype(F32)
    dec_normed = norm(embedded, vec[16], vec[17])
    sq = (mm(dec_normed, dq_w) * SCALE).astype(BF)
    sk = mm(dec_normed, dk_w, BF)
    sv = mm(dec_normed, dv_w, BF)
    dec_mixed, dec_lse = attend(sq, sk, sv, token_counts)
    stream4 = embedded + mm(dec_mixed, do_w)
    cross_normed = norm(stream4, vec[22], vec[23])
    xq = (mm(cross_normed, cq_w) * SCALE).astype(BF)

    part, part_lse = attend(xq, mk, mv)
    parts, lses = unpack(exchange(pack(part, part_lse)))
    top = jnp.max(lses, axis=0)
    share = jnp.exp(lses - top)
    total = jnp.sum(share, axis=0)
    cross_lse = top + jnp.log(total)
    share = share / total
    cross_mixed = jnp.sum(
        parts.astype(F32).reshape(seqs, slots, HEADS, HEAD) * share[..., None], axis=0
    ).reshape(slots, D)
    cross_mixed = cross_mixed.astype(BF)

    own = lambda a: lax.dynamic_slice_in_dim(a, me * slots, slots, 0)
    stream4 = own(stream4)
    stream5 = stream4 + mm(cross_mixed, co_w)
    dec_mlp_normed, dec_pre, dec_hidden, stream6 = mlp(stream5, vec[28], vec[29], de, dc)
    live = (own(place) < token_counts[0])[:, None]
    decoded = jnp.where(live, stream6, 0.0).astype(BF)

    grads = [None] * 32

    def mlp_back(ex, co, gain, normed, pre, hidden, stream, up):
        up, d_low, d_pre, d_gain, d_bias = mlp_backward(up, stream, vec[gain], pre, full[ex], full[co])
        grads[co], grads[ex] = (hidden, d_low), (normed, d_pre)
        grads[gain], grads[gain + 1] = d_gain[0], d_bias[0]
        return up

    up = jnp.where(live, cotangent.astype(F32), 0.0)
    up = mlp_back(30, 31, 28, dec_mlp_normed, dec_pre, dec_hidden, stream5, up)
    d_low = up.astype(BF)
    grads[27] = (cross_mixed, d_low)
    d_mixed = mm_t(d_low, co_w, BF)
    d_mixed, lse_all = unpack(lax.all_gather(pack(d_mixed, cross_lse.T), "seq", axis=0, tiled=True))
    lse_all = lse_all.T
    sums = lax.psum(jnp.stack(attend_sums(xq, mk, mv, d_mixed, lse_all)), "seq")
    dxq, dmk, dmv = attend_back(xq, mk, mv, d_mixed, lse_all, inner=sums[1] / sums[0], out=F32)
    dxq = jnp.sum(exchange(dxq), axis=0)
    dxq = (low(dxq) * SCALE).astype(BF)
    grads[24] = (own(cross_normed), dxq)
    back, grads[22], grads[23] = norm_back(stream4, vec[22], mm_t(dxq, cq_w))
    up = up + back
    d_low = up.astype(BF)
    grads[21] = (own(dec_mixed), d_low)
    d_mixed = lax.all_gather(mm_t(d_low, do_w, BF), "seq", axis=0, tiled=True)
    dsq, dsk, dsv = attend_back(sq, sk, sv, d_mixed, dec_lse, token_counts)

    def inputs_back(first, gain, normed, stream, dq, dk, dv, up):
        dq = (dq.astype(F32) * SCALE).astype(BF)
        total = 0.0
        for i, g in enumerate((dq, dk, dv)):
            grads[first + i] = (normed, g)
            total = total + mm_t(g, full[first + i])
        back, grads[gain], grads[gain + 1] = norm_back(stream, vec[gain], total)
        return up + back

    up = inputs_back(18, 16, own(dec_normed), own(embedded), own(dsq), own(dsk), own(dsv), up)

    cols = exchange_columns(up.astype(BF))
    every = lax.all_gather(cols, "dp", axis=0, tiled=True)
    grad_table = dot(hot, every, 0, 0)
    per_clip = every.reshape(dps, dps, -1, D // seqs)
    grad_position = jnp.sum(
        lax.dynamic_index_in_dim(per_clip, lax.axis_index("dp"), 1, False).astype(F32), axis=0
    )

    grads[25] = (memory, dmk)
    grads[26] = (memory, dmv)
    up, grads[12], grads[13] = norm_back(stream2, vec[12], mm_t(dmk, ck_w) + mm_t(dmv, cv_w))
    up = mlp_back(10, 11, 8, enc_mlp_normed, enc_pre, enc_hidden, stream1, up)
    d_low = up.astype(BF)
    grads[7] = (enc_mixed, d_low)
    d_mixed = mm_t(d_low, eo, BF)
    dq, dk, dv = clip_attend_back(q, k_all, v_all, d_mixed, enc_lse)
    up = inputs_back(4, 2, enc_normed, stream0, dq, dk, dv, up)

    d_second = (gelu_slope(second_pre) * up).astype(BF)
    grads[1] = ([even0, odd0, even1], d_second)
    rim = extended(d_second, 1)
    d_even = mm_t(rim[1:], conv2[0]) + mm_t(rim[:n], conv2[2])
    d_odd = mm_t(rim[1:], conv2[1])
    d_even = jnp.where(even_keep, gelu_slope(even_pre) * low(d_even), 0.0).astype(BF)
    d_odd = jnp.where(odd_keep, gelu_slope(odd_pre) * low(d_odd), 0.0).astype(BF)
    grads[0] = (outer(odd_in[:frames], d_odd[:frames], F32) + outer(even_in[1:], d_even[1:], F32)).reshape(
        3, mels, D
    )
    me_g, mo_g = mm_t(d_even, conv1), mm_t(d_odd, conv1)
    mel_grad = jnp.concatenate(
        [
            me_g[1:, :mels] + me_g[:-1, 2 * mels :] + mo_g[:-1, mels : 2 * mels],
            me_g[1:, mels : 2 * mels] + mo_g[1:, :mels] + mo_g[:-1, 2 * mels :],
        ],
        axis=1,
    ).reshape(1, 2 * frames, mels)

    done = (reduce_grads if fast else reduce_plain)(grads, shards)
    done[14], done[15] = grad_table, grad_position
    return tuple([decoded[None], mel_grad] + done)


def exchange_columns(v):
    n = lax.axis_size("seq")
    wide = v.shape[1] // n
    v = v.reshape(v.shape[0], n, wide).transpose(1, 0, 2)
    return lax.all_to_all(v, "seq", split_axis=0, concat_axis=0, tiled=True).reshape(-1, wide)


def solution(mesh):
    place = {
        "1": P(None, "seq", "dp"),
        "2": P(None, "dp", "seq"),
        "v": P(BOTH),
        "m": P("dp", "seq"),
        "t": P("dp", "seq"),
    }
    rows = P("dp", "seq", None)
    weights = tuple(place[k] for k in KINDS)
    return jax.shard_map(
        body,
        mesh=mesh,
        in_specs=(rows, P("dp", "seq"), P("dp")) + weights + (rows,),
        out_specs=(rows, rows) + weights,
        check_vma=False,
    )
```

```python
import functools
import math

import jax
import jax.numpy as jnp
from jax import lax
from jax.experimental import pallas as pl
from jax.experimental.pallas import tpu as pltpu
from jax.sharding import PartitionSpec as P

D = 768
HEADS = 12
HEAD = 64
EPSILON = 1e-05
NEGATIVE = -1e30
SCALE = 1.0 / math.sqrt(HEAD)
BF = jnp.bfloat16
F32 = jnp.float32
BOTH = ("dp", "seq")

KINDS = "12vvmmmmvvmmvvtmvvmmmmvvmmmmvvmm"


def dot(a, b, ca, cb, out=F32):
    return lax.dot_general(a, b, (((ca,), (cb,)), ((), ())), preferred_element_type=F32).astype(out)


def mm(a, b, out=F32):
    return dot(a, b, 1, 0, out)


def mm_t(a, b, out=F32):
    return dot(a, b, 1, 1, out)


def outer(a, b, out=BF):
    return dot(a, b, 0, 0, out)


def norm_parts(values):
    center = values - jnp.mean(values, axis=-1, keepdims=True)
    spread = jnp.mean(center * center, axis=-1, keepdims=True)
    inv = lax.rsqrt(spread + EPSILON)
    return center * inv, inv


def norm(values, gain, bias):
    return (norm_parts(values)[0] * gain + bias).astype(BF)


def norm_back(values, gain, up):
    hat, inv = norm_parts(values)
    g = up * gain
    back = inv * (
        g - jnp.mean(g, axis=-1, keepdims=True) - hat * jnp.mean(g * hat, axis=-1, keepdims=True)
    )
    return back, jnp.sum(up * hat, axis=0), jnp.sum(up, axis=0)


def gelu(v):
    return v * (0.5 + 0.5 * lax.erf(v * math.sqrt(0.5)))


def gelu_slope(v):
    return (0.5 + 0.5 * lax.erf(v * math.sqrt(0.5))) + v * jnp.exp(-0.5 * v * v) * (
        1.0 / math.sqrt(2.0 * math.pi)
    )


def low(v):
    return lax.reduce_precision(v, 8, 7)


PAIR = 2 * HEAD


def tdot(a, b, ca, cb):
    return lax.dot_general(a, b, (((ca,), (cb,)), ((), ())), preferred_element_type=F32)


def one_head(rows, half):
    lane = lax.broadcasted_iota(jnp.int32, rows.shape, 1)
    return jnp.where((lane < HEAD) == (half == 0), rows, jnp.zeros_like(rows))


def masked(s, count_ref):
    if count_ref is None:
        return s
    key = lax.broadcasted_iota(jnp.int32, s.shape, 0)
    query = lax.broadcasted_iota(jnp.int32, s.shape, 1)
    return jnp.where((key <= query) & (key < count_ref[0]), s, NEGATIVE)


def pack(rows, log_sums):
    cols, rest = [rows], log_sums.T
    for _ in range(3):
        term = low(rest)
        cols.append(term.astype(BF))
        rest = rest - term
    wide = sum(c.shape[1] for c in cols)
    return jnp.concatenate(cols + [jnp.zeros((rows.shape[0], -wide % 128), BF)], axis=1)


def unpack(packed):
    terms = [packed[..., D + i * HEADS : D + (i + 1) * HEADS].astype(F32) for i in range(3)]
    return packed[..., :D], terms[0] + terms[1] + terms[2]


def shift(v, axis, step):
    n = lax.axis_size(axis)
    return lax.ppermute(v, axis, [(i, i + step) for i in range(n) if 0 <= i + step < n])


def extended(x, width):
    before = shift(x[-width:], "seq", 1)
    after = shift(x[:width], "seq", -1)
    return jnp.concatenate([before, x, after], axis=0)


def exchange(v):
    n = lax.axis_size("seq")
    got = lax.all_to_all(v, "seq", split_axis=0, concat_axis=0, tiled=True)
    return got.reshape(n, v.shape[0] // n, v.shape[1])


def sinusoid(first_frame, frame_count):
    half = D // 2
    frequency = jnp.exp(jnp.arange(half).astype(F32) * (-math.log(10000.0) / (half - 1)))
    places = (first_frame + jnp.arange(frame_count)).astype(F32)
    angles = places[:, None] * frequency[None, :]
    return jnp.concatenate([jnp.sin(angles), jnp.cos(angles)], axis=1)


def to_whole(flat, shape, kind, dps, seqs):
    if kind == "v":
        return flat.reshape(-1)
    if kind == "1":
        t, i, o = shape
        return (
            flat.reshape(dps, seqs, t, i, o)
            .transpose(2, 1, 3, 0, 4)
            .reshape(t, seqs * i, dps * o)
        )
    if kind == "2":
        t, i, o = shape
        return (
            flat.reshape(dps, seqs, t, i, o)
            .transpose(2, 0, 3, 1, 4)
            .reshape(t, dps * i, seqs * o)
        )
    r, c = shape
    return flat.reshape(dps, seqs, r, c).transpose(0, 2, 1, 3).reshape(dps * r, seqs * c)


def to_owner(g, kind, dps, seqs):
    n = dps * seqs
    if kind == "v":
        return g.reshape(n, -1)
    if kind == "1":
        t, i, o = g.shape
        g = g.reshape(t, seqs, i // seqs, dps, o // dps).transpose(3, 1, 0, 2, 4)
    elif kind == "2":
        t, i, o = g.shape
        g = g.reshape(t, dps, i // dps, seqs, o // seqs).transpose(1, 3, 0, 2, 4)
    else:
        r, c = g.shape
        g = g.reshape(dps, r // dps, seqs, c // seqs).transpose(0, 2, 1, 3)
    return g.reshape(n, -1)


def gather_plain(shards):
    dps, seqs = lax.axis_size("dp"), lax.axis_size("seq")
    flat = jnp.concatenate([w.reshape(-1) for w in shards if w is not None])
    got = lax.all_gather(flat[None], BOTH, axis=0, tiled=True)
    out, at = [], 0
    for w, kind in zip(shards, KINDS):
        if w is None:
            out.append(None)
            continue
        out.append(to_whole(got[:, at : at + w.size], w.shape, kind, dps, seqs))
        at += w.size
    for i in BROAD:
        out[i] = out[i].reshape(D, seqs, -1).transpose(1, 0, 2)
    return out


def product(factors):
    left, right = factors
    if right.ndim == 3:
        return jnp.concatenate([outer(left, r) for r in right], axis=1)
    if isinstance(left, list) or left.ndim == 3:
        return jnp.stack([outer(l, right) for l in left])
    return outer(left, right)


def reduce_plain(grads, shards):
    dps, seqs = lax.axis_size("dp"), lax.axis_size("seq")
    grads = [product(g) if isinstance(g, tuple) else g for g in grads]
    for i in TALL:
        grads[i] = grads[i].reshape(-1, D)
    flat = jnp.concatenate(
        [to_owner(g.astype(BF), k, dps, seqs) for g, k in zip(grads, KINDS) if g is not None], axis=1
    )
    own = lax.psum_scatter(flat, BOTH, scatter_dimension=0, tiled=True).astype(F32)[0]
    out, at = [], 0
    for w, g in zip(shards, grads):
        if g is None:
            out.append(None)
            continue
        out.append(own[at : at + w.size].reshape(w.shape))
        at += w.size
    return out


MESH = pl.DeviceIdType.MESH
LANES = 384


def where_am_i():
    d, s = lax.axis_index("dp"), lax.axis_index("seq")
    return d // 2, d % 2, s // 2, s % 2


def partners(z, y, x, c):
    at = lambda z, y, x, c: (z * 2 + y, x * 2 + c)
    zs = [at((z + j) % 4, y, x, c) for j in (1, 2, 3)]
    return zs, at(z, 1 - y, x, c), at(z, y, 1 - x, c), at(z, y, x, 1 - c)


def greet(zs, yp, xp, cp):
    barrier = pltpu.get_barrier_semaphore()
    everyone = zs + [yp, xp, cp]
    for dev in everyone:
        pl.semaphore_signal(barrier, inc=1, device_id=dev, device_id_type=MESH)
    pl.semaphore_wait(barrier, len(everyone))


def remote(src, dst, send, recv, dev):
    return pltpu.make_async_remote_copy(
        src_ref=src, dst_ref=dst, send_sem=send, recv_sem=recv, device_id=dev, device_id_type=MESH
    )


def split_at(i, rows):
    return rows // 2 if rows % 32 == 0 else 16 + 16 * (i % 2)


def lanes(x):
    return pl.ds(pl.multiple_of(x * LANES, LANES), LANES)


def spot(ref, wide, zs, ys, xs, c, rs):
    full = lambda v: slice(None) if v is None else v
    if wide:
        return ref.at[full(xs), c, full(zs), full(ys), rs, :]
    return ref.at[full(zs), full(ys), c, rs, slice(None) if xs is None else lanes(xs)]


def add_into(dst, *srcs):
    lead = srcs[0].shape[:-2]
    total = math.prod(lead)

    def one(k, _):
        at = []
        for size in reversed(lead):
            at.append(lax.rem(k, size))
            k = lax.div(k, size)
        at = tuple(reversed(at))
        acc = srcs[0][at].astype(F32)
        for s in srcs[1:]:
            acc = acc + s[at].astype(F32)
        dst[at] = acc.astype(dst.dtype)
        return 0

    lax.fori_loop(0, total, one, 0)


RB = 48


def item_shapes(kind, h):
    if kind == "n":
        g = RB - h
        return [
            (4, 2, RB, D),
            (4, h, D),
            (4, 2, g, LANES),
            (4, h, LANES),
            (4, g, LANES),
            (4, RB, LANES),
            (3, RB, LANES),
        ]
    if kind == "t":
        return [
            (4, 4, 2, RB, D),
            (4, 2, RB, D),
            (4, 4, RB, LANES),
            (4, 2, RB, LANES),
            (4, 2, RB, LANES),
            (4, 2, 2, RB, LANES),
            (3, 2, 2, RB, LANES),
        ]
    w = D if kind == "w" else 128
    return [
        (2, 4, 2, 2, RB, w),
        (2, 4, RB, w),
        (4, 2, RB, w),
        (4, RB, w),
        (4, RB, w),
        (4, 2, RB, w),
        (3, 2, RB, w),
    ]


def halves_of(k):
    return 16 + 16 * (k % 2)


def reduce_kernel(items, jobs, inputs, outputs, *refs):
    n = len(items)
    take = lambda count: (refs[:count], refs[count:])
    ins, refs = take(inputs)
    outs, refs = take(outputs)
    rc, refs = take(n)
    r1a, refs = take(n)
    r1b, refs = take(n)
    r2a, refs = take(n)
    r2b, refs = take(n)
    s3, refs = take(n)
    rz, refs = take(n)
    sbuf, refs = take(n)
    ring, wide_ring, given, xbuf, ybuf = refs[:5]
    loads, csend, crecv, xsend, xrecv, ysend, yrecv, zsend, zrecv, fsend, frecv = refs[5:]
    z, y, x, c = where_am_i()
    zs, yp, xp, cp = partners(z, y, x, c)
    greet(zs, yp, xp, cp)
    started = []

    def start(copy):
        copy.start()
        started.append(copy)
        return copy

    cores, ones, twos, threes, loaded = {}, {}, {}, {}, {}
    half = lambda i: halves_of(i)
    at = {(j[0], j[1]): t for t, j in enumerate(jobs)}

    def load(t):
        _, part, xi, yi, rows = jobs[t]
        xsrc, ysrc = ins[xi], ins[yi]
        if len(xsrc.shape) == 3:
            xsrc = xsrc.at[part]
        elif xsrc.shape[0] > rows:
            xsrc = xsrc.at[0:rows]
        if len(ysrc.shape) == 3:
            ysrc = ysrc.at[2 * (part // 2) + (c if part % 2 else 1 - c)]
        pair = []
        for k, (src, buf) in enumerate(((xsrc, xbuf), (ysrc, ybuf))):
            copy = pltpu.make_async_copy(src, buf.at[t % 2, 0:rows], loads.at[t % 2, k])
            copy.start()
            pair.append(copy)
        loaded[t] = pair

    def room(t):
        return wide_ring if items[jobs[t][0]][1] == F32 else ring.at[t % RING]

    def compute(t):
        i, part, _, _, rows = jobs[t]
        if t >= RING and t - RING in cores and items[jobs[t - RING][0]][1] == BF:
            cores[t - RING].wait_send()
        for copy in loaded[t]:
            copy.wait()
        room_t = room(t)
        left = xbuf[t % 2, 0:rows, :]

        def column(k, _):
            cols = pl.ds(pl.multiple_of(k * 256, 256), 256)
            product = tdot(left, ybuf[t % 2, 0:rows, cols], 0, 0)
            room_t[:, :, :, :, cols] = product.reshape(4, 2, 2, RB, 256).astype(room_t.dtype)
            return 0

        lax.fori_loop(0, D // 256, column, 0)
        if t + 2 < len(jobs):
            load(t + 2)
        kind = items[i][0]
        if kind == "n":
            cores[t] = remote(room_t.at[:, :, 1 - c], rc[i], csend.at[t], crecv.at[t], cp)
        elif kind == "t":
            cores[t] = remote(room_t.at[:, :, 1 - c], rc[i].at[part], csend.at[t], crecv.at[t], cp)
        elif part % 2 == 0:
            cores[t] = remote(room_t, rc[i].at[part // 2], csend.at[t], crecv.at[t], cp)
        if t in cores:
            cores[t].start()

    def add_own(t):
        i, part, _, _, _ = jobs[t]
        kind, mine = items[i][0], room(t)
        if kind == "w":
            if part % 2 == 0:
                return False
            cores[at[i, part - 1]].wait_recv()
            add_into(rc[i].at[part // 2], mine, rc[i].at[part // 2])
            return part == 3
        cores[t].wait_recv()
        dst = rc[i] if kind == "n" else rc[i].at[part]
        add_into(dst, mine.at[:, :, c], dst)
        return kind == "n" or part == 3

    def views(i):
        kind, h = items[i][0], half(i)
        r, a, b = rc[i], r1a[i], r1b[i]
        here, there = lanes(x), lanes(1 - x)
        if kind == "n":
            one = (r.at[:, 1 - y, 0:h, :], r.at[:, :, h:RB, there], r.at[:, y, 0:h, :], r.at[:, :, h:RB, here])
            two = (a.at[:, :, there], b.at[:, 1 - y], a.at[:, :, here], b.at[:, y])
            parts = (s3[i].at[:, 0:h, :], s3[i].at[:, h:RB, :])
        elif kind == "t":
            up, down = pl.ds(2 * y, 2), pl.ds(2 * (1 - y), 2)
            one = (r.at[:, down, 0], r.at[:, :, 1, :, there], r.at[:, up, 0], r.at[:, :, 1, :, here])
            two = (a.at[:, :, :, there], b.at[:, down], a.at[:, :, :, here], b.at[:, up])
            parts = (s3[i].at[:, 0], s3[i].at[:, 1])
        else:
            one = (r.at[:, :, 1 - y, 0], r.at[1 - x, :, :, 1], r.at[:, :, y, 0], r.at[x, :, :, 1])
            two = (a.at[1 - x], b.at[:, 1 - y], a.at[x], b.at[:, y])
            parts = (s3[i].at[:, 0], s3[i].at[:, 1])
        return one, two, parts

    def send_1(i):
        (over_y, over_x, _, _), _, _ = views(i)
        ones[i] = [
            start(remote(over_y, r1a[i], ysend.at[i, 0], yrecv.at[i, 0], yp)),
            start(remote(over_x, r1b[i], xsend.at[i, 0], xrecv.at[i, 0], xp)),
        ]

    def send_2(i):
        (_, _, stay_a, stay_b), (over_x, over_y, _, _), _ = views(i)
        ones[i][0].wait_recv()
        add_into(r1a[i], stay_a, r1a[i])
        first = start(remote(over_x, r2a[i], xsend.at[i, 1], xrecv.at[i, 1], xp))
        ones[i][1].wait_recv()
        add_into(r1b[i], stay_b, r1b[i])
        twos[i] = [first, start(remote(over_y, r2b[i], ysend.at[i, 1], yrecv.at[i, 1], yp))]

    def send_z(i):
        _, (_, _, stay_a, stay_b), (part_a, part_b) = views(i)
        twos[i][0].wait_recv()
        add_into(part_a, stay_a, r2a[i])
        twos[i][1].wait_recv()
        add_into(part_b, stay_b, r2b[i])
        threes[i] = [
            start(remote(s3[i].at[(z + j + 1) % 4], rz[i].at[j], zsend.at[i, j], zrecv.at[i, j], zs[j]))
            for j in range(3)
        ]

    finals = []

    def finish(i):
        kind, _, out, tap = items[i]
        for copy in threes[i]:
            copy.wait_recv()
        acc = s3[i][z].astype(F32)
        for j in range(3):
            acc = acc + rz[i][j].astype(F32)
        dst = outs[out] if tap is None else outs[out].at[tap]
        if kind in "wm":
            dst[...] = acc
            return
        mine = acc[..., : LANES // 2]
        theirs = acc[..., LANES // 2 :]
        keep = jnp.where(c == 0, mine, theirs)
        other = jnp.where(c == 0, theirs, mine)
        if kind == "n":
            sbuf[i][...] = other
            dst[c] = keep
            finals.append(start(remote(sbuf[i], dst.at[c], fsend.at[i], frecv.at[i], cp)))
            return
        for a in (0, 1):
            for b in (0, 1):
                dst[b, a, c] = keep[a, b]
                sbuf[i][b, a] = other[a, b]
        finals.append(start(remote(sbuf[i], dst.at[:, :, c], fsend.at[i], frecv.at[i], cp)))

    g = [i for i in range(n) if items[i][0] == "m"][0]
    last = len(jobs)
    theirs = start(remote(ins[-1].at[:, 1 - c], rc[g], csend.at[last], crecv.at[last], cp))
    mine = pltpu.make_async_copy(ins[-1].at[:, c], given, loads.at[0, 2])
    mine.start()
    load(0)
    load(1)
    queue = [[], [], []]
    steps = (send_2, send_z, finish)

    def advance(keep):
        for k in (2, 1, 0):
            while len(queue[k]) > keep:
                i = queue[k].pop(0)
                steps[k](i)
                if k < 2:
                    queue[k + 1].append(i)

    mine.wait()
    for t in range(last + 1):
        if t < last:
            compute(t)
        if t == 1:
            theirs.wait_recv()
            add_into(rc[g], given, rc[g])
            send_1(g)
            queue[0].append(g)
        if t >= 1 and add_own(t - 1):
            i = jobs[t - 1][0]
            send_1(i)
            queue[0].append(i)
        advance(LAG)
    for keep in range(LAG - 1, -1, -1):
        advance(keep)
    while queue[0] or queue[1] or queue[2]:
        advance(0)
    for copy in finals:
        copy.wait_recv()
    for copy in started:
        copy.wait_send()
    for t in cores:
        if t + RING >= last or items[jobs[t][0]][1] == F32:
            cores[t].wait_send()


RING = 3
LAG = 1


def reduce_fast(items, jobs, ins, out_shapes):
    n, m = len(items), len(jobs)
    sem = pltpu.SemaphoreType.DMA
    groups = [[] for _ in range(8)]
    for i, (kind, dtype, _, _) in enumerate(items):
        for group, shape in zip(groups, item_shapes(kind, halves_of(i))):
            group.append(pltpu.VMEM(shape, dtype))
        last = {"n": (RB, LANES // 2), "t": (2, 2, RB, LANES // 2)}.get(kind, (8, 128))
        groups[7].append(pltpu.VMEM(last, F32))
    scratch = [s for group in groups for s in group]
    scratch += [
        pltpu.VMEM((RING, 4, 2, 2, RB, D), BF),
        pltpu.VMEM((4, 2, 2, RB, D), F32),
        pltpu.VMEM((2, 4, 2, 2, RB, 128), BF),
    ]
    most = max(j[4] for j in jobs)
    scratch += [pltpu.VMEM((2, most, D), BF)] * 2
    scratch += [sem((2, 3)), sem((m + 1,)), sem((m + 1,))]
    scratch += [sem((n, 2))] * 4 + [sem((n, 3))] * 2 + [sem((n,))] * 2
    vmem = pl.BlockSpec(memory_space=pltpu.VMEM)
    return pl.pallas_call(
        functools.partial(reduce_kernel, items, jobs, len(ins), len(out_shapes)),
        out_shape=[jax.ShapeDtypeStruct(s, F32) for s in out_shapes],
        in_specs=[pl.BlockSpec(memory_space=pl.ANY)] * len(ins),
        out_specs=[vmem] * len(out_shapes),
        scratch_shapes=scratch,
        compiler_params=pltpu.CompilerParams(
            collective_id=2, has_side_effects=True, vmem_limit_bytes=62 << 20
        ),
    )(*ins)


def lanes_of(pair):
    return pl.ds(pl.multiple_of(pair * PAIR, PAIR), PAIR)


def clip_partners():
    d, s = lax.axis_index("dp"), lax.axis_index("seq")
    x, c = s // 2, s % 2
    return (d, (1 - x) * 2 + c), (d, x * 2 + 1 - c)


def greet_pair(xp, cp):
    barrier = pltpu.get_barrier_semaphore()
    for dev in (xp, cp):
        pl.semaphore_signal(barrier, inc=1, device_id=dev, device_id_type=MESH)
    pl.semaphore_wait(barrier, 2)


def forward_head(q_one, k_slab, v_slab, half, count):
    s = masked(tdot(k_slab, q_one, 1, 1), count)
    top = jnp.max(s, axis=0, keepdims=True)
    e = jnp.exp(s - top)
    total = jnp.sum(e, axis=0, keepdims=True)
    mixed = tdot(v_slab, e.astype(BF), 0, 0)[half * HEAD : (half + 1) * HEAD]
    return mixed / total, top + jnp.log(total)


def forward_pair(pair, q, k, v, o, lse, count):
    at = lanes_of(pair)
    q_slab, k_slab, v_slab = q[:, at], k[:, at], v[:, at]
    both = []
    for half in (0, 1):
        mixed, log_sum = forward_head(one_head(q_slab, half), k_slab, v_slab, half, count)
        both.append(mixed)
        lse[pl.ds(2 * pair + half, 1), :] = log_sum
    o[:, at] = jnp.concatenate(both, axis=0).T.astype(o.dtype)


def backward_pair(pair, q, k, v, up, lse, dq, dk, dv, count, known):
    at = lanes_of(pair)
    q_slab, k_slab, v_slab, u_slab = q[:, at], k[:, at], v[:, at], up[:, at]
    both, dk_sum, dv_sum = [], 0.0, 0.0
    for half in (0, 1):
        row = pl.ds(2 * pair + half, 1)
        q_one, u_one = one_head(q_slab, half), one_head(u_slab, half)
        p = jnp.exp(masked(tdot(k_slab, q_one, 1, 1), count) - lse[row, :])
        dp = tdot(v_slab, u_one, 1, 1)
        if known is None:
            mass = jnp.sum(p, axis=0, keepdims=True)
            inner = jnp.sum(p * dp, axis=0, keepdims=True) / mass
        else:
            inner = known[row, :]
        ds = (p * (dp - inner)).astype(BF)
        dv_sum = dv_sum + tdot(p.astype(BF), u_one, 1, 0)
        dk_sum = dk_sum + tdot(ds, q_one, 1, 0)
        both.append(tdot(k_slab, ds, 0, 0)[half * HEAD : (half + 1) * HEAD])
    dq[:, at] = jnp.concatenate(both, axis=0).T.astype(dq.dtype)
    dk[:, at] = dk_sum.astype(dk.dtype)
    dv[:, at] = dv_sum.astype(dv.dtype)


def attend_kernel(causal, *refs):
    count = refs[0] if causal else None
    q, k, v, o, lse = refs[1:] if causal else refs

    def step(pair, _):
        forward_pair(pair, q, k, v, o, lse, count)
        return 0

    lax.fori_loop(0, HEADS // 2, step, 0)


def sums_kernel(q, k, v, up, lse, mass, inner):
    def step(pair, _):
        at = lanes_of(pair)
        q_slab, k_slab, v_slab, u_slab = q[:, at], k[:, at], v[:, at], up[:, at]
        for half in (0, 1):
            row = pl.ds(2 * pair + half, 1)
            p = jnp.exp(tdot(k_slab, one_head(q_slab, half), 1, 1) - lse[row, :])
            dp = tdot(v_slab, one_head(u_slab, half), 1, 1)
            mass[row, :] = jnp.sum(p, axis=0, keepdims=True)
            inner[row, :] = jnp.sum(p * dp, axis=0, keepdims=True)
        return 0

    lax.fori_loop(0, HEADS // 2, step, 0)


def back_kernel(causal, given, *refs):
    count, known = None, None
    if causal:
        count, refs = refs[0], refs[1:]
    q, k, v, up, lse = refs[:5]
    refs = refs[5:]
    if given:
        known, refs = refs[0], refs[1:]
    dq, dk, dv = refs

    def step(pair, _):
        backward_pair(pair, q, k, v, up, lse, dq, dk, dv, count, known)
        return 0

    lax.fori_loop(0, HEADS // 2, step, 0)


def clip_attend_kernel(q, k, v, o, lse, k_all, v_all, xsend, xrecv, csend, crecv):
    xp, cp = clip_partners()
    r = q.shape[0]
    greet_pair(xp, cp)
    pairs = HEADS // 2

    def across(pair):
        at = lanes_of(pair)
        return [
            remote(src.at[:, at], dst.at[r : 2 * r, at], xsend.at[j, pair], xrecv.at[j, pair], xp)
            for j, (src, dst) in enumerate(((k, k_all), (v, v_all)))
        ]

    def beside(pair):
        at = lanes_of(pair)
        return [
            remote(a.at[0 : 2 * r, at], a.at[2 * r : 4 * r, at], csend.at[j, pair], crecv.at[j, pair], cp)
            for j, a in enumerate((k_all, v_all))
        ]

    for pair in range(pairs):
        for copy in across(pair):
            copy.start()
    k_all[0:r, :] = k[...]
    v_all[0:r, :] = v[...]

    def pass_on(pair):
        for copy in across(pair):
            copy.wait_recv()
        for copy in beside(pair):
            copy.start()

    pass_on(0)

    def step(pair, _):
        @pl.when(pair + 1 < pairs)
        def _():
            pass_on(pair + 1)

        for copy in beside(pair):
            copy.wait_recv()
        forward_pair(pair, q, k_all, v_all, o, lse, None)
        return 0

    lax.fori_loop(0, pairs, step, 0)
    for pair in range(pairs):
        for copy in across(pair) + beside(pair):
            copy.wait_send()


def clip_back_kernel(q, k, v, up, lse, dq, dk, dv, *refs):
    k_sum, v_sum, k_near, v_near, k_far, v_far, xsend, xrecv, csend, crecv = refs
    xp, cp = clip_partners()
    r = q.shape[0]
    greet_pair(xp, cp)
    pairs = HEADS // 2
    sums, nears, fars, outs = (k_sum, v_sum), (k_near, v_near), (k_far, v_far), (dk, dv)

    def beside(pair):
        at = lanes_of(pair)
        return [
            remote(sums[j].at[2 * r : 4 * r, at], nears[j].at[:, at], csend.at[j, pair], crecv.at[j, pair], cp)
            for j in (0, 1)
        ]

    def across(pair):
        at = lanes_of(pair)
        return [
            remote(sums[j].at[r : 2 * r, at], fars[j].at[:, at], xsend.at[j, pair], xrecv.at[j, pair], xp)
            for j in (0, 1)
        ]

    def step(t, _):
        @pl.when(t < pairs)
        def _():
            backward_pair(t, q, k, v, up, lse, dq, k_sum, v_sum, None, None)
            for copy in beside(t):
                copy.start()

        @pl.when((t >= 1) & (t <= pairs))
        def _():
            pair = t - 1
            at = lanes_of(pair)
            for copy in beside(pair):
                copy.wait_recv()
            for j in (0, 1):
                near = sums[j][0 : 2 * r, at].astype(F32) + nears[j][:, at].astype(F32)
                sums[j][0 : 2 * r, at] = near.astype(BF)
            for copy in across(pair):
                copy.start()

        @pl.when(t >= 2)
        def _():
            pair = t - 2
            at = lanes_of(pair)
            for copy in across(pair):
                copy.wait_recv()
            for j in (0, 1):
                total = sums[j][0:r, at].astype(F32) + fars[j][:, at].astype(F32)
                outs[j][:, at] = total.astype(BF)

        return 0

    lax.fori_loop(0, pairs + 2, step, 0)
    for pair in range(pairs):
        for copy in across(pair) + beside(pair):
            copy.wait_send()


def local_call(kernel, out_shape, args, cost, count=None, scratch=(), barrier=None):
    vmem = pl.BlockSpec(memory_space=pltpu.VMEM)
    specs = [vmem] * len(args)
    if count is not None:
        specs, args = [pl.BlockSpec(memory_space=pltpu.SMEM)] + specs, [count] + args
    params = dict(vmem_limit_bytes=56 << 20)
    if barrier is not None:
        params.update(collective_id=barrier, has_side_effects=True)
    return pl.pallas_call(
        kernel,
        out_shape=[jax.ShapeDtypeStruct(s, t) for s, t in out_shape],
        in_specs=specs,
        out_specs=[vmem] * len(out_shape),
        scratch_shapes=list(scratch),
        cost_estimate=pl.CostEstimate(flops=cost, bytes_accessed=8 << 20, transcendentals=0),
        compiler_params=pltpu.CompilerParams(**params),
    )(*args)


def rows_cost(q, k):
    return 8 * q.shape[0] * k.shape[0] * D


def attend(q, k, v, count=None):
    shapes = [(q.shape, BF), ((HEADS, q.shape[0]), F32)]
    kernel = functools.partial(attend_kernel, count is not None)
    return local_call(kernel, shapes, [q, k, v], rows_cost(q, k), count)


def attend_sums(q, k, v, up, lse):
    return local_call(sums_kernel, [(lse.shape, F32)] * 2, [q, k, v, up, lse], rows_cost(q, k))


def attend_back(q, k, v, up, lse, count=None, inner=None, out=BF):
    shapes = [(q.shape, out), (k.shape, BF), (k.shape, BF)]
    kernel = functools.partial(back_kernel, count is not None, inner is not None)
    args = [q, k, v, up, lse] + ([] if inner is None else [inner])
    return local_call(kernel, shapes, args, 3 * rows_cost(q, k), count)


def clip_attend(q, k, v):
    r = k.shape[0]
    shapes = [(q.shape, BF), ((HEADS, r), F32), ((4 * r, D), BF), ((4 * r, D), BF)]
    sems = [pltpu.SemaphoreType.DMA((2, HEADS // 2))] * 4
    return local_call(clip_attend_kernel, shapes, [q, k, v], 4 * rows_cost(q, k), None, sems, 3)


def clip_attend_back(q, k_all, v_all, up, lse):
    r = q.shape[0]
    scratch = [pltpu.VMEM((4 * r, D), BF)] * 2 + [pltpu.VMEM((2 * r, D), BF)] * 2
    scratch += [pltpu.VMEM((r, D), BF)] * 2 + [pltpu.SemaphoreType.DMA((2, HEADS // 2))] * 4
    args = [q, k_all, v_all, up, lse]
    return local_call(clip_back_kernel, [(q.shape, BF)] * 3, args, 3 * rows_cost(q, k_all), None, scratch, 4)


def mlp_kernel(stream, gain, bias, expand, contract, normed, pre, hidden, out):
    @pl.when(pl.program_id(0) == 0)
    def _():
        normed[...] = norm(stream[...], gain[...], bias[...])
        out[...] = stream[...]

    before = tdot(normed[...], expand[0], 1, 0)
    pre[0] = before
    after = gelu(before).astype(BF)
    hidden[0] = after
    out[...] += tdot(after, contract[0], 1, 0)


def mlp_back_kernel(up, stream, gain, pre, expand, contract, out, d_low, d_pre, d_gain, d_bias, total):
    s = pl.program_id(0)

    @pl.when(s == 0)
    def _():
        d_low[...] = up[...].astype(BF)
        total[...] = jnp.zeros_like(total)

    d_hidden = low(tdot(d_low[...], contract[0], 1, 1))
    grad = (gelu_slope(pre[0]) * d_hidden).astype(BF)
    d_pre[0] = grad
    total[...] += tdot(grad, expand[0], 1, 1)

    @pl.when(s == pl.num_programs(0) - 1)
    def _():
        hat, inv = norm_parts(stream[...])
        g = total[...] * gain[...]
        mean = lambda v: jnp.mean(v, axis=-1, keepdims=True)
        out[...] = up[...] + inv * (g - mean(g) - hat * mean(g * hat))
        d_gain[...] = jnp.sum(total[...] * hat, axis=0, keepdims=True)
        d_bias[...] = jnp.sum(total[...], axis=0, keepdims=True)


def blocks(kernel, grid, ins, outs, args, cost, scratch=()):
    def spec(shape, cut):
        if cut:
            return pl.BlockSpec((1,) + shape[1:], lambda s: (s,) + (0,) * (len(shape) - 1))
        return pl.BlockSpec(shape, lambda s: (0,) * len(shape))

    return pl.pallas_call(
        kernel,
        grid=(grid,),
        out_shape=[jax.ShapeDtypeStruct(s, t) for s, t, _ in outs],
        in_specs=[spec(a.shape, cut) for a, cut in zip(args, ins)],
        out_specs=[spec(s, cut) for s, _, cut in outs],
        scratch_shapes=list(scratch),
        cost_estimate=pl.CostEstimate(flops=cost, bytes_accessed=16 << 20, transcendentals=0),
        compiler_params=pltpu.CompilerParams(vmem_limit_bytes=48 << 20),
    )(*args)


def mlp(stream, gain, bias, expand, contract):
    n, (r, _) = expand.shape[0], stream.shape
    outs = [((r, D), BF, False), ((n, r, D), F32, True), ((n, r, D), BF, True), ((r, D), F32, False)]
    args = [stream, gain[None], bias[None], expand, contract.reshape(n, D, D)]
    return blocks(mlp_kernel, n, [False] * 3 + [True] * 2, outs, args, 4 * n * r * D * D)


def mlp_backward(up, stream, gain, pre, expand, contract):
    n, (r, _) = expand.shape[0], stream.shape
    outs = [((r, D), F32, False), ((r, D), BF, False), ((n, r, D), BF, True)]
    outs += [((1, D), F32, False)] * 2
    args = [up, stream, gain[None], pre, expand, contract.reshape(n, D, D)]
    scratch = [pltpu.VMEM((r, D), F32)]
    return blocks(mlp_back_kernel, n, [False] * 3 + [True] * 3, outs, args, 4 * n * r * D * D, scratch)


SQUARE = (4, 5, 6, 7, 18, 19, 20, 21, 24, 25, 26, 27)
TALL = (11, 31)
BROAD = (10, 30)
VECTORS = tuple(i for i in range(32) if KINDS[i] == "v")


ROW_PAD = 400
CHUNK = 80
SMALL_ROWS = 96


def gather_split(i, rows):
    return rows // 2 if rows % 32 == 0 else 16 + 16 * (i % 2)


def stem_kernel(plan, inputs, outputs, rows_held, *refs):
    n = len(plan)
    ins, refs = refs[:inputs], refs[inputs:]
    patches, angles, table, refs = refs[:3], refs[3], refs[4], refs[5:]
    outs, refs = refs[:outputs], refs[outputs:]
    even_pre, odd_pre, even, odd, even_next, second, stream, normed, q, k_all, v_all, o, lse, vec = refs[:14]
    looked, refs = refs[14], refs[:14] + refs[15:]
    got, stage, refs = refs[14 : 14 + n], refs[14 + n : 14 + 2 * n], refs[14 + 2 * n :]
    small, weights, k_own, v_own, found, heard, strips = refs[:7]
    lsem, zsend, zrecv, xsend, xrecv, ysend, yrecv, csend, crecv, psend, precv = refs[7:18]
    wsem, kxs, kxr, kcs, kcr, tsend, trecv, usend, urecv = refs[18:]
    z, y, x, c = where_am_i()
    zs, yp, xp, cp = partners(z, y, x, c)
    greet(zs, yp, xp, cp)
    dst, src, swaps = [], [], []
    for i, (k, rows, out, tap, kind) in enumerate(plan):
        dst.append(outs[out] if tap is None else outs[out].at[tap])
        src.append(ins[k] if tap is None else ins[k].at[tap])
        swaps.append(None)
        if kind == "n":
            theirs = src[i].at[pl.ds(pl.multiple_of((1 - c) * rows, 16), rows), :]
            swaps[i] = remote(theirs, got[i], psend.at[i], precv.at[i], cp)
            swaps[i].start()

    def item(i):
        rows, wide = plan[i][1], plan[i][4] == "w"
        h = gather_split(i, rows)
        return rows, wide, slice(0, h), slice(h, rows)

    stages = {}

    def start(i, key, copies):
        for cpy in copies:
            cpy.start()
        stages[i, key] = copies

    def send_z(i):
        rows, wide, _, _ = item(i)
        block = src[i]
        if not wide:
            mine = src[i][pl.ds(pl.multiple_of(c * rows, 16), rows), :]
            swaps[i].wait_recv()
            theirs = got[i][...]
            stage[i][...] = jnp.concatenate(
                [jnp.where(c == 0, mine, theirs), jnp.where(c == 0, theirs, mine)], axis=1
            )
            block = stage[i]
        here = spot(dst[i], wide, z, y, x, c, slice(None))
        start(i, 0, [remote(block, here, zsend.at[i, j], zrecv.at[i, j], zs[j]) for j in range(3)])
        start(i, 4, [pltpu.make_async_copy(block, here, lsem.at[i])])

    def send_1(i):
        rows, wide, a, b = item(i)
        for cpy in stages[i, 0]:
            cpy.wait_recv()
        stages[i, 4][0].wait()
        ax = spot(dst[i], wide, None, y, x, c, a)
        by = spot(dst[i], wide, None, y, x, c, b)
        start(
            i,
            1,
            [
                remote(ax, ax, xsend.at[i, 0], xrecv.at[i, 0], xp),
                remote(by, by, ysend.at[i, 0], yrecv.at[i, 0], yp),
            ],
        )

    def send_2(i):
        rows, wide, a, b = item(i)
        for cpy in stages[i, 1]:
            cpy.wait_recv()
        ay = spot(dst[i], wide, None, y, None, c, a)
        bx = spot(dst[i], wide, None, None, x, c, b)
        start(
            i,
            2,
            [
                remote(ay, ay, ysend.at[i, 1], yrecv.at[i, 1], yp),
                remote(bx, bx, xsend.at[i, 1], xrecv.at[i, 1], xp),
            ],
        )

    def send_core(i):
        rows, wide, a, b = item(i)
        for cpy in stages[i, 2]:
            cpy.wait_recv()
        half = spot(dst[i], wide, None, None, None, c, slice(None))
        start(i, 3, [remote(half, half, csend.at[i], crecv.at[i], cp)])

    arrived = set()

    def arrive(i):
        if i not in arrived:
            stages[i, 3][0].wait_recv()
            arrived.add(i)

    r = q.shape[0]
    pairs = HEADS // 2

    def fetch(items, slots):
        copies = []
        for i, slot in zip(items, slots):
            arrive(i)
            copies.append(pltpu.make_async_copy(dst[i], weights.at[slot], wsem.at[slot]))
            copies[-1].start()
        for cpy in copies:
            cpy.wait()

    def weight(slot):
        return weights[slot].reshape(D, D)

    def open_small():
        arrive(0)
        copy = pltpu.make_async_copy(dst[0], small, wsem.at[3])
        copy.start()
        copy.wait()
        cells = []
        for zy in range(8):
            for s in range(4):
                cells.append(small[s // 2, s % 2, zy // 2, zy % 2, 64:80, 0:24].astype(F32))
        vec[...] = jnp.concatenate(cells, axis=1)

    def convolve(patch, pre, act, edge):
        def one(t, _):
            rows = pl.ds(pl.multiple_of(t * CHUNK, 16), CHUNK)
            left = patch[rows, :]
            cells = []
            for zy in range(8):
                taps = [small[s // 2, s % 2, zy // 2, zy % 2, 0:64, :] for s in range(4)]
                cells.append(tdot(left, jnp.concatenate(taps, axis=0), 1, 0)[:, 0:96])
            before = jnp.concatenate(cells, axis=1)
            if pre is not None:
                pre[rows, :] = before
            after = gelu(before)
            if edge is not None:
                row, outside = edge
                at = t * CHUNK + lax.broadcasted_iota(jnp.int32, after.shape, 0)
                after = jnp.where((at == row) & outside, 0.0, after)
            act[rows, :] = after.astype(BF)
            return 0

        lax.fori_loop(0, ROW_PAD // CHUNK, one, 0)

    me = 2 * x + c
    part = 128
    slots = looked.shape[0]
    eighth = slots // 8

    def other_clip(m):
        return lax.rem(z + m // 2, 4), lax.rem(y + m % 2, 2)

    def tell(m):
        zt, yt = other_clip(m)
        return remote(found.at[m], heard.at[m], tsend.at[m], trecv.at[m], (zt * 2 + yt, 2 * x + c))

    def look_up(m):
        zt, yt = other_clip(m)
        cells = []
        for s in range(4):
            for half in (0, 1):
                code = small[s // 2, s % 2, zt, yt, 0:64, 96:128].astype(F32)[0:eighth]
                cells.append(code[:, 2 * half : 2 * half + 1] * 256.0 + code[:, 2 * half + 1 : 2 * half + 2])
        first = (z * 2 + y) * rows_held
        place = jnp.concatenate(cells, axis=0).astype(jnp.int32) - first

        def one(k, total):
            lane = lax.broadcasted_iota(jnp.int32, (slots, 384), 1) + k * 384
            hot = jnp.where((lane == place) & (lane < rows_held), 1.0, 0.0).astype(BF)
            return total + tdot(hot, table[pl.ds(pl.multiple_of(k * 384, 384), 384), :], 1, 0)

        total = lax.fori_loop(0, table.shape[0] // 384, one, jnp.zeros((slots, D // 4), F32))
        if m == 0:
            heard[0] = total.astype(BF)
        else:
            found[m] = total.astype(BF)
            tell(m).start()

    def strip(over):
        if over == 0:
            return remote(strips.at[x, c], strips.at[x, c], usend.at[0], urecv.at[0], xp)
        return remote(strips.at[:, c], strips.at[:, c], usend.at[1], urecv.at[1], cp)

    def sum_found():
        total = heard[0].astype(F32)
        for m in range(1, 8):
            tell(m).wait_recv()
            total = total + heard[m].astype(F32)
        strips[x, c] = total.astype(BF)
        strip(0).start()

    def pass_strips():
        strip(0).wait_recv()
        strip(1).start()

    def join_strips():
        strip(1).wait_recv()
        looked[...] = jnp.concatenate([strips[s // 2, s % 2] for s in range(4)], axis=1)

    def convolve_second(t):
        rows = slice(t * part, (t + 1) * part)
        total = tdot(even[rows, :], weight(0), 1, 0)
        total = total + tdot(odd[rows, :], weight(1), 1, 0)
        total = total + tdot(even_next[rows, :], weight(2), 1, 0)
        second[rows, :] = total
        out = gelu(total) + angles[rows, :]
        stream[rows, :] = out
        normed[rows, :] = norm(out, vec[0:1, :], vec[1:2, :])

    def project():
        for t in range(r // part):
            rows = slice(t * part, (t + 1) * part)
            left = normed[rows, :]
            q[rows, :] = (tdot(left, weight(0), 1, 0) * SCALE).astype(BF)
            k_own[rows, :] = tdot(left, weight(1), 1, 0).astype(BF)
            v_own[rows, :] = tdot(left, weight(2), 1, 0).astype(BF)
        for pair in range(pairs):
            for cpy in across(pair):
                cpy.start()
        k_all[0:r, :] = k_own[...]
        v_all[0:r, :] = v_own[...]

    def across(pair):
        at = lanes_of(pair)
        return [
            remote(a.at[:, at], b.at[r : 2 * r, at], kxs.at[j, pair], kxr.at[j, pair], xp)
            for j, (a, b) in enumerate(((k_own, k_all), (v_own, v_all)))
        ]

    def beside(pair):
        at = lanes_of(pair)
        return [
            remote(a.at[0 : 2 * r, at], a.at[2 * r : 4 * r, at], kcs.at[j, pair], kcr.at[j, pair], cp)
            for j, a in enumerate((k_all, v_all))
        ]

    def pass_on(pair):
        for cpy in across(pair):
            cpy.wait_recv()
        for cpy in beside(pair):
            cpy.start()

    def attend_pair(pair):
        if pair + 1 < pairs:
            pass_on(pair + 1)
        for cpy in beside(pair):
            cpy.wait_recv()
        forward_pair(pair, q, k_all, v_all, o, lse, None)

    pieces = [
        open_small,
        lambda: convolve(patches[0], even_pre, even, (0, me == 0)),
        lambda: (look_up(0), look_up(1)),
        lambda: convolve(patches[1], odd_pre, odd, (r, me == 3)),
        lambda: (look_up(2), look_up(3)),
        lambda: convolve(patches[2], None, even_next, None),
        lambda: (look_up(4), look_up(5)),
        lambda: (fetch((1, 2, 3), (0, 1, 2)), convolve_second(0)),
    ]
    pieces += [functools.partial(convolve_second, t) for t in range(1, r // part)]
    pieces += [lambda: (fetch((4, 5, 6), (0, 1, 2)), project()), lambda: (look_up(6), look_up(7))]
    pieces += [lambda: (pass_on(0), sum_found()), lambda: (attend_pair(0), pass_strips())]
    pieces += [lambda: (attend_pair(1), join_strips())]
    pieces += [functools.partial(attend_pair, pair) for pair in range(2, pairs)]

    for t in range(n + AHEAD[2]):
        if t == 0:
            for i in range(min(n, AHEAD[3])):
                send_z(i)
        if t + AHEAD[3] < n:
            send_z(t + AHEAD[3])
        if 0 <= t - AHEAD[0] < n:
            send_1(t - AHEAD[0])
        if 0 <= t - AHEAD[1] < n:
            send_2(t - AHEAD[1])
        if 0 <= t - AHEAD[2] < n:
            send_core(t - AHEAD[2])
        if t >= PIECES_FROM and pieces:
            pieces.pop(0)()
    while pieces:
        pieces.pop(0)()
    for i in range(n):
        if swaps[i] is not None:
            swaps[i].wait_send()
        arrive(i)
        for key in range(4):
            for cpy in stages[i, key]:
                cpy.wait_send()
    for pair in range(pairs):
        for cpy in across(pair) + beside(pair):
            cpy.wait_send()
    for m in range(1, 8):
        tell(m).wait_send()
    strip(0).wait_send()
    strip(1).wait_send()


AHEAD = (0, 1, 3, 6)
PIECES_FROM = 5


def gather_and_stem(plan, ins, out_shapes, patches, angles, table, slots, rows_held):
    n, r = len(plan), angles.shape[0]
    sem = pltpu.SemaphoreType.DMA
    hbm, vmem = pl.BlockSpec(memory_space=pl.ANY), pl.BlockSpec(memory_space=pltpu.VMEM)
    got, stage = [], []
    for _, rows, _, _, kind in plan:
        got.append(pltpu.VMEM((rows, LANES // 2) if kind == "n" else (16, 128), BF))
        stage.append(pltpu.VMEM((rows, LANES) if kind == "n" else (16, 128), BF))
    sems = [sem((n,)), sem((n, 3)), sem((n, 3))] + [sem((n, 2))] * 4 + [sem((n,))] * 4
    made = [((ROW_PAD, D), F32)] * 2 + [((ROW_PAD, D), BF)] * 3 + [((r, D), F32)] * 2
    made += [((r, D), BF)] * 2 + [((4 * r, D), BF)] * 2 + [((r, D), BF), ((HEADS, r), F32), ((16, D), F32)]
    made += [((slots, D), BF)]
    held = [pltpu.VMEM((2, 2, 4, 2, SMALL_ROWS, 128), BF), pltpu.VMEM((3, 4, 2, 2, 48, D), BF)]
    held += [pltpu.VMEM((r, D), BF)] * 2 + [pltpu.VMEM((8, slots, D // 4), BF)] * 2
    held += [pltpu.VMEM((2, 2, slots, D // 4), BF)]
    return pl.pallas_call(
        functools.partial(stem_kernel, plan, len(ins), len(out_shapes), rows_held),
        out_shape=[jax.ShapeDtypeStruct(s, BF) for s in out_shapes]
        + [jax.ShapeDtypeStruct(s, t) for s, t in made],
        in_specs=[vmem] * (len(ins) + 5),
        out_specs=[hbm] * len(out_shapes) + [vmem] * len(made),
        scratch_shapes=got + stage + held + sems + [sem((4,))] + [sem((2, HEADS // 2))] * 4 + [sem((8,))] * 2 + [sem((2,))] * 2,
        compiler_params=pltpu.CompilerParams(
            collective_id=1, has_side_effects=True, vmem_limit_bytes=60 << 20
        ),
    )(*ins, *patches, angles, table)


def small_block(shards, ids):
    w = shards[0]
    t, i, o = w.shape
    halves = ids.reshape(2, -1)
    codes = jnp.stack([halves[0] // 256, halves[0] % 256, halves[1] // 256, halves[1] % 256], axis=1)
    codes = jnp.pad(codes.astype(BF), ((0, 64 - codes.shape[0]), (0, 32 - 4)))
    top = jnp.concatenate([jnp.pad(w.reshape(t * i, o), ((0, 64 - t * i), (0, 0))), codes], axis=1)
    rows = jnp.stack([shards[k] for k in VECTORS])
    rows = jnp.pad(rows, ((0, SMALL_ROWS - 64 - rows.shape[0]), (0, 128 - rows.shape[1])))
    return jnp.concatenate([top, rows])


def patch_rows(patch, mels):
    p = patch.reshape(patch.shape[0], 3, 4, mels // 4).transpose(0, 2, 1, 3).reshape(patch.shape[0], 4, -1)
    p = jnp.pad(p, ((0, ROW_PAD - p.shape[0]), (0, 0), (0, 64 - p.shape[2])))
    return p.reshape(ROW_PAD, 256)


def gather_weights(shards, patches, angles, ids, table):
    plan, ins, shapes, at = [], [], [], {}
    for i in SQUARE + (1,) + TALL + (15,):
        w = shards[i]
        if i == 15:
            w = jnp.concatenate([w, jnp.zeros((-w.shape[0] % 32, w.shape[1]), BF)])
        rows = w.shape[-2] // 2
        for tap in range(3) if w.ndim == 3 else (None,):
            at[i, tap] = len(plan)
            plan.append((len(ins), rows, len(shapes), None, "n"))
            ins.append(w if tap is None else w[tap])
            shapes.append((4, 2, 2, rows, D))
    for i in BROAD:
        at[i, None] = len(plan)
        plan.append((len(ins), shards[i].shape[0], len(shapes), None, "w"))
        ins.append(shards[i])
        shapes.append((2, 2, 4, 2) + shards[i].shape)
    at[0, None] = len(plan)
    plan.append((len(ins), SMALL_ROWS, len(shapes), None, "w"))
    ins.append(small_block(shards, ids))
    shapes.append((2, 2, 4, 2, SMALL_ROWS, 128))
    first = [at[0, None], at[1, 0], at[1, 1], at[1, 2], at[4, None], at[5, None], at[6, None]]
    order = first + [k for k in range(len(plan)) if k not in first]
    rows_held = table.shape[0]
    table = jnp.pad(table, ((0, -rows_held % 384), (0, 0)))
    outs = gather_and_stem([plan[k] for k in order], ins, shapes, patches, angles, table, 4 * ids.size, rows_held)
    outs, made = outs[: len(plan)], outs[len(plan) :]
    full = [None] * 32
    for i in SQUARE + TALL:
        full[i] = outs[at[i, None]].reshape(-1, D)
    full[1] = [outs[at[1, tap]].reshape(D, D) for tap in range(3)]
    r = shards[15].shape[0]
    full[15] = outs[at[15, None]].reshape(8, -1, D)[:, :r].reshape(8 * r, D)
    for i in BROAD:
        full[i] = outs[at[i, None]].reshape(4, D, D)
    t, a, b = shards[0].shape
    small = outs[at[0, None]]
    codes = small[..., : ids.size // 2, 96:100].astype(jnp.int32)
    all_ids = jnp.stack([codes[..., 2 * h] * 256 + codes[..., 2 * h + 1] for h in (0, 1)], axis=4)
    all_ids = all_ids.transpose(2, 3, 0, 1, 4, 5).reshape(-1)
    conv1 = small[..., : t * a, :b].reshape(2, 2, 4, 2, t, a, b)
    full[0] = conv1.transpose(4, 0, 1, 5, 2, 3, 6).reshape(t, 4 * a, 8 * b)
    for k, i in enumerate(VECTORS):
        full[i] = made[13][k]
    return full, made[:13], all_ids, made[14]


ORDER = (31, 30, 27, 24, 21, 18, 19, 20, 11, 10, 25, 26, 7, 4, 5, 6, 1)
EXACT = 25
HEAD_START = 1
MIX = 2


def reduce_grads(grads, shards):
    items, jobs, ins, shapes, seen = [], [], [], [], {}

    def place(v):
        if id(v) not in seen:
            seen[id(v)] = len(ins)
            ins.append(v)
        return seen[id(v)]

    for i in ORDER:
        left, right = grads[i]
        if i in TALL:
            jobs += [(len(items), s, place(left), place(right), left.shape[1]) for s in range(4)]
            items.append(("t", BF, len(shapes), None))
            shapes.append((2, 2, 2, RB, LANES // 2))
        elif i in BROAD:
            jobs += [(len(items), s, place(left), place(right), left.shape[0]) for s in range(4)]
            items.append(("w", BF, len(shapes), None))
            shapes.append((2, RB, D))
        elif i == 1:
            for tap, l in enumerate(left):
                jobs.append((len(items), 0, place(l), place(right), right.shape[0]))
                items.append(("n", BF, len(shapes), tap))
            shapes.append((3, 2, RB, LANES // 2))
        else:
            jobs.append((len(items), 0, place(left), place(right), left.shape[0]))
            items.append(("n", F32 if i == EXACT else BF, len(shapes), None))
            shapes.append((2, RB, LANES // 2))
    t, a, b = shards[0].shape
    conv1 = grads[0].reshape(t, 2, 2, a, 4, 2, b).transpose(1, 2, 4, 5, 0, 3, 6).reshape(2, 2, 4, 2, t * a, b)
    n = shards[VECTORS[0]].size
    vecs = jnp.stack([grads[i] for i in VECTORS]).reshape(-1, 4, 2, 2, 2, n).transpose(3, 4, 1, 2, 0, 5)
    none = ((0, 0),) * 4
    conv1 = jnp.pad(conv1.astype(BF), none + ((0, 64 - t * a), (0, 128 - b)))
    vecs = jnp.pad(vecs.astype(BF), none + ((0, SMALL_ROWS - 64 - len(VECTORS)), (0, 128 - n)))
    ins.append(jnp.concatenate([conv1, vecs], axis=4).reshape(2, 2, 4, 2, 2, RB, 128))
    items.append(("m", BF, len(shapes), None))
    shapes.append((2, RB, 128))
    small = [j for j in jobs if items[j[0]][0] == "n"]
    large = [j for j in jobs if items[j[0]][0] != "n"]
    jobs, large = small[:HEAD_START], list(large)
    for j in small[HEAD_START:]:
        jobs += large[:MIX] + [j]
        large = large[MIX:]
    jobs = jobs[:-1] + large + jobs[-1:]
    got = reduce_fast(items, jobs, ins, shapes)
    out = [None] * 32
    for i, v in zip(ORDER, got):
        out[i] = v.reshape(shards[i].shape)
    small = got[-1].reshape(SMALL_ROWS, 128)
    out[0] = small[: t * a, :b].reshape(t, a, b)
    for k, i in enumerate(VECTORS):
        out[i] = small[64 + k, :n]
    return out


def one_hot(ids, table):
    first = lax.axis_index("dp") * table.shape[0]
    return ((ids - first)[:, None] == jnp.arange(table.shape[0])[None, :]).astype(BF)


def body(mel_frames, token_ids, token_counts, *rest):
    shards, cotangent = list(rest[:32]), rest[32][0]
    table = shards[14]
    dps, seqs = lax.axis_size("dp"), lax.axis_size("seq")
    me = lax.axis_index("seq")
    slots = token_ids.shape[1]
    all_slots = slots * seqs
    frames = mel_frames.shape[1] // 2

    fast = dps == 8 and seqs == 4
    weights = shards[:14] + [None] + shards[15:]
    pairs = extended(mel_frames[0], 2).reshape(frames + 2, -1)
    mels = mel_frames.shape[2]
    n = frames + 1
    even_in = jnp.concatenate([pairs[:n], pairs[1:, :mels]], axis=1)
    odd_in = jnp.concatenate([pairs[:n, mels:], pairs[1:]], axis=1)
    angles = sinusoid(me * frames, frames)
    row = jnp.arange(n)[:, None]
    even_keep = (row > 0) | (me > 0)
    odd_keep = (row < n - 1) | (me < seqs - 1)
    if fast:
        patches = [patch_rows(p, mels) for p in (even_in, odd_in, even_in[1:])]
        full, made, ids, looked = gather_weights(weights, patches, angles, token_ids[0], table)
        even_pre, odd_pre, even0, odd0, even1, second_pre, stream0, enc_normed, q, k_all, v_all = made[:11]
        enc_mixed, enc_lse = made[11:]
    else:
        full = gather_plain(weights)
        conv1, conv2 = full[0].reshape(-1, D), full[1]
        even_pre, odd_pre = mm(even_in, conv1), mm(odd_in, conv1)
        even = jnp.where(even_keep, gelu(even_pre), 0.0).astype(BF)
        odd0 = jnp.where(odd_keep, gelu(odd_pre), 0.0).astype(BF)[:frames]
        even0, even1 = even[:frames], even[1:]
        second_pre = mm(even0, conv2[0]) + mm(odd0, conv2[1]) + mm(even1, conv2[2])
        stream0 = gelu(second_pre) + angles
        enc_normed = norm(stream0, full[2].astype(F32), full[3].astype(F32))
        q = (mm(enc_normed, full[4]) * SCALE).astype(BF)
        k, v = mm(enc_normed, full[5], BF), mm(enc_normed, full[6], BF)
        enc_mixed, enc_lse, k_all, v_all = clip_attend(q, k, v)
        ids = lax.all_gather(token_ids[0], BOTH, axis=0, tiled=True)
        looked = lax.psum_scatter(mm(one_hot(ids, table), table, BF), "dp", scatter_dimension=0, tiled=True)
        looked = lax.all_gather(looked, "seq", axis=0, tiled=True)
        looked = looked.reshape(seqs, all_slots, D // seqs).transpose(1, 0, 2).reshape(all_slots, D)
    vec = {i: full[i].astype(F32) for i in range(32) if KINDS[i] == "v"}
    conv1, conv2, position = full[0].reshape(-1, D), full[1], full[15]
    eo = full[7]
    ee, ec = full[10:12]
    dq_w, dk_w, dv_w, do_w = full[18:22]
    cq_w, ck_w, cv_w, co_w = full[24:28]
    de, dc = full[30:32]


    stream1 = stream0 + mm(enc_mixed, eo)
    enc_mlp_normed, enc_pre, enc_hidden, stream2 = mlp(stream1, vec[8], vec[9], ee, ec)
    memory = norm(stream2, vec[12], vec[13])
    mk = mm(memory, ck_w, BF)
    mv = mm(memory, cv_w, BF)

    place = jnp.arange(all_slots)
    embedded = looked.astype(F32) + position.astype(F32)
    dec_normed = norm(embedded, vec[16], vec[17])
    sq = (mm(dec_normed, dq_w) * SCALE).astype(BF)
    sk = mm(dec_normed, dk_w, BF)
    sv = mm(dec_normed, dv_w, BF)
    dec_mixed, dec_lse = attend(sq, sk, sv, token_counts)
    stream4 = embedded + mm(dec_mixed, do_w)
    cross_normed = norm(stream4, vec[22], vec[23])
    xq = (mm(cross_normed, cq_w) * SCALE).astype(BF)

    part, part_lse = attend(xq, mk, mv)
    parts, lses = unpack(exchange(pack(part, part_lse)))
    top = jnp.max(lses, axis=0)
    share = jnp.exp(lses - top)
    total = jnp.sum(share, axis=0)
    cross_lse = top + jnp.log(total)
    share = share / total
    cross_mixed = jnp.sum(
        parts.astype(F32).reshape(seqs, slots, HEADS, HEAD) * share[..., None], axis=0
    ).reshape(slots, D)
    cross_mixed = cross_mixed.astype(BF)

    own = lambda a: lax.dynamic_slice_in_dim(a, me * slots, slots, 0)
    stream4 = own(stream4)
    stream5 = stream4 + mm(cross_mixed, co_w)
    dec_mlp_normed, dec_pre, dec_hidden, stream6 = mlp(stream5, vec[28], vec[29], de, dc)
    live = (own(place) < token_counts[0])[:, None]
    decoded = jnp.where(live, stream6, 0.0).astype(BF)

    grads = [None] * 32

    def mlp_back(ex, co, gain, normed, pre, hidden, stream, up):
        up, d_low, d_pre, d_gain, d_bias = mlp_backward(up, stream, vec[gain], pre, full[ex], full[co])
        grads[co], grads[ex] = (hidden, d_low), (normed, d_pre)
        grads[gain], grads[gain + 1] = d_gain[0], d_bias[0]
        return up

    up = jnp.where(live, cotangent.astype(F32), 0.0)
    up = mlp_back(30, 31, 28, dec_mlp_normed, dec_pre, dec_hidden, stream5, up)
    d_low = up.astype(BF)
    grads[27] = (cross_mixed, d_low)
    d_mixed = mm_t(d_low, co_w, BF)
    d_mixed, lse_all = unpack(lax.all_gather(pack(d_mixed, cross_lse.T), "seq", axis=0, tiled=True))
    lse_all = lse_all.T
    sums = lax.psum(jnp.stack(attend_sums(xq, mk, mv, d_mixed, lse_all)), "seq")
    dxq, dmk, dmv = attend_back(xq, mk, mv, d_mixed, lse_all, inner=sums[1] / sums[0], out=F32)
    dxq = jnp.sum(exchange(dxq), axis=0)
    dxq = (low(dxq) * SCALE).astype(BF)
    grads[24] = (own(cross_normed), dxq)
    back, grads[22], grads[23] = norm_back(stream4, vec[22], mm_t(dxq, cq_w))
    up = up + back
    d_low = up.astype(BF)
    grads[21] = (own(dec_mixed), d_low)
    d_mixed = lax.all_gather(mm_t(d_low, do_w, BF), "seq", axis=0, tiled=True)
    dsq, dsk, dsv = attend_back(sq, sk, sv, d_mixed, dec_lse, token_counts)

    def inputs_back(first, gain, normed, stream, dq, dk, dv, up):
        dq = (dq.astype(F32) * SCALE).astype(BF)
        total = 0.0
        for i, g in enumerate((dq, dk, dv)):
            grads[first + i] = (normed, g)
            total = total + mm_t(g, full[first + i])
        back, grads[gain], grads[gain + 1] = norm_back(stream, vec[gain], total)
        return up + back

    up = inputs_back(18, 16, own(dec_normed), own(embedded), own(dsq), own(dsk), own(dsv), up)

    cols = exchange_columns(up.astype(BF))

    grads[25] = (memory, dmk)
    grads[26] = (memory, dmv)
    up, grads[12], grads[13] = norm_back(stream2, vec[12], mm_t(dmk, ck_w) + mm_t(dmv, cv_w))
    up = mlp_back(10, 11, 8, enc_mlp_normed, enc_pre, enc_hidden, stream1, up)
    d_low = up.astype(BF)
    grads[7] = (enc_mixed, d_low)
    d_mixed = mm_t(d_low, eo, BF)
    dq, dk, dv = clip_attend_back(q, k_all, v_all, d_mixed, enc_lse)
    up = inputs_back(4, 2, enc_normed, stream0, dq, dk, dv, up)

    d_second = (gelu_slope(second_pre) * up).astype(BF)
    grads[1] = ([even0, odd0, even1], d_second)
    rim = extended(d_second, 1)
    padded = even_pre.shape[0]
    rim = jnp.pad(rim, ((0, padded + 1 - rim.shape[0]), (0, 0)))
    row = jnp.arange(padded)[:, None]
    even_keep = ((row > 0) | (me > 0)) & (row < n)
    odd_keep = (row < n - 1) | ((me < seqs - 1) & (row < n))
    d_even = mm_t(rim[1:], conv2[0]) + mm_t(rim[:padded], conv2[2])
    d_odd = mm_t(rim[1:], conv2[1])
    d_even = jnp.where(even_keep, gelu_slope(even_pre) * low(d_even), 0.0).astype(BF)
    d_odd = jnp.where(odd_keep, gelu_slope(odd_pre) * low(d_odd), 0.0).astype(BF)
    grads[0] = (outer(odd_in[:frames], d_odd[:frames], F32) + outer(even_in[1:], d_even[1:n], F32)).reshape(
        3, mels, D
    )
    me_g, mo_g = mm_t(d_even, conv1), mm_t(d_odd, conv1)
    mel_grad = jnp.concatenate(
        [
            me_g[1:n, :mels] + me_g[: n - 1, 2 * mels :] + mo_g[: n - 1, mels : 2 * mels],
            me_g[1:n, mels : 2 * mels] + mo_g[1:n, :mels] + mo_g[: n - 1, 2 * mels :],
        ],
        axis=1,
    ).reshape(1, 2 * frames, mels)

    every = lax.all_gather(cols, "dp", axis=0, tiled=True)
    done = (reduce_grads if fast else reduce_plain)(grads, shards)
    done[14] = dot(one_hot(ids, table), every, 0, 0)
    per_clip = every.reshape(dps, dps, -1, D // seqs)
    done[15] = jnp.sum(
        lax.dynamic_index_in_dim(per_clip, lax.axis_index("dp"), 1, False).astype(F32), axis=0
    )
    return tuple([decoded[None], mel_grad] + done)


def exchange_columns(v):
    n = lax.axis_size("seq")
    wide = v.shape[1] // n
    v = v.reshape(v.shape[0], n, wide).transpose(1, 0, 2)
    return lax.all_to_all(v, "seq", split_axis=0, concat_axis=0, tiled=True).reshape(-1, wide)


def solution(mesh):
    place = {
        "1": P(None, "seq", "dp"),
        "2": P(None, "dp", "seq"),
        "v": P(BOTH),
        "m": P("dp", "seq"),
        "t": P("dp", "seq"),
    }
    rows = P("dp", "seq", None)
    weights = tuple(place[k] for k in KINDS)
    return jax.shard_map(
        body,
        mesh=mesh,
        in_specs=(rows, P("dp", "seq"), P("dp")) + weights + (rows,),
        out_specs=(rows, rows) + weights,
        check_vma=False,
    )
```

```python
import functools
import math

import jax
import jax.numpy as jnp
from jax import lax
from jax.experimental import pallas as pl
from jax.experimental.pallas import tpu as pltpu
from jax.sharding import PartitionSpec as P

D = 768
HEADS = 12
HEAD = 64
EPSILON = 1e-05
NEGATIVE = -1e30
SCALE = 1.0 / math.sqrt(HEAD)
BF = jnp.bfloat16
F32 = jnp.float32
BOTH = ("dp", "seq")

KINDS = "12vvmmmmvvmmvvtmvvmmmmvvmmmmvvmm"


def dot(a, b, ca, cb, out=F32):
    return lax.dot_general(a, b, (((ca,), (cb,)), ((), ())), preferred_element_type=F32).astype(out)


def mm(a, b, out=F32):
    return dot(a, b, 1, 0, out)


def mm_t(a, b, out=F32):
    return dot(a, b, 1, 1, out)


def outer(a, b, out=BF):
    return dot(a, b, 0, 0, out)


def norm_parts(values):
    center = values - jnp.mean(values, axis=-1, keepdims=True)
    spread = jnp.mean(center * center, axis=-1, keepdims=True)
    inv = lax.rsqrt(spread + EPSILON)
    return center * inv, inv


def norm(values, gain, bias):
    return (norm_parts(values)[0] * gain + bias).astype(BF)


def norm_back(values, gain, up):
    hat, inv = norm_parts(values)
    g = up * gain
    back = inv * (
        g - jnp.mean(g, axis=-1, keepdims=True) - hat * jnp.mean(g * hat, axis=-1, keepdims=True)
    )
    return back, jnp.sum(up * hat, axis=0), jnp.sum(up, axis=0)


def gelu(v):
    return v * (0.5 + 0.5 * lax.erf(v * math.sqrt(0.5)))


def gelu_slope(v):
    return (0.5 + 0.5 * lax.erf(v * math.sqrt(0.5))) + v * jnp.exp(-0.5 * v * v) * (
        1.0 / math.sqrt(2.0 * math.pi)
    )


def low(v):
    return lax.reduce_precision(v, 8, 7)


PAIR = 2 * HEAD


def tdot(a, b, ca, cb):
    return lax.dot_general(a, b, (((ca,), (cb,)), ((), ())), preferred_element_type=F32)


def one_head(rows, half):
    lane = lax.broadcasted_iota(jnp.int32, rows.shape, 1)
    return jnp.where((lane < HEAD) == (half == 0), rows, jnp.zeros_like(rows))


def masked(s, count_ref):
    if count_ref is None:
        return s
    key = lax.broadcasted_iota(jnp.int32, s.shape, 0)
    query = lax.broadcasted_iota(jnp.int32, s.shape, 1)
    return jnp.where((key <= query) & (key < count_ref[0]), s, NEGATIVE)


def pack(rows, log_sums):
    cols, rest = [rows], log_sums.T
    for _ in range(3):
        term = low(rest)
        cols.append(term.astype(BF))
        rest = rest - term
    wide = sum(c.shape[1] for c in cols)
    return jnp.concatenate(cols + [jnp.zeros((rows.shape[0], -wide % 128), BF)], axis=1)


def unpack(packed):
    terms = [packed[..., D + i * HEADS : D + (i + 1) * HEADS].astype(F32) for i in range(3)]
    return packed[..., :D], terms[0] + terms[1] + terms[2]


def shift(v, axis, step):
    n = lax.axis_size(axis)
    return lax.ppermute(v, axis, [(i, i + step) for i in range(n) if 0 <= i + step < n])


def extended(x, width):
    before = shift(x[-width:], "seq", 1)
    after = shift(x[:width], "seq", -1)
    return jnp.concatenate([before, x, after], axis=0)


def sinusoid(first_frame, frame_count):
    half = D // 2
    frequency = jnp.exp(jnp.arange(half).astype(F32) * (-math.log(10000.0) / (half - 1)))
    places = (first_frame + jnp.arange(frame_count)).astype(F32)
    angles = places[:, None] * frequency[None, :]
    return jnp.concatenate([jnp.sin(angles), jnp.cos(angles)], axis=1)


def to_whole(flat, shape, kind, dps, seqs):
    if kind == "v":
        return flat.reshape(-1)
    if kind == "1":
        t, i, o = shape
        return (
            flat.reshape(dps, seqs, t, i, o)
            .transpose(2, 1, 3, 0, 4)
            .reshape(t, seqs * i, dps * o)
        )
    if kind == "2":
        t, i, o = shape
        return (
            flat.reshape(dps, seqs, t, i, o)
            .transpose(2, 0, 3, 1, 4)
            .reshape(t, dps * i, seqs * o)
        )
    r, c = shape
    return flat.reshape(dps, seqs, r, c).transpose(0, 2, 1, 3).reshape(dps * r, seqs * c)


def to_owner(g, kind, dps, seqs):
    n = dps * seqs
    if kind == "v":
        return g.reshape(n, -1)
    if kind == "1":
        t, i, o = g.shape
        g = g.reshape(t, seqs, i // seqs, dps, o // dps).transpose(3, 1, 0, 2, 4)
    elif kind == "2":
        t, i, o = g.shape
        g = g.reshape(t, dps, i // dps, seqs, o // seqs).transpose(1, 3, 0, 2, 4)
    else:
        r, c = g.shape
        g = g.reshape(dps, r // dps, seqs, c // seqs).transpose(0, 2, 1, 3)
    return g.reshape(n, -1)


def gather_plain(shards):
    dps, seqs = lax.axis_size("dp"), lax.axis_size("seq")
    flat = jnp.concatenate([w.reshape(-1) for w in shards if w is not None])
    got = lax.all_gather(flat[None], BOTH, axis=0, tiled=True)
    out, at = [], 0
    for w, kind in zip(shards, KINDS):
        if w is None:
            out.append(None)
            continue
        out.append(to_whole(got[:, at : at + w.size], w.shape, kind, dps, seqs))
        at += w.size
    for i in BROAD:
        out[i] = out[i].reshape(D, seqs, -1).transpose(1, 0, 2)
    return out


def product(factors):
    left, right = factors
    if right.ndim == 3:
        return jnp.concatenate([outer(left, r) for r in right], axis=1)
    if isinstance(left, list) or left.ndim == 3:
        return jnp.stack([outer(l, right) for l in left])
    return outer(left, right)


def reduce_plain(grads, shards):
    dps, seqs = lax.axis_size("dp"), lax.axis_size("seq")
    grads = [product(g) if isinstance(g, tuple) else g for g in grads]
    for i in TALL:
        grads[i] = grads[i].reshape(-1, D)
    flat = jnp.concatenate(
        [to_owner(g.astype(BF), k, dps, seqs) for g, k in zip(grads, KINDS) if g is not None], axis=1
    )
    own = lax.psum_scatter(flat, BOTH, scatter_dimension=0, tiled=True).astype(F32)[0]
    out, at = [], 0
    for w, g in zip(shards, grads):
        if g is None:
            out.append(None)
            continue
        out.append(own[at : at + w.size].reshape(w.shape))
        at += w.size
    return out


MESH = pl.DeviceIdType.MESH
LANES = 384


def where_am_i():
    d, s = lax.axis_index("dp"), lax.axis_index("seq")
    return d // 2, d % 2, s // 2, s % 2


def partners(z, y, x, c):
    at = lambda z, y, x, c: (z * 2 + y, x * 2 + c)
    zs = [at((z + j) % 4, y, x, c) for j in (1, 2, 3)]
    return zs, at(z, 1 - y, x, c), at(z, y, 1 - x, c), at(z, y, x, 1 - c)


def greet(zs, yp, xp, cp):
    barrier = pltpu.get_barrier_semaphore()
    everyone = zs + [yp, xp, cp]
    for dev in everyone:
        pl.semaphore_signal(barrier, inc=1, device_id=dev, device_id_type=MESH)
    pl.semaphore_wait(barrier, len(everyone))


def remote(src, dst, send, recv, dev):
    return pltpu.make_async_remote_copy(
        src_ref=src, dst_ref=dst, send_sem=send, recv_sem=recv, device_id=dev, device_id_type=MESH
    )


def split_at(i, rows):
    return rows // 2 if rows % 32 == 0 else 16 + 16 * (i % 2)


def lanes(x):
    return pl.ds(pl.multiple_of(x * LANES, LANES), LANES)


def spot(ref, wide, zs, ys, xs, c, rs):
    full = lambda v: slice(None) if v is None else v
    if wide:
        return ref.at[full(xs), c, full(zs), full(ys), rs, :]
    return ref.at[full(zs), full(ys), c, rs, slice(None) if xs is None else lanes(xs)]


def add_into(dst, *srcs):
    lead = srcs[0].shape[:-2]
    total = math.prod(lead)

    def one(k, _):
        at = []
        for size in reversed(lead):
            at.append(lax.rem(k, size))
            k = lax.div(k, size)
        at = tuple(reversed(at))
        acc = srcs[0][at].astype(F32)
        for s in srcs[1:]:
            acc = acc + s[at].astype(F32)
        dst[at] = acc.astype(dst.dtype)
        return 0

    lax.fori_loop(0, total, one, 0)


RB = 48


def item_shapes(kind, h):
    if kind == "n":
        g = RB - h
        return [
            (4, 2, RB, D),
            (4, h, D),
            (4, 2, g, LANES),
            (4, h, LANES),
            (4, g, LANES),
            (4, RB, LANES),
            (3, RB, LANES),
        ]
    if kind == "t":
        return [
            (4, 4, 2, RB, D),
            (4, 2, RB, D),
            (4, 4, RB, LANES),
            (4, 2, RB, LANES),
            (4, 2, RB, LANES),
            (4, 2, 2, RB, LANES),
            (3, 2, 2, RB, LANES),
        ]
    w = D if kind == "w" else 128
    return [
        (2, 4, 2, 2, RB, w),
        (2, 4, RB, w),
        (4, 2, RB, w),
        (4, RB, w),
        (4, RB, w),
        (4, 2, RB, w),
        (3, 2, RB, w),
    ]


def halves_of(k):
    return 16 + 16 * (k % 2)


def reduce_kernel(items, jobs, inputs, outputs, *refs):
    n = len(items)
    take = lambda count: (refs[:count], refs[count:])
    ins, refs = take(inputs)
    outs, refs = take(outputs)
    rc, refs = take(n)
    r1a, refs = take(n)
    r1b, refs = take(n)
    r2a, refs = take(n)
    r2b, refs = take(n)
    s3, refs = take(n)
    rz, refs = take(n)
    sbuf, refs = take(n)
    ring, wide_ring, given, xbuf, ybuf = refs[:5]
    loads, csend, crecv, xsend, xrecv, ysend, yrecv, zsend, zrecv, fsend, frecv = refs[5:]
    z, y, x, c = where_am_i()
    zs, yp, xp, cp = partners(z, y, x, c)
    greet(zs, yp, xp, cp)
    started = []

    def start(copy):
        copy.start()
        started.append(copy)
        return copy

    cores, ones, twos, threes, loaded = {}, {}, {}, {}, {}
    half = lambda i: halves_of(i)
    at = {(j[0], j[1]): t for t, j in enumerate(jobs)}

    def load(t):
        _, part, xi, yi, rows = jobs[t]
        xsrc, ysrc = ins[xi], ins[yi]
        if len(xsrc.shape) == 3:
            xsrc = xsrc.at[part]
        elif xsrc.shape[0] > rows:
            xsrc = xsrc.at[0:rows]
        if len(ysrc.shape) == 3:
            ysrc = ysrc.at[2 * (part // 2) + (c if part % 2 else 1 - c)]
        pair = []
        for k, (src, buf) in enumerate(((xsrc, xbuf), (ysrc, ybuf))):
            copy = pltpu.make_async_copy(src, buf.at[t % 2, 0:rows], loads.at[t % 2, k])
            copy.start()
            pair.append(copy)
        loaded[t] = pair

    def room(t):
        return wide_ring if items[jobs[t][0]][1] == F32 else ring.at[t % RING]

    def compute(t):
        i, part, _, _, rows = jobs[t]
        if t >= RING and t - RING in cores and items[jobs[t - RING][0]][1] == BF:
            cores[t - RING].wait_send()
        for copy in loaded[t]:
            copy.wait()
        room_t = room(t)
        left = xbuf[t % 2, 0:rows, :]

        def column(k, _):
            cols = pl.ds(pl.multiple_of(k * 256, 256), 256)
            product = tdot(left, ybuf[t % 2, 0:rows, cols], 0, 0)
            room_t[:, :, :, :, cols] = product.reshape(4, 2, 2, RB, 256).astype(room_t.dtype)
            return 0

        lax.fori_loop(0, D // 256, column, 0)
        if t + 2 < len(jobs):
            load(t + 2)
        kind = items[i][0]
        if kind == "n":
            cores[t] = remote(room_t.at[:, :, 1 - c], rc[i], csend.at[t], crecv.at[t], cp)
        elif kind == "t":
            cores[t] = remote(room_t.at[:, :, 1 - c], rc[i].at[part], csend.at[t], crecv.at[t], cp)
        elif part % 2 == 0:
            cores[t] = remote(room_t, rc[i].at[part // 2], csend.at[t], crecv.at[t], cp)
        if t in cores:
            cores[t].start()

    def add_own(t):
        i, part, _, _, _ = jobs[t]
        kind, mine = items[i][0], room(t)
        if kind == "w":
            if part % 2 == 0:
                return False
            cores[at[i, part - 1]].wait_recv()
            add_into(rc[i].at[part // 2], mine, rc[i].at[part // 2])
            return part == 3
        cores[t].wait_recv()
        dst = rc[i] if kind == "n" else rc[i].at[part]
        add_into(dst, mine.at[:, :, c], dst)
        return kind == "n" or part == 3

    def views(i):
        kind, h = items[i][0], half(i)
        r, a, b = rc[i], r1a[i], r1b[i]
        here, there = lanes(x), lanes(1 - x)
        if kind == "n":
            one = (r.at[:, 1 - y, 0:h, :], r.at[:, :, h:RB, there], r.at[:, y, 0:h, :], r.at[:, :, h:RB, here])
            two = (a.at[:, :, there], b.at[:, 1 - y], a.at[:, :, here], b.at[:, y])
            parts = (s3[i].at[:, 0:h, :], s3[i].at[:, h:RB, :])
        elif kind == "t":
            up, down = pl.ds(2 * y, 2), pl.ds(2 * (1 - y), 2)
            one = (r.at[:, down, 0], r.at[:, :, 1, :, there], r.at[:, up, 0], r.at[:, :, 1, :, here])
            two = (a.at[:, :, :, there], b.at[:, down], a.at[:, :, :, here], b.at[:, up])
            parts = (s3[i].at[:, 0], s3[i].at[:, 1])
        else:
            one = (r.at[:, :, 1 - y, 0], r.at[1 - x, :, :, 1], r.at[:, :, y, 0], r.at[x, :, :, 1])
            two = (a.at[1 - x], b.at[:, 1 - y], a.at[x], b.at[:, y])
            parts = (s3[i].at[:, 0], s3[i].at[:, 1])
        return one, two, parts

    def send_1(i):
        (over_y, over_x, _, _), _, _ = views(i)
        ones[i] = [
            start(remote(over_y, r1a[i], ysend.at[i, 0], yrecv.at[i, 0], yp)),
            start(remote(over_x, r1b[i], xsend.at[i, 0], xrecv.at[i, 0], xp)),
        ]

    def send_2(i):
        (_, _, stay_a, stay_b), (over_x, over_y, _, _), _ = views(i)
        ones[i][0].wait_recv()
        add_into(r1a[i], stay_a, r1a[i])
        first = start(remote(over_x, r2a[i], xsend.at[i, 1], xrecv.at[i, 1], xp))
        ones[i][1].wait_recv()
        add_into(r1b[i], stay_b, r1b[i])
        twos[i] = [first, start(remote(over_y, r2b[i], ysend.at[i, 1], yrecv.at[i, 1], yp))]

    def send_z(i):
        _, (_, _, stay_a, stay_b), (part_a, part_b) = views(i)
        twos[i][0].wait_recv()
        add_into(part_a, stay_a, r2a[i])
        twos[i][1].wait_recv()
        add_into(part_b, stay_b, r2b[i])
        threes[i] = [
            start(remote(s3[i].at[(z + j + 1) % 4], rz[i].at[j], zsend.at[i, j], zrecv.at[i, j], zs[j]))
            for j in range(3)
        ]

    finals = []

    def finish(i):
        kind, _, out, tap = items[i]
        for copy in threes[i]:
            copy.wait_recv()
        acc = s3[i][z].astype(F32)
        for j in range(3):
            acc = acc + rz[i][j].astype(F32)
        dst = outs[out] if tap is None else outs[out].at[tap]
        if kind in "wm":
            dst[...] = acc
            return
        mine = acc[..., : LANES // 2]
        theirs = acc[..., LANES // 2 :]
        keep = jnp.where(c == 0, mine, theirs)
        other = jnp.where(c == 0, theirs, mine)
        if kind == "n":
            sbuf[i][...] = other
            dst[c] = keep
            finals.append(start(remote(sbuf[i], dst.at[c], fsend.at[i], frecv.at[i], cp)))
            return
        for a in (0, 1):
            for b in (0, 1):
                dst[b, a, c] = keep[a, b]
                sbuf[i][b, a] = other[a, b]
        finals.append(start(remote(sbuf[i], dst.at[:, :, c], fsend.at[i], frecv.at[i], cp)))

    g = [i for i in range(n) if items[i][0] == "m"][0]
    last = len(jobs)
    theirs = start(remote(ins[-1].at[:, 1 - c], rc[g], csend.at[last], crecv.at[last], cp))
    mine = pltpu.make_async_copy(ins[-1].at[:, c], given, loads.at[0, 2])
    mine.start()
    load(0)
    load(1)
    queue = [[], [], []]
    steps = (send_2, send_z, finish)

    def advance(keep):
        for k in (2, 1, 0):
            while len(queue[k]) > keep:
                i = queue[k].pop(0)
                steps[k](i)
                if k < 2:
                    queue[k + 1].append(i)

    mine.wait()
    for t in range(last + 1):
        if t < last:
            compute(t)
        if t == 1:
            theirs.wait_recv()
            add_into(rc[g], given, rc[g])
            send_1(g)
            queue[0].append(g)
        if t >= 1 and add_own(t - 1):
            i = jobs[t - 1][0]
            send_1(i)
            queue[0].append(i)
        advance(LAG)
    for keep in range(LAG - 1, -1, -1):
        advance(keep)
    while queue[0] or queue[1] or queue[2]:
        advance(0)
    for copy in finals:
        copy.wait_recv()
    for copy in started:
        copy.wait_send()
    for t in cores:
        if t + RING >= last or items[jobs[t][0]][1] == F32:
            cores[t].wait_send()


RING = 3
LAG = 1


def reduce_fast(items, jobs, ins, out_shapes):
    n, m = len(items), len(jobs)
    sem = pltpu.SemaphoreType.DMA
    groups = [[] for _ in range(8)]
    for i, (kind, dtype, _, _) in enumerate(items):
        for group, shape in zip(groups, item_shapes(kind, halves_of(i))):
            group.append(pltpu.VMEM(shape, dtype))
        last = {"n": (RB, LANES // 2), "t": (2, 2, RB, LANES // 2)}.get(kind, (8, 128))
        groups[7].append(pltpu.VMEM(last, F32))
    scratch = [s for group in groups for s in group]
    scratch += [
        pltpu.VMEM((RING, 4, 2, 2, RB, D), BF),
        pltpu.VMEM((4, 2, 2, RB, D), F32),
        pltpu.VMEM((2, 4, 2, 2, RB, 128), BF),
    ]
    most = max(j[4] for j in jobs)
    scratch += [pltpu.VMEM((2, most, D), BF)] * 2
    scratch += [sem((2, 3)), sem((m + 1,)), sem((m + 1,))]
    scratch += [sem((n, 2))] * 4 + [sem((n, 3))] * 2 + [sem((n,))] * 2
    vmem = pl.BlockSpec(memory_space=pltpu.VMEM)
    return pl.pallas_call(
        functools.partial(reduce_kernel, items, jobs, len(ins), len(out_shapes)),
        out_shape=[jax.ShapeDtypeStruct(s, F32) for s in out_shapes],
        in_specs=[pl.BlockSpec(memory_space=pl.ANY)] * len(ins),
        out_specs=[vmem] * len(out_shapes),
        scratch_shapes=scratch,
        compiler_params=pltpu.CompilerParams(
            collective_id=2, has_side_effects=True, vmem_limit_bytes=62 << 20
        ),
    )(*ins)


def lanes_of(pair):
    return pl.ds(pl.multiple_of(pair * PAIR, PAIR), PAIR)


def clip_partners():
    d, s = lax.axis_index("dp"), lax.axis_index("seq")
    x, c = s // 2, s % 2
    return (d, (1 - x) * 2 + c), (d, x * 2 + 1 - c)


def greet_pair(xp, cp):
    barrier = pltpu.get_barrier_semaphore()
    for dev in (xp, cp):
        pl.semaphore_signal(barrier, inc=1, device_id=dev, device_id_type=MESH)
    pl.semaphore_wait(barrier, 2)


def forward_head(q_one, k_slab, v_slab, half, count):
    s = masked(tdot(k_slab, q_one, 1, 1), count)
    top = jnp.max(s, axis=0, keepdims=True)
    e = jnp.exp(s - top)
    total = jnp.sum(e, axis=0, keepdims=True)
    mixed = tdot(v_slab, e.astype(BF), 0, 0)[half * HEAD : (half + 1) * HEAD]
    return mixed / total, top + jnp.log(total)


def forward_pair(pair, q, k, v, o, lse, count):
    at = lanes_of(pair)
    q_slab, k_slab, v_slab = q[:, at], k[:, at], v[:, at]
    both = []
    for half in (0, 1):
        mixed, log_sum = forward_head(one_head(q_slab, half), k_slab, v_slab, half, count)
        both.append(mixed)
        lse[pl.ds(2 * pair + half, 1), :] = log_sum
    o[:, at] = jnp.concatenate(both, axis=0).T.astype(o.dtype)


def backward_pair(pair, q, k, v, up, lse, dq, dk, dv, count, known):
    at = lanes_of(pair)
    q_slab, k_slab, v_slab, u_slab = q[:, at], k[:, at], v[:, at], up[:, at]
    both, dk_sum, dv_sum = [], 0.0, 0.0
    for half in (0, 1):
        row = pl.ds(2 * pair + half, 1)
        q_one, u_one = one_head(q_slab, half), one_head(u_slab, half)
        p = jnp.exp(masked(tdot(k_slab, q_one, 1, 1), count) - lse[row, :])
        dp = tdot(v_slab, u_one, 1, 1)
        if known is None:
            mass = jnp.sum(p, axis=0, keepdims=True)
            inner = jnp.sum(p * dp, axis=0, keepdims=True) / mass
        else:
            inner = known[row, :]
        ds = (p * (dp - inner)).astype(BF)
        dv_sum = dv_sum + tdot(p.astype(BF), u_one, 1, 0)
        dk_sum = dk_sum + tdot(ds, q_one, 1, 0)
        both.append(tdot(k_slab, ds, 0, 0)[half * HEAD : (half + 1) * HEAD])
    dq[:, at] = jnp.concatenate(both, axis=0).T.astype(dq.dtype)
    dk[:, at] = dk_sum.astype(dk.dtype)
    dv[:, at] = dv_sum.astype(dv.dtype)


def attend_kernel(causal, *refs):
    count = refs[0] if causal else None
    q, k, v, o, lse = refs[1:] if causal else refs

    def step(pair, _):
        forward_pair(pair, q, k, v, o, lse, count)
        return 0

    lax.fori_loop(0, HEADS // 2, step, 0)


def back_kernel(causal, given, *refs):
    count, known = None, None
    if causal:
        count, refs = refs[0], refs[1:]
    q, k, v, up, lse = refs[:5]
    refs = refs[5:]
    if given:
        known, refs = refs[0], refs[1:]
    dq, dk, dv = refs

    def step(pair, _):
        backward_pair(pair, q, k, v, up, lse, dq, dk, dv, count, known)
        return 0

    lax.fori_loop(0, HEADS // 2, step, 0)


def clip_attend_kernel(q, k, v, o, lse, k_all, v_all, xsend, xrecv, csend, crecv):
    xp, cp = clip_partners()
    r = q.shape[0]
    greet_pair(xp, cp)
    pairs = HEADS // 2

    def across(pair):
        at = lanes_of(pair)
        return [
            remote(src.at[:, at], dst.at[r : 2 * r, at], xsend.at[j, pair], xrecv.at[j, pair], xp)
            for j, (src, dst) in enumerate(((k, k_all), (v, v_all)))
        ]

    def beside(pair):
        at = lanes_of(pair)
        return [
            remote(a.at[0 : 2 * r, at], a.at[2 * r : 4 * r, at], csend.at[j, pair], crecv.at[j, pair], cp)
            for j, a in enumerate((k_all, v_all))
        ]

    for pair in range(pairs):
        for copy in across(pair):
            copy.start()
    k_all[0:r, :] = k[...]
    v_all[0:r, :] = v[...]

    def pass_on(pair):
        for copy in across(pair):
            copy.wait_recv()
        for copy in beside(pair):
            copy.start()

    pass_on(0)

    def step(pair, _):
        @pl.when(pair + 1 < pairs)
        def _():
            pass_on(pair + 1)

        for copy in beside(pair):
            copy.wait_recv()
        forward_pair(pair, q, k_all, v_all, o, lse, None)
        return 0

    lax.fori_loop(0, pairs, step, 0)
    for pair in range(pairs):
        for copy in across(pair) + beside(pair):
            copy.wait_send()


def clip_back_kernel(q, k, v, up, lse, dq, dk, dv, *refs):
    k_sum, v_sum, k_near, v_near, k_far, v_far, xsend, xrecv, csend, crecv = refs
    xp, cp = clip_partners()
    r = q.shape[0]
    greet_pair(xp, cp)
    pairs = HEADS // 2
    sums, nears, fars, outs = (k_sum, v_sum), (k_near, v_near), (k_far, v_far), (dk, dv)

    def beside(pair):
        at = lanes_of(pair)
        return [
            remote(sums[j].at[2 * r : 4 * r, at], nears[j].at[:, at], csend.at[j, pair], crecv.at[j, pair], cp)
            for j in (0, 1)
        ]

    def across(pair):
        at = lanes_of(pair)
        return [
            remote(sums[j].at[r : 2 * r, at], fars[j].at[:, at], xsend.at[j, pair], xrecv.at[j, pair], xp)
            for j in (0, 1)
        ]

    def step(t, _):
        @pl.when(t < pairs)
        def _():
            backward_pair(t, q, k, v, up, lse, dq, k_sum, v_sum, None, None)
            for copy in beside(t):
                copy.start()

        @pl.when((t >= 1) & (t <= pairs))
        def _():
            pair = t - 1
            at = lanes_of(pair)
            for copy in beside(pair):
                copy.wait_recv()
            for j in (0, 1):
                near = sums[j][0 : 2 * r, at].astype(F32) + nears[j][:, at].astype(F32)
                sums[j][0 : 2 * r, at] = near.astype(BF)
            for copy in across(pair):
                copy.start()

        @pl.when(t >= 2)
        def _():
            pair = t - 2
            at = lanes_of(pair)
            for copy in across(pair):
                copy.wait_recv()
            for j in (0, 1):
                total = sums[j][0:r, at].astype(F32) + fars[j][:, at].astype(F32)
                outs[j][:, at] = total.astype(BF)

        return 0

    lax.fori_loop(0, pairs + 2, step, 0)
    for pair in range(pairs):
        for copy in across(pair) + beside(pair):
            copy.wait_send()


def clip_peers():
    d, s = lax.axis_index("dp"), lax.axis_index("seq")
    return [(d, lax.rem(s + j, 4)) for j in (1, 2, 3)], s


def greet_peers(peers):
    barrier = pltpu.get_barrier_semaphore()
    for dev in peers:
        pl.semaphore_signal(barrier, inc=1, device_id=dev, device_id_type=MESH)
    pl.semaphore_wait(barrier, 3)


def cross_kernel(q, k, v, parts, lses, o, osend, orecv, lsend, lrecv):
    peers, me = clip_peers()
    greet_peers(peers)
    r = parts.shape[1]
    pairs = HEADS // 2
    rows = lambda s: pl.ds(pl.multiple_of(s * r, 16), r)

    def tell(j, pair):
        at = lanes_of(pair)
        return remote(
            o.at[rows(peers[j][1]), at], parts.at[j + 1, :, at], osend.at[j, pair], orecv.at[j, pair], peers[j]
        )

    def step(pair, _):
        forward_pair(pair, q, k, v, o, lses.at[0], None)
        for j in range(3):
            tell(j, pair).start()
        return 0

    lax.fori_loop(0, pairs, step, 0)
    sums = [remote(lses.at[0], lses.at[j + 1], lsend.at[j], lrecv.at[j], peers[j]) for j in range(3)]
    for copy in sums:
        copy.start()
    parts[0] = o[rows(me), :]
    for copy in sums + [tell(j, pair) for j in range(3) for pair in range(pairs)]:
        copy.wait_recv()
    for copy in sums + [tell(j, pair) for j in range(3) for pair in range(pairs)]:
        copy.wait_send()


def cross_back_kernel(q, k, v, up, lse, dq, dk, dv, sums, known, mine, theirs, ssend, srecv, dsend, drecv):
    peers, me = clip_peers()
    greet_peers(peers)
    r = dq.shape[0]
    pairs = HEADS // 2
    rows = lambda s: pl.ds(pl.multiple_of(s * r, 16), r)

    def first(pair, _):
        at = lanes_of(pair)
        q_slab, k_slab, v_slab, u_slab = q[:, at], k[:, at], v[:, at], up[:, at]
        for half in (0, 1):
            row = 2 * pair + half
            p = jnp.exp(tdot(k_slab, one_head(q_slab, half), 1, 1) - lse[pl.ds(row, 1), :])
            dp = tdot(v_slab, one_head(u_slab, half), 1, 1)
            sums[0, pl.ds(row, 1), :] = jnp.sum(p, axis=0, keepdims=True)
            sums[0, pl.ds(16 + row, 1), :] = jnp.sum(p * dp, axis=0, keepdims=True)
        return 0

    sums[0] = jnp.zeros(sums.shape[1:], F32)
    lax.fori_loop(0, pairs, first, 0)
    shared = [remote(sums.at[0], sums.at[j + 1], ssend.at[j], srecv.at[j], peers[j]) for j in range(3)]
    for copy in shared:
        copy.start()
    for copy in shared:
        copy.wait_recv()
    total = sums[0] + sums[1] + sums[2] + sums[3]
    known[...] = total[16 : 16 + HEADS] / total[0:HEADS]

    def tell(j, pair):
        at = lanes_of(pair)
        return remote(
            mine.at[rows(peers[j][1]), at], theirs.at[j, :, at], dsend.at[j, pair], drecv.at[j, pair], peers[j]
        )

    def second(pair, _):
        backward_pair(pair, q, k, v, up, lse, mine, dk, dv, None, known)
        for j in range(3):
            tell(j, pair).start()
        return 0

    lax.fori_loop(0, pairs, second, 0)
    for j in range(3):
        for pair in range(pairs):
            tell(j, pair).wait_recv()
    dq[...] = mine[rows(me), :] + theirs[0] + theirs[1] + theirs[2]
    for copy in shared + [tell(j, pair) for j in range(3) for pair in range(pairs)]:
        copy.wait_send()


def local_call(kernel, out_shape, args, cost, count=None, scratch=(), barrier=None):
    vmem = pl.BlockSpec(memory_space=pltpu.VMEM)
    specs = [vmem] * len(args)
    if count is not None:
        specs, args = [pl.BlockSpec(memory_space=pltpu.SMEM)] + specs, [count] + args
    params = dict(vmem_limit_bytes=56 << 20)
    if barrier is not None:
        params.update(collective_id=barrier, has_side_effects=True)
    return pl.pallas_call(
        kernel,
        out_shape=[jax.ShapeDtypeStruct(s, t) for s, t in out_shape],
        in_specs=specs,
        out_specs=[vmem] * len(out_shape),
        scratch_shapes=list(scratch),
        cost_estimate=pl.CostEstimate(flops=cost, bytes_accessed=8 << 20, transcendentals=0),
        compiler_params=pltpu.CompilerParams(**params),
    )(*args)


def rows_cost(q, k):
    return 8 * q.shape[0] * k.shape[0] * D


def attend(q, k, v, count=None):
    shapes = [(q.shape, BF), ((HEADS, q.shape[0]), F32)]
    kernel = functools.partial(attend_kernel, count is not None)
    return local_call(kernel, shapes, [q, k, v], rows_cost(q, k), count)


def cross_attend(q, k, v):
    r = q.shape[0] // 4
    sem = pltpu.SemaphoreType.DMA
    scratch = [pltpu.VMEM(q.shape, BF)] + [sem((3, HEADS // 2))] * 2 + [sem((3,))] * 2
    shapes = [((4, r, D), BF), ((4, HEADS, q.shape[0]), F32)]
    return local_call(cross_kernel, shapes, [q, k, v], rows_cost(q, k), None, scratch, 6)


def cross_back(q, k, v, up, lse):
    slots = q.shape[0]
    sem = pltpu.SemaphoreType.DMA
    scratch = [pltpu.VMEM((4, 32, slots), F32), pltpu.VMEM((HEADS, slots), F32)]
    scratch += [pltpu.VMEM((slots, D), F32), pltpu.VMEM((3, slots // 4, D), F32)]
    scratch += [sem((3,))] * 2 + [sem((3, HEADS // 2))] * 2
    shapes = [((slots // 4, D), F32), (k.shape, BF), (k.shape, BF)]
    return local_call(cross_back_kernel, shapes, [q, k, v, up, lse], 4 * rows_cost(q, k), None, scratch, 7)


def attend_back(q, k, v, up, lse, count=None, inner=None, out=BF):
    shapes = [(q.shape, out), (k.shape, BF), (k.shape, BF)]
    kernel = functools.partial(back_kernel, count is not None, inner is not None)
    args = [q, k, v, up, lse] + ([] if inner is None else [inner])
    return local_call(kernel, shapes, args, 3 * rows_cost(q, k), count)


def clip_attend(q, k, v):
    r = k.shape[0]
    shapes = [(q.shape, BF), ((HEADS, r), F32), ((4 * r, D), BF), ((4 * r, D), BF)]
    sems = [pltpu.SemaphoreType.DMA((2, HEADS // 2))] * 4
    return local_call(clip_attend_kernel, shapes, [q, k, v], 4 * rows_cost(q, k), None, sems, 3)


def clip_attend_back(q, k_all, v_all, up, lse):
    r = q.shape[0]
    scratch = [pltpu.VMEM((4 * r, D), BF)] * 2 + [pltpu.VMEM((2 * r, D), BF)] * 2
    scratch += [pltpu.VMEM((r, D), BF)] * 2 + [pltpu.SemaphoreType.DMA((2, HEADS // 2))] * 4
    args = [q, k_all, v_all, up, lse]
    return local_call(clip_back_kernel, [(q.shape, BF)] * 3, args, 3 * rows_cost(q, k_all), None, scratch, 4)


def mlp_kernel(stream, gain, bias, expand, contract, normed, pre, hidden, out):
    @pl.when(pl.program_id(0) == 0)
    def _():
        normed[...] = norm(stream[...], gain[...], bias[...])
        out[...] = stream[...]

    before = tdot(normed[...], expand[0], 1, 0)
    pre[0] = before
    after = gelu(before).astype(BF)
    hidden[0] = after
    out[...] += tdot(after, contract[0], 1, 0)


def mlp_back_kernel(up, stream, gain, pre, expand, contract, out, d_low, d_pre, d_gain, d_bias, total):
    s = pl.program_id(0)

    @pl.when(s == 0)
    def _():
        d_low[...] = up[...].astype(BF)
        total[...] = jnp.zeros_like(total)

    d_hidden = low(tdot(d_low[...], contract[0], 1, 1))
    grad = (gelu_slope(pre[0]) * d_hidden).astype(BF)
    d_pre[0] = grad
    total[...] += tdot(grad, expand[0], 1, 1)

    @pl.when(s == pl.num_programs(0) - 1)
    def _():
        hat, inv = norm_parts(stream[...])
        g = total[...] * gain[...]
        mean = lambda v: jnp.mean(v, axis=-1, keepdims=True)
        out[...] = up[...] + inv * (g - mean(g) - hat * mean(g * hat))
        d_gain[...] = jnp.sum(total[...] * hat, axis=0, keepdims=True)
        d_bias[...] = jnp.sum(total[...], axis=0, keepdims=True)


def blocks(kernel, grid, ins, outs, args, cost, scratch=()):
    def spec(shape, cut):
        if cut:
            return pl.BlockSpec((1,) + shape[1:], lambda s: (s,) + (0,) * (len(shape) - 1))
        return pl.BlockSpec(shape, lambda s: (0,) * len(shape))

    return pl.pallas_call(
        kernel,
        grid=(grid,),
        out_shape=[jax.ShapeDtypeStruct(s, t) for s, t, _ in outs],
        in_specs=[spec(a.shape, cut) for a, cut in zip(args, ins)],
        out_specs=[spec(s, cut) for s, _, cut in outs],
        scratch_shapes=list(scratch),
        cost_estimate=pl.CostEstimate(flops=cost, bytes_accessed=16 << 20, transcendentals=0),
        compiler_params=pltpu.CompilerParams(vmem_limit_bytes=48 << 20),
    )(*args)


def mlp(stream, gain, bias, expand, contract):
    n, (r, _) = expand.shape[0], stream.shape
    outs = [((r, D), BF, False), ((n, r, D), F32, True), ((n, r, D), BF, True), ((r, D), F32, False)]
    args = [stream, gain[None], bias[None], expand, contract.reshape(n, D, D)]
    return blocks(mlp_kernel, n, [False] * 3 + [True] * 2, outs, args, 4 * n * r * D * D)


def mlp_backward(up, stream, gain, pre, expand, contract):
    n, (r, _) = expand.shape[0], stream.shape
    outs = [((r, D), F32, False), ((r, D), BF, False), ((n, r, D), BF, True)]
    outs += [((1, D), F32, False)] * 2
    args = [up, stream, gain[None], pre, expand, contract.reshape(n, D, D)]
    scratch = [pltpu.VMEM((r, D), F32)]
    return blocks(mlp_back_kernel, n, [False] * 3 + [True] * 3, outs, args, 4 * n * r * D * D, scratch)


SQUARE = (4, 5, 6, 7, 18, 19, 20, 21, 24, 25, 26, 27)
TALL = (11, 31)
BROAD = (10, 30)
VECTORS = tuple(i for i in range(32) if KINDS[i] == "v")


ROW_PAD = 400
CHUNK = 80
SMALL_ROWS = 96


def gather_split(i, rows):
    return rows // 2 if rows % 32 == 0 else 16 + 16 * (i % 2)


def stem_kernel(plan, inputs, outputs, rows_held, *refs):
    n = len(plan)
    ins, refs = refs[:inputs], refs[inputs:]
    patches, angles, table, refs = refs[:3], refs[3], refs[4], refs[5:]
    outs, refs = refs[:outputs], refs[outputs:]
    even_pre, odd_pre, even, odd, even_next, second, stream, normed, q, k_all, v_all, o, lse, vec = refs[:14]
    looked, refs = refs[14], refs[:14] + refs[15:]
    got, stage, refs = refs[14 : 14 + n], refs[14 + n : 14 + 2 * n], refs[14 + 2 * n :]
    small, weights, k_own, v_own, found, heard, strips = refs[:7]
    lsem, zsend, zrecv, xsend, xrecv, ysend, yrecv, csend, crecv, psend, precv = refs[7:18]
    wsem, kxs, kxr, kcs, kcr, tsend, trecv, usend, urecv = refs[18:]
    z, y, x, c = where_am_i()
    zs, yp, xp, cp = partners(z, y, x, c)
    greet(zs, yp, xp, cp)
    dst, src, swaps = [], [], []
    for i, (k, rows, out, tap, kind) in enumerate(plan):
        dst.append(outs[out] if tap is None else outs[out].at[tap])
        src.append(ins[k] if tap is None else ins[k].at[tap])
        swaps.append(None)
        if kind == "n":
            theirs = src[i].at[pl.ds(pl.multiple_of((1 - c) * rows, 16), rows), :]
            swaps[i] = remote(theirs, got[i], psend.at[i], precv.at[i], cp)
            swaps[i].start()

    def item(i):
        rows, wide = plan[i][1], plan[i][4] == "w"
        h = gather_split(i, rows)
        return rows, wide, slice(0, h), slice(h, rows)

    stages = {}

    def start(i, key, copies):
        for cpy in copies:
            cpy.start()
        stages[i, key] = copies

    def send_z(i):
        rows, wide, _, _ = item(i)
        block = src[i]
        if not wide:
            mine = src[i][pl.ds(pl.multiple_of(c * rows, 16), rows), :]
            swaps[i].wait_recv()
            theirs = got[i][...]
            stage[i][...] = jnp.concatenate(
                [jnp.where(c == 0, mine, theirs), jnp.where(c == 0, theirs, mine)], axis=1
            )
            block = stage[i]
        here = spot(dst[i], wide, z, y, x, c, slice(None))
        start(i, 0, [remote(block, here, zsend.at[i, j], zrecv.at[i, j], zs[j]) for j in range(3)])
        start(i, 4, [pltpu.make_async_copy(block, here, lsem.at[i])])

    def send_1(i):
        rows, wide, a, b = item(i)
        for cpy in stages[i, 0]:
            cpy.wait_recv()
        stages[i, 4][0].wait()
        ax = spot(dst[i], wide, None, y, x, c, a)
        by = spot(dst[i], wide, None, y, x, c, b)
        start(
            i,
            1,
            [
                remote(ax, ax, xsend.at[i, 0], xrecv.at[i, 0], xp),
                remote(by, by, ysend.at[i, 0], yrecv.at[i, 0], yp),
            ],
        )

    def send_2(i):
        rows, wide, a, b = item(i)
        for cpy in stages[i, 1]:
            cpy.wait_recv()
        ay = spot(dst[i], wide, None, y, None, c, a)
        bx = spot(dst[i], wide, None, None, x, c, b)
        start(
            i,
            2,
            [
                remote(ay, ay, ysend.at[i, 1], yrecv.at[i, 1], yp),
                remote(bx, bx, xsend.at[i, 1], xrecv.at[i, 1], xp),
            ],
        )

    def send_core(i):
        rows, wide, a, b = item(i)
        for cpy in stages[i, 2]:
            cpy.wait_recv()
        half = spot(dst[i], wide, None, None, None, c, slice(None))
        start(i, 3, [remote(half, half, csend.at[i], crecv.at[i], cp)])

    arrived = set()

    def arrive(i):
        if i not in arrived:
            stages[i, 3][0].wait_recv()
            arrived.add(i)

    r = q.shape[0]
    pairs = HEADS // 2

    def fetch(items, slots):
        copies = []
        for i, slot in zip(items, slots):
            arrive(i)
            copies.append(pltpu.make_async_copy(dst[i], weights.at[slot], wsem.at[slot]))
            copies[-1].start()
        for cpy in copies:
            cpy.wait()

    def weight(slot):
        return weights[slot].reshape(D, D)

    def open_small():
        arrive(0)
        copy = pltpu.make_async_copy(dst[0], small, wsem.at[3])
        copy.start()
        copy.wait()
        cells = []
        for zy in range(8):
            for s in range(4):
                cells.append(small[s // 2, s % 2, zy // 2, zy % 2, 64:80, 0:24].astype(F32))
        vec[...] = jnp.concatenate(cells, axis=1)

    def convolve(patch, pre, act, edge):
        def one(t, _):
            rows = pl.ds(pl.multiple_of(t * CHUNK, 16), CHUNK)
            left = patch[rows, :]
            cells = []
            for zy in range(8):
                taps = [small[s // 2, s % 2, zy // 2, zy % 2, 0:64, :] for s in range(4)]
                cells.append(tdot(left, jnp.concatenate(taps, axis=0), 1, 0)[:, 0:96])
            before = jnp.concatenate(cells, axis=1)
            if pre is not None:
                pre[rows, :] = before
            after = gelu(before)
            if edge is not None:
                row, outside = edge
                at = t * CHUNK + lax.broadcasted_iota(jnp.int32, after.shape, 0)
                after = jnp.where((at == row) & outside, 0.0, after)
            act[rows, :] = after.astype(BF)
            return 0

        lax.fori_loop(0, ROW_PAD // CHUNK, one, 0)

    me = 2 * x + c
    part = 128
    slots = looked.shape[0]
    eighth = slots // 8

    def other_clip(m):
        return lax.rem(z + m // 2, 4), lax.rem(y + m % 2, 2)

    def tell(m):
        zt, yt = other_clip(m)
        return remote(found.at[m], heard.at[m], tsend.at[m], trecv.at[m], (zt * 2 + yt, 2 * x + c))

    def look_up(m):
        zt, yt = other_clip(m)
        cells = []
        for s in range(4):
            for half in (0, 1):
                code = small[s // 2, s % 2, zt, yt, 0:64, 96:128].astype(F32)[0:eighth]
                cells.append(code[:, 2 * half : 2 * half + 1] * 256.0 + code[:, 2 * half + 1 : 2 * half + 2])
        first = (z * 2 + y) * rows_held
        place = jnp.concatenate(cells, axis=0).astype(jnp.int32) - first

        def one(k, total):
            lane = lax.broadcasted_iota(jnp.int32, (slots, 384), 1) + k * 384
            hot = jnp.where((lane == place) & (lane < rows_held), 1.0, 0.0).astype(BF)
            return total + tdot(hot, table[pl.ds(pl.multiple_of(k * 384, 384), 384), :], 1, 0)

        total = lax.fori_loop(0, table.shape[0] // 384, one, jnp.zeros((slots, D // 4), F32))
        if m == 0:
            heard[0] = total.astype(BF)
        else:
            found[m] = total.astype(BF)
            tell(m).start()

    def strip(over):
        if over == 0:
            return remote(strips.at[x, c], strips.at[x, c], usend.at[0], urecv.at[0], xp)
        return remote(strips.at[:, c], strips.at[:, c], usend.at[1], urecv.at[1], cp)

    def sum_found():
        total = heard[0].astype(F32)
        for m in range(1, 8):
            tell(m).wait_recv()
            total = total + heard[m].astype(F32)
        strips[x, c] = total.astype(BF)
        strip(0).start()

    def pass_strips():
        strip(0).wait_recv()
        strip(1).start()

    def join_strips():
        strip(1).wait_recv()
        looked[...] = jnp.concatenate([strips[s // 2, s % 2] for s in range(4)], axis=1)

    def convolve_second(t):
        rows = slice(t * part, (t + 1) * part)
        total = tdot(even[rows, :], weight(0), 1, 0)
        total = total + tdot(odd[rows, :], weight(1), 1, 0)
        total = total + tdot(even_next[rows, :], weight(2), 1, 0)
        second[rows, :] = total
        out = gelu(total) + angles[rows, :]
        stream[rows, :] = out
        normed[rows, :] = norm(out, vec[0:1, :], vec[1:2, :])

    def project():
        for t in range(r // part):
            rows = slice(t * part, (t + 1) * part)
            left = normed[rows, :]
            q[rows, :] = (tdot(left, weight(0), 1, 0) * SCALE).astype(BF)
            k_own[rows, :] = tdot(left, weight(1), 1, 0).astype(BF)
            v_own[rows, :] = tdot(left, weight(2), 1, 0).astype(BF)
        for pair in range(pairs):
            for cpy in across(pair):
                cpy.start()
        k_all[0:r, :] = k_own[...]
        v_all[0:r, :] = v_own[...]

    def across(pair):
        at = lanes_of(pair)
        return [
            remote(a.at[:, at], b.at[r : 2 * r, at], kxs.at[j, pair], kxr.at[j, pair], xp)
            for j, (a, b) in enumerate(((k_own, k_all), (v_own, v_all)))
        ]

    def beside(pair):
        at = lanes_of(pair)
        return [
            remote(a.at[0 : 2 * r, at], a.at[2 * r : 4 * r, at], kcs.at[j, pair], kcr.at[j, pair], cp)
            for j, a in enumerate((k_all, v_all))
        ]

    def pass_on(pair):
        for cpy in across(pair):
            cpy.wait_recv()
        for cpy in beside(pair):
            cpy.start()

    def attend_pair(pair):
        if pair + 1 < pairs:
            pass_on(pair + 1)
        for cpy in beside(pair):
            cpy.wait_recv()
        forward_pair(pair, q, k_all, v_all, o, lse, None)

    pieces = [
        open_small,
        lambda: convolve(patches[0], even_pre, even, (0, me == 0)),
        lambda: (look_up(0), look_up(1)),
        lambda: convolve(patches[1], odd_pre, odd, (r, me == 3)),
        lambda: (look_up(2), look_up(3)),
        lambda: convolve(patches[2], None, even_next, None),
        lambda: (look_up(4), look_up(5)),
        lambda: (fetch((1, 2, 3), (0, 1, 2)), convolve_second(0)),
    ]
    pieces += [functools.partial(convolve_second, t) for t in range(1, r // part)]
    pieces += [lambda: (fetch((4, 5, 6), (0, 1, 2)), project()), lambda: (look_up(6), look_up(7))]
    pieces += [lambda: (pass_on(0), sum_found()), lambda: (attend_pair(0), pass_strips())]
    pieces += [lambda: (attend_pair(1), join_strips())]
    pieces += [functools.partial(attend_pair, pair) for pair in range(2, pairs)]

    for t in range(n + AHEAD[2]):
        if t == 0:
            for i in range(min(n, AHEAD[3])):
                send_z(i)
        if t + AHEAD[3] < n:
            send_z(t + AHEAD[3])
        if 0 <= t - AHEAD[0] < n:
            send_1(t - AHEAD[0])
        if 0 <= t - AHEAD[1] < n:
            send_2(t - AHEAD[1])
        if 0 <= t - AHEAD[2] < n:
            send_core(t - AHEAD[2])
        if t >= PIECES_FROM and pieces:
            pieces.pop(0)()
    while pieces:
        pieces.pop(0)()
    for i in range(n):
        if swaps[i] is not None:
            swaps[i].wait_send()
        arrive(i)
        for key in range(4):
            for cpy in stages[i, key]:
                cpy.wait_send()
    for pair in range(pairs):
        for cpy in across(pair) + beside(pair):
            cpy.wait_send()
    for m in range(1, 8):
        tell(m).wait_send()
    strip(0).wait_send()
    strip(1).wait_send()


AHEAD = (0, 1, 3, 6)
PIECES_FROM = 5


def gather_and_stem(plan, ins, out_shapes, patches, angles, table, slots, rows_held):
    n, r = len(plan), angles.shape[0]
    sem = pltpu.SemaphoreType.DMA
    hbm, vmem = pl.BlockSpec(memory_space=pl.ANY), pl.BlockSpec(memory_space=pltpu.VMEM)
    got, stage = [], []
    for _, rows, _, _, kind in plan:
        got.append(pltpu.VMEM((rows, LANES // 2) if kind == "n" else (16, 128), BF))
        stage.append(pltpu.VMEM((rows, LANES) if kind == "n" else (16, 128), BF))
    sems = [sem((n,)), sem((n, 3)), sem((n, 3))] + [sem((n, 2))] * 4 + [sem((n,))] * 4
    made = [((ROW_PAD, D), F32)] * 2 + [((ROW_PAD, D), BF)] * 3 + [((r, D), F32)] * 2
    made += [((r, D), BF)] * 2 + [((4 * r, D), BF)] * 2 + [((r, D), BF), ((HEADS, r), F32), ((16, D), F32)]
    made += [((slots, D), BF)]
    held = [pltpu.VMEM((2, 2, 4, 2, SMALL_ROWS, 128), BF), pltpu.VMEM((3, 4, 2, 2, 48, D), BF)]
    held += [pltpu.VMEM((r, D), BF)] * 2 + [pltpu.VMEM((8, slots, D // 4), BF)] * 2
    held += [pltpu.VMEM((2, 2, slots, D // 4), BF)]
    return pl.pallas_call(
        functools.partial(stem_kernel, plan, len(ins), len(out_shapes), rows_held),
        out_shape=[jax.ShapeDtypeStruct(s, BF) for s in out_shapes]
        + [jax.ShapeDtypeStruct(s, t) for s, t in made],
        in_specs=[vmem] * (len(ins) + 5),
        out_specs=[hbm] * len(out_shapes) + [vmem] * len(made),
        scratch_shapes=got + stage + held + sems + [sem((4,))] + [sem((2, HEADS // 2))] * 4 + [sem((8,))] * 2 + [sem((2,))] * 2,
        compiler_params=pltpu.CompilerParams(
            collective_id=1, has_side_effects=True, vmem_limit_bytes=60 << 20
        ),
    )(*ins, *patches, angles, table)


def small_block(shards, ids):
    w = shards[0]
    t, i, o = w.shape
    halves = ids.reshape(2, -1)
    codes = jnp.stack([halves[0] // 256, halves[0] % 256, halves[1] // 256, halves[1] % 256], axis=1)
    codes = jnp.pad(codes.astype(BF), ((0, 64 - codes.shape[0]), (0, 32 - 4)))
    top = jnp.concatenate([jnp.pad(w.reshape(t * i, o), ((0, 64 - t * i), (0, 0))), codes], axis=1)
    rows = jnp.stack([shards[k] for k in VECTORS])
    rows = jnp.pad(rows, ((0, SMALL_ROWS - 64 - rows.shape[0]), (0, 128 - rows.shape[1])))
    return jnp.concatenate([top, rows])


def patch_rows(patch, mels):
    p = patch.reshape(patch.shape[0], 3, 4, mels // 4).transpose(0, 2, 1, 3).reshape(patch.shape[0], 4, -1)
    p = jnp.pad(p, ((0, ROW_PAD - p.shape[0]), (0, 0), (0, 64 - p.shape[2])))
    return p.reshape(ROW_PAD, 256)


def gather_weights(shards, patches, angles, ids, table):
    plan, ins, shapes, at = [], [], [], {}
    for i in SQUARE + (1,) + TALL + (15,):
        w = shards[i]
        if i == 15:
            w = jnp.concatenate([w, jnp.zeros((-w.shape[0] % 32, w.shape[1]), BF)])
        rows = w.shape[-2] // 2
        for tap in range(3) if w.ndim == 3 else (None,):
            at[i, tap] = len(plan)
            plan.append((len(ins), rows, len(shapes), None, "n"))
            ins.append(w if tap is None else w[tap])
            shapes.append((4, 2, 2, rows, D))
    for i in BROAD:
        at[i, None] = len(plan)
        plan.append((len(ins), shards[i].shape[0], len(shapes), None, "w"))
        ins.append(shards[i])
        shapes.append((2, 2, 4, 2) + shards[i].shape)
    at[0, None] = len(plan)
    plan.append((len(ins), SMALL_ROWS, len(shapes), None, "w"))
    ins.append(small_block(shards, ids))
    shapes.append((2, 2, 4, 2, SMALL_ROWS, 128))
    first = [at[0, None], at[1, 0], at[1, 1], at[1, 2], at[4, None], at[5, None], at[6, None]]
    order = first + [k for k in range(len(plan)) if k not in first]
    rows_held = table.shape[0]
    table = jnp.pad(table, ((0, -rows_held % 384), (0, 0)))
    outs = gather_and_stem([plan[k] for k in order], ins, shapes, patches, angles, table, 4 * ids.size, rows_held)
    outs, made = outs[: len(plan)], outs[len(plan) :]
    full = [None] * 32
    for i in SQUARE + TALL:
        full[i] = outs[at[i, None]].reshape(-1, D)
    full[1] = [outs[at[1, tap]].reshape(D, D) for tap in range(3)]
    r = shards[15].shape[0]
    full[15] = outs[at[15, None]].reshape(8, -1, D)[:, :r].reshape(8 * r, D)
    for i in BROAD:
        full[i] = outs[at[i, None]].reshape(4, D, D)
    t, a, b = shards[0].shape
    small = outs[at[0, None]]
    codes = small[..., : ids.size // 2, 96:100].astype(jnp.int32)
    all_ids = jnp.stack([codes[..., 2 * h] * 256 + codes[..., 2 * h + 1] for h in (0, 1)], axis=4)
    all_ids = all_ids.transpose(2, 3, 0, 1, 4, 5).reshape(-1)
    conv1 = small[..., : t * a, :b].reshape(2, 2, 4, 2, t, a, b)
    full[0] = conv1.transpose(4, 0, 1, 5, 2, 3, 6).reshape(t, 4 * a, 8 * b)
    for k, i in enumerate(VECTORS):
        full[i] = made[13][k]
    return full, made[:13], all_ids, made[14]


ORDER = (31, 30, 27, 24, 21, 18, 19, 20, 11, 10, 25, 26, 7, 4, 5, 6, 1)
EXACT = 25
HEAD_START = 1
MIX = 2


def reduce_grads(grads, shards):
    items, jobs, ins, shapes, seen = [], [], [], [], {}

    def place(v):
        if id(v) not in seen:
            seen[id(v)] = len(ins)
            ins.append(v)
        return seen[id(v)]

    for i in ORDER:
        left, right = grads[i]
        if i in TALL:
            jobs += [(len(items), s, place(left), place(right), left.shape[1]) for s in range(4)]
            items.append(("t", BF, len(shapes), None))
            shapes.append((2, 2, 2, RB, LANES // 2))
        elif i in BROAD:
            jobs += [(len(items), s, place(left), place(right), left.shape[0]) for s in range(4)]
            items.append(("w", BF, len(shapes), None))
            shapes.append((2, RB, D))
        elif i == 1:
            for tap, l in enumerate(left):
                jobs.append((len(items), 0, place(l), place(right), right.shape[0]))
                items.append(("n", BF, len(shapes), tap))
            shapes.append((3, 2, RB, LANES // 2))
        else:
            jobs.append((len(items), 0, place(left), place(right), left.shape[0]))
            items.append(("n", F32 if i == EXACT else BF, len(shapes), None))
            shapes.append((2, RB, LANES // 2))
    t, a, b = shards[0].shape
    conv1 = grads[0].reshape(t, 2, 2, a, 4, 2, b).transpose(1, 2, 4, 5, 0, 3, 6).reshape(2, 2, 4, 2, t * a, b)
    n = shards[VECTORS[0]].size
    vecs = jnp.stack([grads[i] for i in VECTORS]).reshape(-1, 4, 2, 2, 2, n).transpose(3, 4, 1, 2, 0, 5)
    none = ((0, 0),) * 4
    conv1 = jnp.pad(conv1.astype(BF), none + ((0, 64 - t * a), (0, 128 - b)))
    vecs = jnp.pad(vecs.astype(BF), none + ((0, SMALL_ROWS - 64 - len(VECTORS)), (0, 128 - n)))
    ins.append(jnp.concatenate([conv1, vecs], axis=4).reshape(2, 2, 4, 2, 2, RB, 128))
    items.append(("m", BF, len(shapes), None))
    shapes.append((2, RB, 128))
    small = [j for j in jobs if items[j[0]][0] == "n"]
    large = [j for j in jobs if items[j[0]][0] != "n"]
    jobs, large = small[:HEAD_START], list(large)
    for j in small[HEAD_START:]:
        jobs += large[:MIX] + [j]
        large = large[MIX:]
    jobs = jobs[:-1] + large + jobs[-1:]
    got = reduce_fast(items, jobs, ins, shapes)
    out = [None] * 32
    for i, v in zip(ORDER, got):
        out[i] = v.reshape(shards[i].shape)
    small = got[-1].reshape(SMALL_ROWS, 128)
    out[0] = small[: t * a, :b].reshape(t, a, b)
    for k, i in enumerate(VECTORS):
        out[i] = small[64 + k, :n]
    return out


def one_hot(ids, table):
    first = lax.axis_index("dp") * table.shape[0]
    return ((ids - first)[:, None] == jnp.arange(table.shape[0])[None, :]).astype(BF)


def body(mel_frames, token_ids, token_counts, *rest):
    shards, cotangent = list(rest[:32]), rest[32][0]
    table = shards[14]
    dps, seqs = lax.axis_size("dp"), lax.axis_size("seq")
    me = lax.axis_index("seq")
    slots = token_ids.shape[1]
    all_slots = slots * seqs
    frames = mel_frames.shape[1] // 2

    fast = dps == 8 and seqs == 4
    weights = shards[:14] + [None] + shards[15:]
    pairs = extended(mel_frames[0], 2).reshape(frames + 2, -1)
    mels = mel_frames.shape[2]
    n = frames + 1
    even_in = jnp.concatenate([pairs[:n], pairs[1:, :mels]], axis=1)
    odd_in = jnp.concatenate([pairs[:n, mels:], pairs[1:]], axis=1)
    angles = sinusoid(me * frames, frames)
    row = jnp.arange(n)[:, None]
    even_keep = (row > 0) | (me > 0)
    odd_keep = (row < n - 1) | (me < seqs - 1)
    if fast:
        patches = [patch_rows(p, mels) for p in (even_in, odd_in, even_in[1:])]
        full, made, ids, looked = gather_weights(weights, patches, angles, token_ids[0], table)
        even_pre, odd_pre, even0, odd0, even1, second_pre, stream0, enc_normed, q, k_all, v_all = made[:11]
        enc_mixed, enc_lse = made[11:]
    else:
        full = gather_plain(weights)
        conv1, conv2 = full[0].reshape(-1, D), full[1]
        even_pre, odd_pre = mm(even_in, conv1), mm(odd_in, conv1)
        even = jnp.where(even_keep, gelu(even_pre), 0.0).astype(BF)
        odd0 = jnp.where(odd_keep, gelu(odd_pre), 0.0).astype(BF)[:frames]
        even0, even1 = even[:frames], even[1:]
        second_pre = mm(even0, conv2[0]) + mm(odd0, conv2[1]) + mm(even1, conv2[2])
        stream0 = gelu(second_pre) + angles
        enc_normed = norm(stream0, full[2].astype(F32), full[3].astype(F32))
        q = (mm(enc_normed, full[4]) * SCALE).astype(BF)
        k, v = mm(enc_normed, full[5], BF), mm(enc_normed, full[6], BF)
        enc_mixed, enc_lse, k_all, v_all = clip_attend(q, k, v)
        ids = lax.all_gather(token_ids[0], BOTH, axis=0, tiled=True)
        looked = lax.psum_scatter(mm(one_hot(ids, table), table, BF), "dp", scatter_dimension=0, tiled=True)
        looked = lax.all_gather(looked, "seq", axis=0, tiled=True)
        looked = looked.reshape(seqs, all_slots, D // seqs).transpose(1, 0, 2).reshape(all_slots, D)
    vec = {i: full[i].astype(F32) for i in range(32) if KINDS[i] == "v"}
    conv1, conv2, position = full[0].reshape(-1, D), full[1], full[15]
    eo = full[7]
    ee, ec = full[10:12]
    dq_w, dk_w, dv_w, do_w = full[18:22]
    cq_w, ck_w, cv_w, co_w = full[24:28]
    de, dc = full[30:32]


    stream1 = stream0 + mm(enc_mixed, eo)
    enc_mlp_normed, enc_pre, enc_hidden, stream2 = mlp(stream1, vec[8], vec[9], ee, ec)
    memory = norm(stream2, vec[12], vec[13])
    mk = mm(memory, ck_w, BF)
    mv = mm(memory, cv_w, BF)

    place = jnp.arange(all_slots)
    embedded = looked.astype(F32) + position.astype(F32)
    dec_normed = norm(embedded, vec[16], vec[17])
    sq = (mm(dec_normed, dq_w) * SCALE).astype(BF)
    sk = mm(dec_normed, dk_w, BF)
    sv = mm(dec_normed, dv_w, BF)
    dec_mixed, dec_lse = attend(sq, sk, sv, token_counts)
    stream4 = embedded + mm(dec_mixed, do_w)
    cross_normed = norm(stream4, vec[22], vec[23])
    xq = (mm(cross_normed, cq_w) * SCALE).astype(BF)

    parts, lses = cross_attend(xq, mk, mv)
    lses = lax.dynamic_slice_in_dim(lses, me * slots, slots, 2).transpose(0, 2, 1)
    top = jnp.max(lses, axis=0)
    share = jnp.exp(lses - top)
    total = jnp.sum(share, axis=0)
    cross_lse = top + jnp.log(total)
    share = share / total
    cross_mixed = jnp.sum(
        parts.astype(F32).reshape(seqs, slots, HEADS, HEAD) * share[..., None], axis=0
    ).reshape(slots, D)
    cross_mixed = cross_mixed.astype(BF)

    own = lambda a: lax.dynamic_slice_in_dim(a, me * slots, slots, 0)
    stream4 = own(stream4)
    stream5 = stream4 + mm(cross_mixed, co_w)
    dec_mlp_normed, dec_pre, dec_hidden, stream6 = mlp(stream5, vec[28], vec[29], de, dc)
    live = (own(place) < token_counts[0])[:, None]
    decoded = jnp.where(live, stream6, 0.0).astype(BF)

    grads = [None] * 32

    def mlp_back(ex, co, gain, normed, pre, hidden, stream, up):
        up, d_low, d_pre, d_gain, d_bias = mlp_backward(up, stream, vec[gain], pre, full[ex], full[co])
        grads[co], grads[ex] = (hidden, d_low), (normed, d_pre)
        grads[gain], grads[gain + 1] = d_gain[0], d_bias[0]
        return up

    up = jnp.where(live, cotangent.astype(F32), 0.0)
    up = mlp_back(30, 31, 28, dec_mlp_normed, dec_pre, dec_hidden, stream5, up)
    d_low = up.astype(BF)
    grads[27] = (cross_mixed, d_low)
    d_mixed = mm_t(d_low, co_w, BF)
    d_mixed, lse_all = unpack(lax.all_gather(pack(d_mixed, cross_lse.T), "seq", axis=0, tiled=True))
    lse_all = lse_all.T
    dxq, dmk, dmv = cross_back(xq, mk, mv, d_mixed, lse_all)
    dxq = (low(dxq) * SCALE).astype(BF)
    grads[24] = (own(cross_normed), dxq)
    back, grads[22], grads[23] = norm_back(stream4, vec[22], mm_t(dxq, cq_w))
    up = up + back
    d_low = up.astype(BF)
    grads[21] = (own(dec_mixed), d_low)
    d_mixed = lax.all_gather(mm_t(d_low, do_w, BF), "seq", axis=0, tiled=True)
    dsq, dsk, dsv = attend_back(sq, sk, sv, d_mixed, dec_lse, token_counts)

    def inputs_back(first, gain, normed, stream, dq, dk, dv, up):
        dq = (dq.astype(F32) * SCALE).astype(BF)
        total = 0.0
        for i, g in enumerate((dq, dk, dv)):
            grads[first + i] = (normed, g)
            total = total + mm_t(g, full[first + i])
        back, grads[gain], grads[gain + 1] = norm_back(stream, vec[gain], total)
        return up + back

    up = inputs_back(18, 16, own(dec_normed), own(embedded), own(dsq), own(dsk), own(dsv), up)

    cols = exchange_columns(up.astype(BF))

    grads[25] = (memory, dmk)
    grads[26] = (memory, dmv)
    up, grads[12], grads[13] = norm_back(stream2, vec[12], mm_t(dmk, ck_w) + mm_t(dmv, cv_w))
    up = mlp_back(10, 11, 8, enc_mlp_normed, enc_pre, enc_hidden, stream1, up)
    d_low = up.astype(BF)
    grads[7] = (enc_mixed, d_low)
    d_mixed = mm_t(d_low, eo, BF)
    dq, dk, dv = clip_attend_back(q, k_all, v_all, d_mixed, enc_lse)
    up = inputs_back(4, 2, enc_normed, stream0, dq, dk, dv, up)

    d_second = (gelu_slope(second_pre) * up).astype(BF)
    grads[1] = ([even0, odd0, even1], d_second)
    rim = extended(d_second, 1)
    padded = even_pre.shape[0]
    rim = jnp.pad(rim, ((0, padded + 1 - rim.shape[0]), (0, 0)))
    row = jnp.arange(padded)[:, None]
    even_keep = ((row > 0) | (me > 0)) & (row < n)
    odd_keep = (row < n - 1) | ((me < seqs - 1) & (row < n))
    d_even = mm_t(rim[1:], conv2[0]) + mm_t(rim[:padded], conv2[2])
    d_odd = mm_t(rim[1:], conv2[1])
    d_even = jnp.where(even_keep, gelu_slope(even_pre) * low(d_even), 0.0).astype(BF)
    d_odd = jnp.where(odd_keep, gelu_slope(odd_pre) * low(d_odd), 0.0).astype(BF)
    grads[0] = (outer(odd_in[:frames], d_odd[:frames], F32) + outer(even_in[1:], d_even[1:n], F32)).reshape(
        3, mels, D
    )
    me_g, mo_g = mm_t(d_even, conv1), mm_t(d_odd, conv1)
    mel_grad = jnp.concatenate(
        [
            me_g[1:n, :mels] + me_g[: n - 1, 2 * mels :] + mo_g[: n - 1, mels : 2 * mels],
            me_g[1:n, mels : 2 * mels] + mo_g[1:n, :mels] + mo_g[: n - 1, 2 * mels :],
        ],
        axis=1,
    ).reshape(1, 2 * frames, mels)

    every = lax.all_gather(cols, "dp", axis=0, tiled=True)
    done = (reduce_grads if fast else reduce_plain)(grads, shards)
    done[14] = dot(one_hot(ids, table), every, 0, 0)
    per_clip = every.reshape(dps, dps, -1, D // seqs)
    done[15] = jnp.sum(
        lax.dynamic_index_in_dim(per_clip, lax.axis_index("dp"), 1, False).astype(F32), axis=0
    )
    return tuple([decoded[None], mel_grad] + done)


def exchange_columns(v):
    n = lax.axis_size("seq")
    wide = v.shape[1] // n
    v = v.reshape(v.shape[0], n, wide).transpose(1, 0, 2)
    return lax.all_to_all(v, "seq", split_axis=0, concat_axis=0, tiled=True).reshape(-1, wide)


def solution(mesh):
    place = {
        "1": P(None, "seq", "dp"),
        "2": P(None, "dp", "seq"),
        "v": P(BOTH),
        "m": P("dp", "seq"),
        "t": P("dp", "seq"),
    }
    rows = P("dp", "seq", None)
    weights = tuple(place[k] for k in KINDS)
    return jax.shard_map(
        body,
        mesh=mesh,
        in_specs=(rows, P("dp", "seq"), P("dp")) + weights + (rows,),
        out_specs=(rows, rows) + weights,
        check_vma=False,
    )
```

```python
import functools
import math

import jax
import jax.numpy as jnp
from jax import lax
from jax.experimental import pallas as pl
from jax.experimental.pallas import tpu as pltpu
from jax.sharding import PartitionSpec as P

D = 768
HEADS = 12
HEAD = 64
EPSILON = 1e-05
NEGATIVE = -1e30
SCALE = 1.0 / math.sqrt(HEAD)
BF = jnp.bfloat16
F32 = jnp.float32
BOTH = ("dp", "seq")

KINDS = "12vvmmmmvvmmvvtmvvmmmmvvmmmmvvmm"


def dot(a, b, ca, cb, out=F32):
    return lax.dot_general(a, b, (((ca,), (cb,)), ((), ())), preferred_element_type=F32).astype(out)


def mm(a, b, out=F32):
    return dot(a, b, 1, 0, out)


def mm_t(a, b, out=F32):
    return dot(a, b, 1, 1, out)


def outer(a, b, out=BF):
    return dot(a, b, 0, 0, out)


def norm_parts(values):
    center = values - jnp.mean(values, axis=-1, keepdims=True)
    spread = jnp.mean(center * center, axis=-1, keepdims=True)
    inv = lax.rsqrt(spread + EPSILON)
    return center * inv, inv


def norm(values, gain, bias):
    return (norm_parts(values)[0] * gain + bias).astype(BF)


def norm_back(values, gain, up):
    hat, inv = norm_parts(values)
    g = up * gain
    back = inv * (
        g - jnp.mean(g, axis=-1, keepdims=True) - hat * jnp.mean(g * hat, axis=-1, keepdims=True)
    )
    return back, jnp.sum(up * hat, axis=0), jnp.sum(up, axis=0)


def gelu(v):
    return v * (0.5 + 0.5 * lax.erf(v * math.sqrt(0.5)))


def gelu_slope(v):
    return (0.5 + 0.5 * lax.erf(v * math.sqrt(0.5))) + v * jnp.exp(-0.5 * v * v) * (
        1.0 / math.sqrt(2.0 * math.pi)
    )


def low(v):
    return lax.reduce_precision(v, 8, 7)


PAIR = 2 * HEAD


def tdot(a, b, ca, cb):
    return lax.dot_general(a, b, (((ca,), (cb,)), ((), ())), preferred_element_type=F32)


def one_head(rows, half):
    lane = lax.broadcasted_iota(jnp.int32, rows.shape, 1)
    return jnp.where((lane < HEAD) == (half == 0), rows, jnp.zeros_like(rows))


def masked(s, count_ref):
    if count_ref is None:
        return s
    key = lax.broadcasted_iota(jnp.int32, s.shape, 0)
    query = lax.broadcasted_iota(jnp.int32, s.shape, 1)
    return jnp.where((key <= query) & (key < count_ref[0]), s, NEGATIVE)


def pack(rows, log_sums):
    cols, rest = [rows], log_sums.T
    for _ in range(3):
        term = low(rest)
        cols.append(term.astype(BF))
        rest = rest - term
    wide = sum(c.shape[1] for c in cols)
    return jnp.concatenate(cols + [jnp.zeros((rows.shape[0], -wide % 128), BF)], axis=1)


def unpack(packed):
    terms = [packed[..., D + i * HEADS : D + (i + 1) * HEADS].astype(F32) for i in range(3)]
    return packed[..., :D], terms[0] + terms[1] + terms[2]


def shift(v, axis, step):
    n = lax.axis_size(axis)
    return lax.ppermute(v, axis, [(i, i + step) for i in range(n) if 0 <= i + step < n])


def extended(x, width):
    before = shift(x[-width:], "seq", 1)
    after = shift(x[:width], "seq", -1)
    return jnp.concatenate([before, x, after], axis=0)


def sinusoid(first_frame, frame_count):
    half = D // 2
    frequency = jnp.exp(jnp.arange(half).astype(F32) * (-math.log(10000.0) / (half - 1)))
    places = (first_frame + jnp.arange(frame_count)).astype(F32)
    angles = places[:, None] * frequency[None, :]
    return jnp.concatenate([jnp.sin(angles), jnp.cos(angles)], axis=1)


def to_whole(flat, shape, kind, dps, seqs):
    if kind == "v":
        return flat.reshape(-1)
    if kind == "1":
        t, i, o = shape
        return (
            flat.reshape(dps, seqs, t, i, o)
            .transpose(2, 1, 3, 0, 4)
            .reshape(t, seqs * i, dps * o)
        )
    if kind == "2":
        t, i, o = shape
        return (
            flat.reshape(dps, seqs, t, i, o)
            .transpose(2, 0, 3, 1, 4)
            .reshape(t, dps * i, seqs * o)
        )
    r, c = shape
    return flat.reshape(dps, seqs, r, c).transpose(0, 2, 1, 3).reshape(dps * r, seqs * c)


def to_owner(g, kind, dps, seqs):
    n = dps * seqs
    if kind == "v":
        return g.reshape(n, -1)
    if kind == "1":
        t, i, o = g.shape
        g = g.reshape(t, seqs, i // seqs, dps, o // dps).transpose(3, 1, 0, 2, 4)
    elif kind == "2":
        t, i, o = g.shape
        g = g.reshape(t, dps, i // dps, seqs, o // seqs).transpose(1, 3, 0, 2, 4)
    else:
        r, c = g.shape
        g = g.reshape(dps, r // dps, seqs, c // seqs).transpose(0, 2, 1, 3)
    return g.reshape(n, -1)


def gather_plain(shards):
    dps, seqs = lax.axis_size("dp"), lax.axis_size("seq")
    flat = jnp.concatenate([w.reshape(-1) for w in shards if w is not None])
    got = lax.all_gather(flat[None], BOTH, axis=0, tiled=True)
    out, at = [], 0
    for w, kind in zip(shards, KINDS):
        if w is None:
            out.append(None)
            continue
        out.append(to_whole(got[:, at : at + w.size], w.shape, kind, dps, seqs))
        at += w.size
    for i in BROAD:
        out[i] = out[i].reshape(D, seqs, -1).transpose(1, 0, 2)
    return out


def product(factors):
    left, right = factors
    if right.ndim == 3:
        return jnp.concatenate([outer(left, r) for r in right], axis=1)
    if isinstance(left, list) or left.ndim == 3:
        return jnp.stack([outer(l, right) for l in left])
    return outer(left, right)


def reduce_plain(grads, shards):
    dps, seqs = lax.axis_size("dp"), lax.axis_size("seq")
    grads = [product(g) if isinstance(g, tuple) else g for g in grads]
    for i in TALL:
        grads[i] = grads[i].reshape(-1, D)
    flat = jnp.concatenate(
        [to_owner(g.astype(BF), k, dps, seqs) for g, k in zip(grads, KINDS) if g is not None], axis=1
    )
    own = lax.psum_scatter(flat, BOTH, scatter_dimension=0, tiled=True).astype(F32)[0]
    out, at = [], 0
    for w, g in zip(shards, grads):
        if g is None:
            out.append(None)
            continue
        out.append(own[at : at + w.size].reshape(w.shape))
        at += w.size
    return out


MESH = pl.DeviceIdType.MESH
LANES = 384


def where_am_i():
    d, s = lax.axis_index("dp"), lax.axis_index("seq")
    return d // 2, d % 2, s // 2, s % 2


def partners(z, y, x, c):
    at = lambda z, y, x, c: (z * 2 + y, x * 2 + c)
    zs = [at((z + j) % 4, y, x, c) for j in (1, 2, 3)]
    return zs, at(z, 1 - y, x, c), at(z, y, 1 - x, c), at(z, y, x, 1 - c)


def greet(zs, yp, xp, cp):
    barrier = pltpu.get_barrier_semaphore()
    everyone = zs + [yp, xp, cp]
    for dev in everyone:
        pl.semaphore_signal(barrier, inc=1, device_id=dev, device_id_type=MESH)
    pl.semaphore_wait(barrier, len(everyone))


def remote(src, dst, send, recv, dev):
    return pltpu.make_async_remote_copy(
        src_ref=src, dst_ref=dst, send_sem=send, recv_sem=recv, device_id=dev, device_id_type=MESH
    )


def split_at(i, rows):
    return rows // 2 if rows % 32 == 0 else 16 + 16 * (i % 2)


def lanes(x):
    return pl.ds(pl.multiple_of(x * LANES, LANES), LANES)


def spot(ref, wide, zs, ys, xs, c, rs):
    full = lambda v: slice(None) if v is None else v
    if wide:
        return ref.at[full(xs), c, full(zs), full(ys), rs, :]
    return ref.at[full(zs), full(ys), c, rs, slice(None) if xs is None else lanes(xs)]


def add_into(dst, *srcs):
    lead = srcs[0].shape[:-2]
    total = math.prod(lead)

    def one(k, _):
        at = []
        for size in reversed(lead):
            at.append(lax.rem(k, size))
            k = lax.div(k, size)
        at = tuple(reversed(at))
        acc = srcs[0][at].astype(F32)
        for s in srcs[1:]:
            acc = acc + s[at].astype(F32)
        dst[at] = acc.astype(dst.dtype)
        return 0

    lax.fori_loop(0, total, one, 0)


RB = 48


def item_shapes(kind, h):
    if kind == "n":
        g = RB - h
        return [
            (4, 2, RB, D),
            (4, h, D),
            (4, 2, g, LANES),
            (4, h, LANES),
            (4, g, LANES),
            (4, RB, LANES),
            (3, RB, LANES),
        ]
    if kind == "t":
        return [
            (4, 4, 2, RB, D),
            (4, 2, RB, D),
            (4, 4, RB, LANES),
            (4, 2, RB, LANES),
            (4, 2, RB, LANES),
            (4, 2, 2, RB, LANES),
            (3, 2, 2, RB, LANES),
        ]
    w = D if kind == "w" else 128
    return [
        (2, 4, 2, 2, RB, w),
        (2, 4, RB, w),
        (4, 2, RB, w),
        (4, RB, w),
        (4, RB, w),
        (4, 2, RB, w),
        (3, 2, RB, w),
    ]


def halves_of(k):
    return 16 + 16 * (k % 2)


def reduce_kernel(items, jobs, inputs, outputs, *refs):
    n = len(items)
    take = lambda count: (refs[:count], refs[count:])
    ins, refs = take(inputs)
    outs, refs = take(outputs)
    rc, refs = take(n)
    r1a, refs = take(n)
    r1b, refs = take(n)
    r2a, refs = take(n)
    r2b, refs = take(n)
    s3, refs = take(n)
    rz, refs = take(n)
    sbuf, refs = take(n)
    ring, wide_ring, given, xbuf, ybuf = refs[:5]
    loads, csend, crecv, xsend, xrecv, ysend, yrecv, zsend, zrecv, fsend, frecv = refs[5:]
    z, y, x, c = where_am_i()
    zs, yp, xp, cp = partners(z, y, x, c)
    greet(zs, yp, xp, cp)
    started = []

    def start(copy):
        copy.start()
        started.append(copy)
        return copy

    cores, ones, twos, threes, loaded = {}, {}, {}, {}, {}
    half = lambda i: halves_of(i)
    at = {(j[0], j[1]): t for t, j in enumerate(jobs)}

    def load(t):
        _, part, xi, yi, rows = jobs[t]
        xsrc, ysrc = ins[xi], ins[yi]
        if len(xsrc.shape) == 3:
            xsrc = xsrc.at[part]
        elif xsrc.shape[0] > rows:
            xsrc = xsrc.at[0:rows]
        if len(ysrc.shape) == 3:
            ysrc = ysrc.at[2 * (part // 2) + (c if part % 2 else 1 - c)]
        pair = []
        for k, (src, buf) in enumerate(((xsrc, xbuf), (ysrc, ybuf))):
            copy = pltpu.make_async_copy(src, buf.at[t % 2, 0:rows], loads.at[t % 2, k])
            copy.start()
            pair.append(copy)
        loaded[t] = pair

    def room(t):
        return wide_ring if items[jobs[t][0]][1] == F32 else ring.at[t % RING]

    def compute(t):
        i, part, _, _, rows = jobs[t]
        if t >= RING and t - RING in cores and items[jobs[t - RING][0]][1] == BF:
            cores[t - RING].wait_send()
        for copy in loaded[t]:
            copy.wait()
        room_t = room(t)
        left = xbuf[t % 2, 0:rows, :]

        def column(k, _):
            cols = pl.ds(pl.multiple_of(k * 256, 256), 256)
            product = tdot(left, ybuf[t % 2, 0:rows, cols], 0, 0)
            room_t[:, :, :, :, cols] = product.reshape(4, 2, 2, RB, 256).astype(room_t.dtype)
            return 0

        lax.fori_loop(0, D // 256, column, 0)
        if t + 2 < len(jobs):
            load(t + 2)
        kind = items[i][0]
        if kind == "n":
            cores[t] = remote(room_t.at[:, :, 1 - c], rc[i], csend.at[t], crecv.at[t], cp)
        elif kind == "t":
            cores[t] = remote(room_t.at[:, :, 1 - c], rc[i].at[part], csend.at[t], crecv.at[t], cp)
        elif part % 2 == 0:
            cores[t] = remote(room_t, rc[i].at[part // 2], csend.at[t], crecv.at[t], cp)
        if t in cores:
            cores[t].start()

    def add_own(t):
        i, part, _, _, _ = jobs[t]
        kind, mine = items[i][0], room(t)
        if kind == "w":
            if part % 2 == 0:
                return False
            cores[at[i, part - 1]].wait_recv()
            add_into(rc[i].at[part // 2], mine, rc[i].at[part // 2])
            return part == 3
        cores[t].wait_recv()
        dst = rc[i] if kind == "n" else rc[i].at[part]
        add_into(dst, mine.at[:, :, c], dst)
        return kind == "n" or part == 3

    def views(i):
        kind, h = items[i][0], half(i)
        r, a, b = rc[i], r1a[i], r1b[i]
        here, there = lanes(x), lanes(1 - x)
        if kind == "n":
            one = (r.at[:, 1 - y, 0:h, :], r.at[:, :, h:RB, there], r.at[:, y, 0:h, :], r.at[:, :, h:RB, here])
            two = (a.at[:, :, there], b.at[:, 1 - y], a.at[:, :, here], b.at[:, y])
            parts = (s3[i].at[:, 0:h, :], s3[i].at[:, h:RB, :])
        elif kind == "t":
            up, down = pl.ds(2 * y, 2), pl.ds(2 * (1 - y), 2)
            one = (r.at[:, down, 0], r.at[:, :, 1, :, there], r.at[:, up, 0], r.at[:, :, 1, :, here])
            two = (a.at[:, :, :, there], b.at[:, down], a.at[:, :, :, here], b.at[:, up])
            parts = (s3[i].at[:, 0], s3[i].at[:, 1])
        else:
            one = (r.at[:, :, 1 - y, 0], r.at[1 - x, :, :, 1], r.at[:, :, y, 0], r.at[x, :, :, 1])
            two = (a.at[1 - x], b.at[:, 1 - y], a.at[x], b.at[:, y])
            parts = (s3[i].at[:, 0], s3[i].at[:, 1])
        return one, two, parts

    def send_1(i):
        (over_y, over_x, _, _), _, _ = views(i)
        ones[i] = [
            start(remote(over_y, r1a[i], ysend.at[i, 0], yrecv.at[i, 0], yp)),
            start(remote(over_x, r1b[i], xsend.at[i, 0], xrecv.at[i, 0], xp)),
        ]

    def send_2(i):
        (_, _, stay_a, stay_b), (over_x, over_y, _, _), _ = views(i)
        ones[i][0].wait_recv()
        add_into(r1a[i], stay_a, r1a[i])
        first = start(remote(over_x, r2a[i], xsend.at[i, 1], xrecv.at[i, 1], xp))
        ones[i][1].wait_recv()
        add_into(r1b[i], stay_b, r1b[i])
        twos[i] = [first, start(remote(over_y, r2b[i], ysend.at[i, 1], yrecv.at[i, 1], yp))]

    def send_z(i):
        _, (_, _, stay_a, stay_b), (part_a, part_b) = views(i)
        twos[i][0].wait_recv()
        add_into(part_a, stay_a, r2a[i])
        twos[i][1].wait_recv()
        add_into(part_b, stay_b, r2b[i])
        threes[i] = [
            start(remote(s3[i].at[(z + j + 1) % 4], rz[i].at[j], zsend.at[i, j], zrecv.at[i, j], zs[j]))
            for j in range(3)
        ]

    finals = []

    def finish(i):
        kind, _, out, tap = items[i]
        for copy in threes[i]:
            copy.wait_recv()
        acc = s3[i][z].astype(F32)
        for j in range(3):
            acc = acc + rz[i][j].astype(F32)
        dst = outs[out] if tap is None else outs[out].at[tap]
        if kind in "wm":
            dst[...] = acc
            return
        mine = acc[..., : LANES // 2]
        theirs = acc[..., LANES // 2 :]
        keep = jnp.where(c == 0, mine, theirs)
        other = jnp.where(c == 0, theirs, mine)
        if kind == "n":
            sbuf[i][...] = other
            dst[c] = keep
            finals.append(start(remote(sbuf[i], dst.at[c], fsend.at[i], frecv.at[i], cp)))
            return
        for a in (0, 1):
            for b in (0, 1):
                dst[b, a, c] = keep[a, b]
                sbuf[i][b, a] = other[a, b]
        finals.append(start(remote(sbuf[i], dst.at[:, :, c], fsend.at[i], frecv.at[i], cp)))

    g = [i for i in range(n) if items[i][0] == "m"][0]
    last = len(jobs)
    theirs = start(remote(ins[-1].at[:, 1 - c], rc[g], csend.at[last], crecv.at[last], cp))
    mine = pltpu.make_async_copy(ins[-1].at[:, c], given, loads.at[0, 2])
    mine.start()
    load(0)
    load(1)
    queue = [[], [], []]
    steps = (send_2, send_z, finish)

    def advance(keep):
        for k in (2, 1, 0):
            while len(queue[k]) > keep:
                i = queue[k].pop(0)
                steps[k](i)
                if k < 2:
                    queue[k + 1].append(i)

    mine.wait()
    for t in range(last + 1):
        if t < last:
            compute(t)
        if t == 1:
            theirs.wait_recv()
            add_into(rc[g], given, rc[g])
            send_1(g)
            queue[0].append(g)
        if t >= 1 and add_own(t - 1):
            i = jobs[t - 1][0]
            send_1(i)
            queue[0].append(i)
        advance(LAG)
    for keep in range(LAG - 1, -1, -1):
        advance(keep)
    while queue[0] or queue[1] or queue[2]:
        advance(0)
    for copy in finals:
        copy.wait_recv()
    for copy in started:
        copy.wait_send()
    for t in cores:
        if t + RING >= last or items[jobs[t][0]][1] == F32:
            cores[t].wait_send()


RING = 3
LAG = 1


def reduce_fast(items, jobs, ins, out_shapes):
    n, m = len(items), len(jobs)
    sem = pltpu.SemaphoreType.DMA
    groups = [[] for _ in range(8)]
    for i, (kind, dtype, _, _) in enumerate(items):
        for group, shape in zip(groups, item_shapes(kind, halves_of(i))):
            group.append(pltpu.VMEM(shape, dtype))
        last = {"n": (RB, LANES // 2), "t": (2, 2, RB, LANES // 2)}.get(kind, (8, 128))
        groups[7].append(pltpu.VMEM(last, F32))
    scratch = [s for group in groups for s in group]
    scratch += [
        pltpu.VMEM((RING, 4, 2, 2, RB, D), BF),
        pltpu.VMEM((4, 2, 2, RB, D), F32),
        pltpu.VMEM((2, 4, 2, 2, RB, 128), BF),
    ]
    most = max(j[4] for j in jobs)
    scratch += [pltpu.VMEM((2, most, D), BF)] * 2
    scratch += [sem((2, 3)), sem((m + 1,)), sem((m + 1,))]
    scratch += [sem((n, 2))] * 4 + [sem((n, 3))] * 2 + [sem((n,))] * 2
    vmem = pl.BlockSpec(memory_space=pltpu.VMEM)
    return pl.pallas_call(
        functools.partial(reduce_kernel, items, jobs, len(ins), len(out_shapes)),
        out_shape=[jax.ShapeDtypeStruct(s, F32) for s in out_shapes],
        in_specs=[pl.BlockSpec(memory_space=pl.ANY)] * len(ins),
        out_specs=[vmem] * len(out_shapes),
        scratch_shapes=scratch,
        compiler_params=pltpu.CompilerParams(
            collective_id=2, has_side_effects=True, vmem_limit_bytes=62 << 20
        ),
    )(*ins)


def lanes_of(pair):
    return pl.ds(pl.multiple_of(pair * PAIR, PAIR), PAIR)


def clip_partners():
    d, s = lax.axis_index("dp"), lax.axis_index("seq")
    x, c = s // 2, s % 2
    return (d, (1 - x) * 2 + c), (d, x * 2 + 1 - c)


def greet_pair(xp, cp):
    barrier = pltpu.get_barrier_semaphore()
    for dev in (xp, cp):
        pl.semaphore_signal(barrier, inc=1, device_id=dev, device_id_type=MESH)
    pl.semaphore_wait(barrier, 2)


def forward_head(q_one, k_slab, v_slab, half, count):
    s = masked(tdot(k_slab, q_one, 1, 1), count)
    top = jnp.max(s, axis=0, keepdims=True)
    e = jnp.exp(s - top)
    total = jnp.sum(e, axis=0, keepdims=True)
    mixed = tdot(v_slab, e.astype(BF), 0, 0)[half * HEAD : (half + 1) * HEAD]
    return mixed / total, top + jnp.log(total)


def forward_pair(pair, q, k, v, o, lse, count):
    at = lanes_of(pair)
    q_slab, k_slab, v_slab = q[:, at], k[:, at], v[:, at]
    both = []
    for half in (0, 1):
        mixed, log_sum = forward_head(one_head(q_slab, half), k_slab, v_slab, half, count)
        both.append(mixed)
        lse[pl.ds(2 * pair + half, 1), :] = log_sum
    o[:, at] = jnp.concatenate(both, axis=0).T.astype(o.dtype)


def backward_pair(pair, q, k, v, up, lse, dq, dk, dv, count, known):
    at = lanes_of(pair)
    q_slab, k_slab, v_slab, u_slab = q[:, at], k[:, at], v[:, at], up[:, at]
    both, dk_sum, dv_sum = [], 0.0, 0.0
    for half in (0, 1):
        row = pl.ds(2 * pair + half, 1)
        q_one, u_one = one_head(q_slab, half), one_head(u_slab, half)
        p = jnp.exp(masked(tdot(k_slab, q_one, 1, 1), count) - lse[row, :])
        dp = tdot(v_slab, u_one, 1, 1)
        if known is None:
            mass = jnp.sum(p, axis=0, keepdims=True)
            inner = jnp.sum(p * dp, axis=0, keepdims=True) / mass
        else:
            inner = known[row, :]
        ds = (p * (dp - inner)).astype(BF)
        dv_sum = dv_sum + tdot(p.astype(BF), u_one, 1, 0)
        dk_sum = dk_sum + tdot(ds, q_one, 1, 0)
        both.append(tdot(k_slab, ds, 0, 0)[half * HEAD : (half + 1) * HEAD])
    dq[:, at] = jnp.concatenate(both, axis=0).T.astype(dq.dtype)
    dk[:, at] = dk_sum.astype(dk.dtype)
    dv[:, at] = dv_sum.astype(dv.dtype)


def attend_kernel(causal, *refs):
    count = refs[0] if causal else None
    q, k, v, o, lse = refs[1:] if causal else refs

    def step(pair, _):
        forward_pair(pair, q, k, v, o, lse, count)
        return 0

    lax.fori_loop(0, HEADS // 2, step, 0)


def clip_attend_kernel(q, k, v, o, lse, k_all, v_all, xsend, xrecv, csend, crecv):
    xp, cp = clip_partners()
    r = q.shape[0]
    greet_pair(xp, cp)
    pairs = HEADS // 2

    def across(pair):
        at = lanes_of(pair)
        return [
            remote(src.at[:, at], dst.at[r : 2 * r, at], xsend.at[j, pair], xrecv.at[j, pair], xp)
            for j, (src, dst) in enumerate(((k, k_all), (v, v_all)))
        ]

    def beside(pair):
        at = lanes_of(pair)
        return [
            remote(a.at[0 : 2 * r, at], a.at[2 * r : 4 * r, at], csend.at[j, pair], crecv.at[j, pair], cp)
            for j, a in enumerate((k_all, v_all))
        ]

    for pair in range(pairs):
        for copy in across(pair):
            copy.start()
    k_all[0:r, :] = k[...]
    v_all[0:r, :] = v[...]

    def pass_on(pair):
        for copy in across(pair):
            copy.wait_recv()
        for copy in beside(pair):
            copy.start()

    pass_on(0)

    def step(pair, _):
        @pl.when(pair + 1 < pairs)
        def _():
            pass_on(pair + 1)

        for copy in beside(pair):
            copy.wait_recv()
        forward_pair(pair, q, k_all, v_all, o, lse, None)
        return 0

    lax.fori_loop(0, pairs, step, 0)
    for pair in range(pairs):
        for copy in across(pair) + beside(pair):
            copy.wait_send()


def clip_back_kernel(q, k, v, up, lse, dq, dk, dv, *refs):
    k_sum, v_sum, k_near, v_near, k_far, v_far, xsend, xrecv, csend, crecv = refs
    xp, cp = clip_partners()
    r = q.shape[0]
    greet_pair(xp, cp)
    pairs = HEADS // 2
    sums, nears, fars, outs = (k_sum, v_sum), (k_near, v_near), (k_far, v_far), (dk, dv)

    def beside(pair):
        at = lanes_of(pair)
        return [
            remote(sums[j].at[2 * r : 4 * r, at], nears[j].at[:, at], csend.at[j, pair], crecv.at[j, pair], cp)
            for j in (0, 1)
        ]

    def across(pair):
        at = lanes_of(pair)
        return [
            remote(sums[j].at[r : 2 * r, at], fars[j].at[:, at], xsend.at[j, pair], xrecv.at[j, pair], xp)
            for j in (0, 1)
        ]

    def step(t, _):
        @pl.when(t < pairs)
        def _():
            backward_pair(t, q, k, v, up, lse, dq, k_sum, v_sum, None, None)
            for copy in beside(t):
                copy.start()

        @pl.when((t >= 1) & (t <= pairs))
        def _():
            pair = t - 1
            at = lanes_of(pair)
            for copy in beside(pair):
                copy.wait_recv()
            for j in (0, 1):
                near = sums[j][0 : 2 * r, at].astype(F32) + nears[j][:, at].astype(F32)
                sums[j][0 : 2 * r, at] = near.astype(BF)
            for copy in across(pair):
                copy.start()

        @pl.when(t >= 2)
        def _():
            pair = t - 2
            at = lanes_of(pair)
            for copy in across(pair):
                copy.wait_recv()
            for j in (0, 1):
                total = sums[j][0:r, at].astype(F32) + fars[j][:, at].astype(F32)
                outs[j][:, at] = total.astype(BF)

        return 0

    lax.fori_loop(0, pairs + 2, step, 0)
    for pair in range(pairs):
        for copy in across(pair) + beside(pair):
            copy.wait_send()


def clip_peers():
    d, s = lax.axis_index("dp"), lax.axis_index("seq")
    return [(d, lax.rem(s + j, 4)) for j in (1, 2, 3)], s


def greet_peers(peers):
    barrier = pltpu.get_barrier_semaphore()
    for dev in peers:
        pl.semaphore_signal(barrier, inc=1, device_id=dev, device_id_type=MESH)
    pl.semaphore_wait(barrier, 3)


def cross_kernel(q, k, v, parts, lses, o, osend, orecv, lsend, lrecv):
    peers, me = clip_peers()
    greet_peers(peers)
    r = parts.shape[1]
    pairs = HEADS // 2
    rows = lambda s: pl.ds(pl.multiple_of(s * r, 16), r)

    def tell(j, pair):
        at = lanes_of(pair)
        return remote(
            o.at[rows(peers[j][1]), at], parts.at[j + 1, :, at], osend.at[j, pair], orecv.at[j, pair], peers[j]
        )

    def step(pair, _):
        forward_pair(pair, q, k, v, o, lses.at[0], None)
        for j in range(3):
            tell(j, pair).start()
        return 0

    lax.fori_loop(0, pairs, step, 0)
    sums = [remote(lses.at[0], lses.at[j + 1], lsend.at[j], lrecv.at[j], peers[j]) for j in range(3)]
    for copy in sums:
        copy.start()
    parts[0] = o[rows(me), :]
    for copy in sums + [tell(j, pair) for j in range(3) for pair in range(pairs)]:
        copy.wait_recv()
    for copy in sums + [tell(j, pair) for j in range(3) for pair in range(pairs)]:
        copy.wait_send()


def cross_back_kernel(q, k, v, up, lse, dq, dk, dv, sums, known, mine, theirs, ssend, srecv, dsend, drecv):
    peers, me = clip_peers()
    greet_peers(peers)
    r = dq.shape[0]
    pairs = HEADS // 2
    rows = lambda s: pl.ds(pl.multiple_of(s * r, 16), r)

    def first(pair, _):
        at = lanes_of(pair)
        q_slab, k_slab, v_slab, u_slab = q[:, at], k[:, at], v[:, at], up[:, at]
        for half in (0, 1):
            row = 2 * pair + half
            p = jnp.exp(tdot(k_slab, one_head(q_slab, half), 1, 1) - lse[pl.ds(row, 1), :])
            dp = tdot(v_slab, one_head(u_slab, half), 1, 1)
            sums[0, pl.ds(row, 1), :] = jnp.sum(p, axis=0, keepdims=True)
            sums[0, pl.ds(16 + row, 1), :] = jnp.sum(p * dp, axis=0, keepdims=True)
        return 0

    sums[0] = jnp.zeros(sums.shape[1:], F32)
    lax.fori_loop(0, pairs, first, 0)
    shared = [remote(sums.at[0], sums.at[j + 1], ssend.at[j], srecv.at[j], peers[j]) for j in range(3)]
    for copy in shared:
        copy.start()
    for copy in shared:
        copy.wait_recv()
    total = sums[0] + sums[1] + sums[2] + sums[3]
    known[...] = total[16 : 16 + HEADS] / total[0:HEADS]

    def tell(j, pair):
        at = lanes_of(pair)
        return remote(
            mine.at[rows(peers[j][1]), at], theirs.at[j, :, at], dsend.at[j, pair], drecv.at[j, pair], peers[j]
        )

    def second(pair, _):
        backward_pair(pair, q, k, v, up, lse, mine, dk, dv, None, known)
        for j in range(3):
            tell(j, pair).start()
        return 0

    lax.fori_loop(0, pairs, second, 0)
    for j in range(3):
        for pair in range(pairs):
            tell(j, pair).wait_recv()
    dq[...] = mine[rows(me), :] + theirs[0] + theirs[1] + theirs[2]
    for copy in shared + [tell(j, pair) for j in range(3) for pair in range(pairs)]:
        copy.wait_send()


def clip_rows_back_kernel(count, q, k, v, own, lse, dq, dk, dv, up, send, recv):
    peers, me = clip_peers()
    greet_peers(peers)
    r = own.shape[0]
    here = pl.ds(pl.multiple_of(me * r, 16), r)

    def tell(j, pair):
        at = lanes_of(pair)
        return remote(own.at[:, at], up.at[here, at], send.at[j, pair], recv.at[j, pair], peers[j])

    every = [tell(j, pair) for pair in range(HEADS // 2) for j in range(3)]
    for copy in every:
        copy.start()
    up[here, :] = own[...]

    def step(pair, _):
        for j in range(3):
            tell(j, pair).wait_recv()
        backward_pair(pair, q, k, v, up, lse, dq, dk, dv, count, None)
        return 0

    lax.fori_loop(0, HEADS // 2, step, 0)
    for copy in every:
        copy.wait_send()


def local_call(kernel, out_shape, args, cost, count=None, scratch=(), barrier=None):
    vmem = pl.BlockSpec(memory_space=pltpu.VMEM)
    specs = [vmem] * len(args)
    if count is not None:
        specs, args = [pl.BlockSpec(memory_space=pltpu.SMEM)] + specs, [count] + args
    params = dict(vmem_limit_bytes=56 << 20)
    if barrier is not None:
        params.update(collective_id=barrier, has_side_effects=True)
    return pl.pallas_call(
        kernel,
        out_shape=[jax.ShapeDtypeStruct(s, t) for s, t in out_shape],
        in_specs=specs,
        out_specs=[vmem] * len(out_shape),
        scratch_shapes=list(scratch),
        cost_estimate=pl.CostEstimate(flops=cost, bytes_accessed=8 << 20, transcendentals=0),
        compiler_params=pltpu.CompilerParams(**params),
    )(*args)


def rows_cost(q, k):
    return 8 * q.shape[0] * k.shape[0] * D


def attend(q, k, v, count=None):
    shapes = [(q.shape, BF), ((HEADS, q.shape[0]), F32)]
    kernel = functools.partial(attend_kernel, count is not None)
    return local_call(kernel, shapes, [q, k, v], rows_cost(q, k), count)


def cross_attend(q, k, v):
    r = q.shape[0] // 4
    sem = pltpu.SemaphoreType.DMA
    scratch = [pltpu.VMEM(q.shape, BF)] + [sem((3, HEADS // 2))] * 2 + [sem((3,))] * 2
    shapes = [((4, r, D), BF), ((4, HEADS, q.shape[0]), F32)]
    return local_call(cross_kernel, shapes, [q, k, v], rows_cost(q, k), None, scratch, 6)


def cross_back(q, k, v, up, lse):
    slots = q.shape[0]
    sem = pltpu.SemaphoreType.DMA
    scratch = [pltpu.VMEM((4, 32, slots), F32), pltpu.VMEM((HEADS, slots), F32)]
    scratch += [pltpu.VMEM((slots, D), F32), pltpu.VMEM((3, slots // 4, D), F32)]
    scratch += [sem((3,))] * 2 + [sem((3, HEADS // 2))] * 2
    shapes = [((slots // 4, D), F32), (k.shape, BF), (k.shape, BF)]
    return local_call(cross_back_kernel, shapes, [q, k, v, up, lse], 4 * rows_cost(q, k), None, scratch, 7)


def clip_rows_back(q, k, v, own, lse, count):
    scratch = [pltpu.VMEM(q.shape, BF)] + [pltpu.SemaphoreType.DMA((3, HEADS // 2))] * 2
    args = [q, k, v, own, lse]
    return local_call(clip_rows_back_kernel, [(q.shape, BF)] * 3, args, 3 * rows_cost(q, k), count, scratch, 8)


def clip_attend(q, k, v):
    r = k.shape[0]
    shapes = [(q.shape, BF), ((HEADS, r), F32), ((4 * r, D), BF), ((4 * r, D), BF)]
    sems = [pltpu.SemaphoreType.DMA((2, HEADS // 2))] * 4
    return local_call(clip_attend_kernel, shapes, [q, k, v], 4 * rows_cost(q, k), None, sems, 3)


def clip_attend_back(q, k_all, v_all, up, lse):
    r = q.shape[0]
    scratch = [pltpu.VMEM((4 * r, D), BF)] * 2 + [pltpu.VMEM((2 * r, D), BF)] * 2
    scratch += [pltpu.VMEM((r, D), BF)] * 2 + [pltpu.SemaphoreType.DMA((2, HEADS // 2))] * 4
    args = [q, k_all, v_all, up, lse]
    return local_call(clip_back_kernel, [(q.shape, BF)] * 3, args, 3 * rows_cost(q, k_all), None, scratch, 4)


def mlp_kernel(stream, gain, bias, expand, contract, normed, pre, hidden, out):
    @pl.when(pl.program_id(0) == 0)
    def _():
        normed[...] = norm(stream[...], gain[...], bias[...])
        out[...] = stream[...]

    before = tdot(normed[...], expand[0], 1, 0)
    pre[0] = before
    after = gelu(before).astype(BF)
    hidden[0] = after
    out[...] += tdot(after, contract[0], 1, 0)


def mlp_back_kernel(up, stream, gain, pre, expand, contract, out, d_low, d_pre, d_gain, d_bias, total):
    s = pl.program_id(0)

    @pl.when(s == 0)
    def _():
        d_low[...] = up[...].astype(BF)
        total[...] = jnp.zeros_like(total)

    d_hidden = low(tdot(d_low[...], contract[0], 1, 1))
    grad = (gelu_slope(pre[0]) * d_hidden).astype(BF)
    d_pre[0] = grad
    total[...] += tdot(grad, expand[0], 1, 1)

    @pl.when(s == pl.num_programs(0) - 1)
    def _():
        hat, inv = norm_parts(stream[...])
        g = total[...] * gain[...]
        mean = lambda v: jnp.mean(v, axis=-1, keepdims=True)
        out[...] = up[...] + inv * (g - mean(g) - hat * mean(g * hat))
        d_gain[...] = jnp.sum(total[...] * hat, axis=0, keepdims=True)
        d_bias[...] = jnp.sum(total[...], axis=0, keepdims=True)


def blocks(kernel, grid, ins, outs, args, cost, scratch=()):
    def spec(shape, cut):
        if cut:
            return pl.BlockSpec((1,) + shape[1:], lambda s: (s,) + (0,) * (len(shape) - 1))
        return pl.BlockSpec(shape, lambda s: (0,) * len(shape))

    return pl.pallas_call(
        kernel,
        grid=(grid,),
        out_shape=[jax.ShapeDtypeStruct(s, t) for s, t, _ in outs],
        in_specs=[spec(a.shape, cut) for a, cut in zip(args, ins)],
        out_specs=[spec(s, cut) for s, _, cut in outs],
        scratch_shapes=list(scratch),
        cost_estimate=pl.CostEstimate(flops=cost, bytes_accessed=16 << 20, transcendentals=0),
        compiler_params=pltpu.CompilerParams(vmem_limit_bytes=48 << 20),
    )(*args)


def mlp(stream, gain, bias, expand, contract):
    n, (r, _) = expand.shape[0], stream.shape
    outs = [((r, D), BF, False), ((n, r, D), F32, True), ((n, r, D), BF, True), ((r, D), F32, False)]
    args = [stream, gain[None], bias[None], expand, contract.reshape(n, D, D)]
    return blocks(mlp_kernel, n, [False] * 3 + [True] * 2, outs, args, 4 * n * r * D * D)


def mlp_backward(up, stream, gain, pre, expand, contract):
    n, (r, _) = expand.shape[0], stream.shape
    outs = [((r, D), F32, False), ((r, D), BF, False), ((n, r, D), BF, True)]
    outs += [((1, D), F32, False)] * 2
    args = [up, stream, gain[None], pre, expand, contract.reshape(n, D, D)]
    scratch = [pltpu.VMEM((r, D), F32)]
    return blocks(mlp_back_kernel, n, [False] * 3 + [True] * 3, outs, args, 4 * n * r * D * D, scratch)


SQUARE = (4, 5, 6, 7, 18, 19, 20, 21, 24, 25, 26, 27)
TALL = (11, 31)
BROAD = (10, 30)
VECTORS = tuple(i for i in range(32) if KINDS[i] == "v")


ROW_PAD = 400
CHUNK = 80
SMALL_ROWS = 96


def gather_split(i, rows):
    return rows // 2 if rows % 32 == 0 else 16 + 16 * (i % 2)


def stem_kernel(plan, inputs, outputs, rows_held, *refs):
    n = len(plan)
    ins, refs = refs[:inputs], refs[inputs:]
    patches, angles, table, refs = refs[:3], refs[3], refs[4], refs[5:]
    outs, refs = refs[:outputs], refs[outputs:]
    even_pre, odd_pre, even, odd, even_next, second, stream, normed, q, k_all, v_all, o, lse, vec = refs[:14]
    looked, refs = refs[14], refs[:14] + refs[15:]
    got, stage, refs = refs[14 : 14 + n], refs[14 + n : 14 + 2 * n], refs[14 + 2 * n :]
    small, weights, k_own, v_own, found, heard, strips = refs[:7]
    lsem, zsend, zrecv, xsend, xrecv, ysend, yrecv, csend, crecv, psend, precv = refs[7:18]
    wsem, kxs, kxr, kcs, kcr, tsend, trecv, usend, urecv = refs[18:]
    z, y, x, c = where_am_i()
    zs, yp, xp, cp = partners(z, y, x, c)
    greet(zs, yp, xp, cp)
    dst, src, swaps = [], [], []
    for i, (k, rows, out, tap, kind) in enumerate(plan):
        dst.append(outs[out] if tap is None else outs[out].at[tap])
        src.append(ins[k] if tap is None else ins[k].at[tap])
        swaps.append(None)
        if kind == "n":
            theirs = src[i].at[pl.ds(pl.multiple_of((1 - c) * rows, 16), rows), :]
            swaps[i] = remote(theirs, got[i], psend.at[i], precv.at[i], cp)
            swaps[i].start()

    def item(i):
        rows, wide = plan[i][1], plan[i][4] == "w"
        h = gather_split(i, rows)
        return rows, wide, slice(0, h), slice(h, rows)

    stages = {}

    def start(i, key, copies):
        for cpy in copies:
            cpy.start()
        stages[i, key] = copies

    def send_z(i):
        rows, wide, _, _ = item(i)
        block = src[i]
        if not wide:
            mine = src[i][pl.ds(pl.multiple_of(c * rows, 16), rows), :]
            swaps[i].wait_recv()
            theirs = got[i][...]
            stage[i][...] = jnp.concatenate(
                [jnp.where(c == 0, mine, theirs), jnp.where(c == 0, theirs, mine)], axis=1
            )
            block = stage[i]
        here = spot(dst[i], wide, z, y, x, c, slice(None))
        start(i, 0, [remote(block, here, zsend.at[i, j], zrecv.at[i, j], zs[j]) for j in range(3)])
        start(i, 4, [pltpu.make_async_copy(block, here, lsem.at[i])])

    def send_1(i):
        rows, wide, a, b = item(i)
        for cpy in stages[i, 0]:
            cpy.wait_recv()
        stages[i, 4][0].wait()
        ax = spot(dst[i], wide, None, y, x, c, a)
        by = spot(dst[i], wide, None, y, x, c, b)
        start(
            i,
            1,
            [
                remote(ax, ax, xsend.at[i, 0], xrecv.at[i, 0], xp),
                remote(by, by, ysend.at[i, 0], yrecv.at[i, 0], yp),
            ],
        )

    def send_2(i):
        rows, wide, a, b = item(i)
        for cpy in stages[i, 1]:
            cpy.wait_recv()
        ay = spot(dst[i], wide, None, y, None, c, a)
        bx = spot(dst[i], wide, None, None, x, c, b)
        start(
            i,
            2,
            [
                remote(ay, ay, ysend.at[i, 1], yrecv.at[i, 1], yp),
                remote(bx, bx, xsend.at[i, 1], xrecv.at[i, 1], xp),
            ],
        )

    def send_core(i):
        rows, wide, a, b = item(i)
        for cpy in stages[i, 2]:
            cpy.wait_recv()
        half = spot(dst[i], wide, None, None, None, c, slice(None))
        start(i, 3, [remote(half, half, csend.at[i], crecv.at[i], cp)])

    arrived = set()

    def arrive(i):
        if i not in arrived:
            stages[i, 3][0].wait_recv()
            arrived.add(i)

    r = q.shape[0]
    pairs = HEADS // 2

    def fetch(items, slots):
        copies = []
        for i, slot in zip(items, slots):
            arrive(i)
            copies.append(pltpu.make_async_copy(dst[i], weights.at[slot], wsem.at[slot]))
            copies[-1].start()
        for cpy in copies:
            cpy.wait()

    def weight(slot):
        return weights[slot].reshape(D, D)

    def open_small():
        arrive(0)
        copy = pltpu.make_async_copy(dst[0], small, wsem.at[3])
        copy.start()
        copy.wait()
        cells = []
        for zy in range(8):
            for s in range(4):
                cells.append(small[s // 2, s % 2, zy // 2, zy % 2, 64:80, 0:24].astype(F32))
        vec[...] = jnp.concatenate(cells, axis=1)

    def convolve(patch, pre, act, edge):
        def one(t, _):
            rows = pl.ds(pl.multiple_of(t * CHUNK, 16), CHUNK)
            left = patch[rows, :]
            cells = []
            for zy in range(8):
                taps = [small[s // 2, s % 2, zy // 2, zy % 2, 0:64, :] for s in range(4)]
                cells.append(tdot(left, jnp.concatenate(taps, axis=0), 1, 0)[:, 0:96])
            before = jnp.concatenate(cells, axis=1)
            if pre is not None:
                pre[rows, :] = before
            after = gelu(before)
            if edge is not None:
                row, outside = edge
                at = t * CHUNK + lax.broadcasted_iota(jnp.int32, after.shape, 0)
                after = jnp.where((at == row) & outside, 0.0, after)
            act[rows, :] = after.astype(BF)
            return 0

        lax.fori_loop(0, ROW_PAD // CHUNK, one, 0)

    me = 2 * x + c
    part = 128
    slots = looked.shape[0]
    eighth = slots // 8

    def other_clip(m):
        return lax.rem(z + m // 2, 4), lax.rem(y + m % 2, 2)

    def tell(m):
        zt, yt = other_clip(m)
        return remote(found.at[m], heard.at[m], tsend.at[m], trecv.at[m], (zt * 2 + yt, 2 * x + c))

    def look_up(m):
        zt, yt = other_clip(m)
        cells = []
        for s in range(4):
            for half in (0, 1):
                code = small[s // 2, s % 2, zt, yt, 0:64, 96:128].astype(F32)[0:eighth]
                cells.append(code[:, 2 * half : 2 * half + 1] * 256.0 + code[:, 2 * half + 1 : 2 * half + 2])
        first = (z * 2 + y) * rows_held
        place = jnp.concatenate(cells, axis=0).astype(jnp.int32) - first

        def one(k, total):
            lane = lax.broadcasted_iota(jnp.int32, (slots, 384), 1) + k * 384
            hot = jnp.where((lane == place) & (lane < rows_held), 1.0, 0.0).astype(BF)
            return total + tdot(hot, table[pl.ds(pl.multiple_of(k * 384, 384), 384), :], 1, 0)

        total = lax.fori_loop(0, table.shape[0] // 384, one, jnp.zeros((slots, D // 4), F32))
        if m == 0:
            heard[0] = total.astype(BF)
        else:
            found[m] = total.astype(BF)
            tell(m).start()

    def strip(over):
        if over == 0:
            return remote(strips.at[x, c], strips.at[x, c], usend.at[0], urecv.at[0], xp)
        return remote(strips.at[:, c], strips.at[:, c], usend.at[1], urecv.at[1], cp)

    def sum_found():
        total = heard[0].astype(F32)
        for m in range(1, 8):
            tell(m).wait_recv()
            total = total + heard[m].astype(F32)
        strips[x, c] = total.astype(BF)
        strip(0).start()

    def pass_strips():
        strip(0).wait_recv()
        strip(1).start()

    def join_strips():
        strip(1).wait_recv()
        looked[...] = jnp.concatenate([strips[s // 2, s % 2] for s in range(4)], axis=1)

    def convolve_second(t):
        rows = slice(t * part, (t + 1) * part)
        total = tdot(even[rows, :], weight(0), 1, 0)
        total = total + tdot(odd[rows, :], weight(1), 1, 0)
        total = total + tdot(even_next[rows, :], weight(2), 1, 0)
        second[rows, :] = total
        out = gelu(total) + angles[rows, :]
        stream[rows, :] = out
        normed[rows, :] = norm(out, vec[0:1, :], vec[1:2, :])

    def project():
        for t in range(r // part):
            rows = slice(t * part, (t + 1) * part)
            left = normed[rows, :]
            q[rows, :] = (tdot(left, weight(0), 1, 0) * SCALE).astype(BF)
            k_own[rows, :] = tdot(left, weight(1), 1, 0).astype(BF)
            v_own[rows, :] = tdot(left, weight(2), 1, 0).astype(BF)
        for pair in range(pairs):
            for cpy in across(pair):
                cpy.start()
        k_all[0:r, :] = k_own[...]
        v_all[0:r, :] = v_own[...]

    def across(pair):
        at = lanes_of(pair)
        return [
            remote(a.at[:, at], b.at[r : 2 * r, at], kxs.at[j, pair], kxr.at[j, pair], xp)
            for j, (a, b) in enumerate(((k_own, k_all), (v_own, v_all)))
        ]

    def beside(pair):
        at = lanes_of(pair)
        return [
            remote(a.at[0 : 2 * r, at], a.at[2 * r : 4 * r, at], kcs.at[j, pair], kcr.at[j, pair], cp)
            for j, a in enumerate((k_all, v_all))
        ]

    def pass_on(pair):
        for cpy in across(pair):
            cpy.wait_recv()
        for cpy in beside(pair):
            cpy.start()

    def attend_pair(pair):
        if pair + 1 < pairs:
            pass_on(pair + 1)
        for cpy in beside(pair):
            cpy.wait_recv()
        forward_pair(pair, q, k_all, v_all, o, lse, None)

    pieces = [
        open_small,
        lambda: convolve(patches[0], even_pre, even, (0, me == 0)),
        lambda: (look_up(0), look_up(1)),
        lambda: convolve(patches[1], odd_pre, odd, (r, me == 3)),
        lambda: (look_up(2), look_up(3)),
        lambda: convolve(patches[2], None, even_next, None),
        lambda: (look_up(4), look_up(5)),
        lambda: (fetch((1, 2, 3), (0, 1, 2)), convolve_second(0)),
    ]
    pieces += [functools.partial(convolve_second, t) for t in range(1, r // part)]
    pieces += [lambda: (fetch((4, 5, 6), (0, 1, 2)), project()), lambda: (look_up(6), look_up(7))]
    pieces += [lambda: (pass_on(0), sum_found()), lambda: (attend_pair(0), pass_strips())]
    pieces += [lambda: (attend_pair(1), join_strips())]
    pieces += [functools.partial(attend_pair, pair) for pair in range(2, pairs)]

    for t in range(n + AHEAD[2]):
        if t == 0:
            for i in range(min(n, AHEAD[3])):
                send_z(i)
        if t + AHEAD[3] < n:
            send_z(t + AHEAD[3])
        if 0 <= t - AHEAD[0] < n:
            send_1(t - AHEAD[0])
        if 0 <= t - AHEAD[1] < n:
            send_2(t - AHEAD[1])
        if 0 <= t - AHEAD[2] < n:
            send_core(t - AHEAD[2])
        if t >= PIECES_FROM and pieces:
            pieces.pop(0)()
    while pieces:
        pieces.pop(0)()
    for i in range(n):
        if swaps[i] is not None:
            swaps[i].wait_send()
        arrive(i)
        for key in range(4):
            for cpy in stages[i, key]:
                cpy.wait_send()
    for pair in range(pairs):
        for cpy in across(pair) + beside(pair):
            cpy.wait_send()
    for m in range(1, 8):
        tell(m).wait_send()
    strip(0).wait_send()
    strip(1).wait_send()


AHEAD = (0, 1, 3, 6)
PIECES_FROM = 5


def gather_and_stem(plan, ins, out_shapes, patches, angles, table, slots, rows_held):
    n, r = len(plan), angles.shape[0]
    sem = pltpu.SemaphoreType.DMA
    hbm, vmem = pl.BlockSpec(memory_space=pl.ANY), pl.BlockSpec(memory_space=pltpu.VMEM)
    got, stage = [], []
    for _, rows, _, _, kind in plan:
        got.append(pltpu.VMEM((rows, LANES // 2) if kind == "n" else (16, 128), BF))
        stage.append(pltpu.VMEM((rows, LANES) if kind == "n" else (16, 128), BF))
    sems = [sem((n,)), sem((n, 3)), sem((n, 3))] + [sem((n, 2))] * 4 + [sem((n,))] * 4
    made = [((ROW_PAD, D), F32)] * 2 + [((ROW_PAD, D), BF)] * 3 + [((r, D), F32)] * 2
    made += [((r, D), BF)] * 2 + [((4 * r, D), BF)] * 2 + [((r, D), BF), ((HEADS, r), F32), ((16, D), F32)]
    made += [((slots, D), BF)]
    held = [pltpu.VMEM((2, 2, 4, 2, SMALL_ROWS, 128), BF), pltpu.VMEM((3, 4, 2, 2, 48, D), BF)]
    held += [pltpu.VMEM((r, D), BF)] * 2 + [pltpu.VMEM((8, slots, D // 4), BF)] * 2
    held += [pltpu.VMEM((2, 2, slots, D // 4), BF)]
    return pl.pallas_call(
        functools.partial(stem_kernel, plan, len(ins), len(out_shapes), rows_held),
        out_shape=[jax.ShapeDtypeStruct(s, BF) for s in out_shapes]
        + [jax.ShapeDtypeStruct(s, t) for s, t in made],
        in_specs=[vmem] * (len(ins) + 5),
        out_specs=[hbm] * len(out_shapes) + [vmem] * len(made),
        scratch_shapes=got + stage + held + sems + [sem((4,))] + [sem((2, HEADS // 2))] * 4 + [sem((8,))] * 2 + [sem((2,))] * 2,
        compiler_params=pltpu.CompilerParams(
            collective_id=1, has_side_effects=True, vmem_limit_bytes=60 << 20
        ),
    )(*ins, *patches, angles, table)


def small_block(shards, ids):
    w = shards[0]
    t, i, o = w.shape
    halves = ids.reshape(2, -1)
    codes = jnp.stack([halves[0] // 256, halves[0] % 256, halves[1] // 256, halves[1] % 256], axis=1)
    codes = jnp.pad(codes.astype(BF), ((0, 64 - codes.shape[0]), (0, 32 - 4)))
    top = jnp.concatenate([jnp.pad(w.reshape(t * i, o), ((0, 64 - t * i), (0, 0))), codes], axis=1)
    rows = jnp.stack([shards[k] for k in VECTORS])
    rows = jnp.pad(rows, ((0, SMALL_ROWS - 64 - rows.shape[0]), (0, 128 - rows.shape[1])))
    return jnp.concatenate([top, rows])


def patch_rows(patch, mels):
    p = patch.reshape(patch.shape[0], 3, 4, mels // 4).transpose(0, 2, 1, 3).reshape(patch.shape[0], 4, -1)
    p = jnp.pad(p, ((0, ROW_PAD - p.shape[0]), (0, 0), (0, 64 - p.shape[2])))
    return p.reshape(ROW_PAD, 256)


def gather_weights(shards, patches, angles, ids, table):
    plan, ins, shapes, at = [], [], [], {}
    for i in SQUARE + (1,) + TALL + (15,):
        w = shards[i]
        if i == 15:
            w = jnp.concatenate([w, jnp.zeros((-w.shape[0] % 32, w.shape[1]), BF)])
        rows = w.shape[-2] // 2
        for tap in range(3) if w.ndim == 3 else (None,):
            at[i, tap] = len(plan)
            plan.append((len(ins), rows, len(shapes), None, "n"))
            ins.append(w if tap is None else w[tap])
            shapes.append((4, 2, 2, rows, D))
    for i in BROAD:
        at[i, None] = len(plan)
        plan.append((len(ins), shards[i].shape[0], len(shapes), None, "w"))
        ins.append(shards[i])
        shapes.append((2, 2, 4, 2) + shards[i].shape)
    at[0, None] = len(plan)
    plan.append((len(ins), SMALL_ROWS, len(shapes), None, "w"))
    ins.append(small_block(shards, ids))
    shapes.append((2, 2, 4, 2, SMALL_ROWS, 128))
    first = [at[0, None], at[1, 0], at[1, 1], at[1, 2], at[4, None], at[5, None], at[6, None]]
    order = first + [k for k in range(len(plan)) if k not in first]
    rows_held = table.shape[0]
    table = jnp.pad(table, ((0, -rows_held % 384), (0, 0)))
    outs = gather_and_stem([plan[k] for k in order], ins, shapes, patches, angles, table, 4 * ids.size, rows_held)
    outs, made = outs[: len(plan)], outs[len(plan) :]
    full = [None] * 32
    for i in SQUARE + TALL:
        full[i] = outs[at[i, None]].reshape(-1, D)
    full[1] = [outs[at[1, tap]].reshape(D, D) for tap in range(3)]
    r = shards[15].shape[0]
    full[15] = outs[at[15, None]].reshape(8, -1, D)[:, :r].reshape(8 * r, D)
    for i in BROAD:
        full[i] = outs[at[i, None]].reshape(4, D, D)
    t, a, b = shards[0].shape
    small = outs[at[0, None]]
    codes = small[..., : ids.size // 2, 96:100].astype(jnp.int32)
    all_ids = jnp.stack([codes[..., 2 * h] * 256 + codes[..., 2 * h + 1] for h in (0, 1)], axis=4)
    all_ids = all_ids.transpose(2, 3, 0, 1, 4, 5).reshape(-1)
    conv1 = small[..., : t * a, :b].reshape(2, 2, 4, 2, t, a, b)
    full[0] = conv1.transpose(4, 0, 1, 5, 2, 3, 6).reshape(t, 4 * a, 8 * b)
    for k, i in enumerate(VECTORS):
        full[i] = made[13][k]
    return full, made[:13], all_ids, made[14]


ORDER = (31, 30, 27, 24, 21, 18, 19, 20, 11, 10, 25, 26, 7, 4, 5, 6, 1)
EXACT = 25
HEAD_START = 1
MIX = 2


def reduce_grads(grads, shards):
    items, jobs, ins, shapes, seen = [], [], [], [], {}

    def place(v):
        if id(v) not in seen:
            seen[id(v)] = len(ins)
            ins.append(v)
        return seen[id(v)]

    for i in ORDER:
        left, right = grads[i]
        if i in TALL:
            jobs += [(len(items), s, place(left), place(right), left.shape[1]) for s in range(4)]
            items.append(("t", BF, len(shapes), None))
            shapes.append((2, 2, 2, RB, LANES // 2))
        elif i in BROAD:
            jobs += [(len(items), s, place(left), place(right), left.shape[0]) for s in range(4)]
            items.append(("w", BF, len(shapes), None))
            shapes.append((2, RB, D))
        elif i == 1:
            for tap, l in enumerate(left):
                jobs.append((len(items), 0, place(l), place(right), right.shape[0]))
                items.append(("n", BF, len(shapes), tap))
            shapes.append((3, 2, RB, LANES // 2))
        else:
            jobs.append((len(items), 0, place(left), place(right), left.shape[0]))
            items.append(("n", F32 if i == EXACT else BF, len(shapes), None))
            shapes.append((2, RB, LANES // 2))
    t, a, b = shards[0].shape
    conv1 = grads[0].reshape(t, 2, 2, a, 4, 2, b).transpose(1, 2, 4, 5, 0, 3, 6).reshape(2, 2, 4, 2, t * a, b)
    n = shards[VECTORS[0]].size
    vecs = jnp.stack([grads[i] for i in VECTORS]).reshape(-1, 4, 2, 2, 2, n).transpose(3, 4, 1, 2, 0, 5)
    none = ((0, 0),) * 4
    conv1 = jnp.pad(conv1.astype(BF), none + ((0, 64 - t * a), (0, 128 - b)))
    vecs = jnp.pad(vecs.astype(BF), none + ((0, SMALL_ROWS - 64 - len(VECTORS)), (0, 128 - n)))
    ins.append(jnp.concatenate([conv1, vecs], axis=4).reshape(2, 2, 4, 2, 2, RB, 128))
    items.append(("m", BF, len(shapes), None))
    shapes.append((2, RB, 128))
    small = [j for j in jobs if items[j[0]][0] == "n"]
    large = [j for j in jobs if items[j[0]][0] != "n"]
    jobs, large = small[:HEAD_START], list(large)
    for j in small[HEAD_START:]:
        jobs += large[:MIX] + [j]
        large = large[MIX:]
    jobs = jobs[:-1] + large + jobs[-1:]
    got = reduce_fast(items, jobs, ins, shapes)
    out = [None] * 32
    for i, v in zip(ORDER, got):
        out[i] = v.reshape(shards[i].shape)
    small = got[-1].reshape(SMALL_ROWS, 128)
    out[0] = small[: t * a, :b].reshape(t, a, b)
    for k, i in enumerate(VECTORS):
        out[i] = small[64 + k, :n]
    return out


def one_hot(ids, table):
    first = lax.axis_index("dp") * table.shape[0]
    return ((ids - first)[:, None] == jnp.arange(table.shape[0])[None, :]).astype(BF)


def body(mel_frames, token_ids, token_counts, *rest):
    shards, cotangent = list(rest[:32]), rest[32][0]
    table = shards[14]
    dps, seqs = lax.axis_size("dp"), lax.axis_size("seq")
    me = lax.axis_index("seq")
    slots = token_ids.shape[1]
    all_slots = slots * seqs
    frames = mel_frames.shape[1] // 2

    fast = dps == 8 and seqs == 4
    weights = shards[:14] + [None] + shards[15:]
    pairs = extended(mel_frames[0], 2).reshape(frames + 2, -1)
    mels = mel_frames.shape[2]
    n = frames + 1
    even_in = jnp.concatenate([pairs[:n], pairs[1:, :mels]], axis=1)
    odd_in = jnp.concatenate([pairs[:n, mels:], pairs[1:]], axis=1)
    angles = sinusoid(me * frames, frames)
    row = jnp.arange(n)[:, None]
    even_keep = (row > 0) | (me > 0)
    odd_keep = (row < n - 1) | (me < seqs - 1)
    if fast:
        patches = [patch_rows(p, mels) for p in (even_in, odd_in, even_in[1:])]
        full, made, ids, looked = gather_weights(weights, patches, angles, token_ids[0], table)
        even_pre, odd_pre, even0, odd0, even1, second_pre, stream0, enc_normed, q, k_all, v_all = made[:11]
        enc_mixed, enc_lse = made[11:]
    else:
        full = gather_plain(weights)
        conv1, conv2 = full[0].reshape(-1, D), full[1]
        even_pre, odd_pre = mm(even_in, conv1), mm(odd_in, conv1)
        even = jnp.where(even_keep, gelu(even_pre), 0.0).astype(BF)
        odd0 = jnp.where(odd_keep, gelu(odd_pre), 0.0).astype(BF)[:frames]
        even0, even1 = even[:frames], even[1:]
        second_pre = mm(even0, conv2[0]) + mm(odd0, conv2[1]) + mm(even1, conv2[2])
        stream0 = gelu(second_pre) + angles
        enc_normed = norm(stream0, full[2].astype(F32), full[3].astype(F32))
        q = (mm(enc_normed, full[4]) * SCALE).astype(BF)
        k, v = mm(enc_normed, full[5], BF), mm(enc_normed, full[6], BF)
        enc_mixed, enc_lse, k_all, v_all = clip_attend(q, k, v)
        ids = lax.all_gather(token_ids[0], BOTH, axis=0, tiled=True)
        looked = lax.psum_scatter(mm(one_hot(ids, table), table, BF), "dp", scatter_dimension=0, tiled=True)
        looked = lax.all_gather(looked, "seq", axis=0, tiled=True)
        looked = looked.reshape(seqs, all_slots, D // seqs).transpose(1, 0, 2).reshape(all_slots, D)
    vec = {i: full[i].astype(F32) for i in range(32) if KINDS[i] == "v"}
    conv1, conv2, position = full[0].reshape(-1, D), full[1], full[15]
    eo = full[7]
    ee, ec = full[10:12]
    dq_w, dk_w, dv_w, do_w = full[18:22]
    cq_w, ck_w, cv_w, co_w = full[24:28]
    de, dc = full[30:32]


    stream1 = stream0 + mm(enc_mixed, eo)
    enc_mlp_normed, enc_pre, enc_hidden, stream2 = mlp(stream1, vec[8], vec[9], ee, ec)
    memory = norm(stream2, vec[12], vec[13])
    mk = mm(memory, ck_w, BF)
    mv = mm(memory, cv_w, BF)

    place = jnp.arange(all_slots)
    embedded = looked.astype(F32) + position.astype(F32)
    dec_normed = norm(embedded, vec[16], vec[17])
    sq = (mm(dec_normed, dq_w) * SCALE).astype(BF)
    sk = mm(dec_normed, dk_w, BF)
    sv = mm(dec_normed, dv_w, BF)
    dec_mixed, dec_lse = attend(sq, sk, sv, token_counts)
    stream4 = embedded + mm(dec_mixed, do_w)
    cross_normed = norm(stream4, vec[22], vec[23])
    xq = (mm(cross_normed, cq_w) * SCALE).astype(BF)

    parts, lses = cross_attend(xq, mk, mv)
    lses = lax.dynamic_slice_in_dim(lses, me * slots, slots, 2).transpose(0, 2, 1)
    top = jnp.max(lses, axis=0)
    share = jnp.exp(lses - top)
    total = jnp.sum(share, axis=0)
    cross_lse = top + jnp.log(total)
    share = share / total
    cross_mixed = jnp.sum(
        parts.astype(F32).reshape(seqs, slots, HEADS, HEAD) * share[..., None], axis=0
    ).reshape(slots, D)
    cross_mixed = cross_mixed.astype(BF)

    own = lambda a: lax.dynamic_slice_in_dim(a, me * slots, slots, 0)
    stream4 = own(stream4)
    stream5 = stream4 + mm(cross_mixed, co_w)
    dec_mlp_normed, dec_pre, dec_hidden, stream6 = mlp(stream5, vec[28], vec[29], de, dc)
    live = (own(place) < token_counts[0])[:, None]
    decoded = jnp.where(live, stream6, 0.0).astype(BF)

    grads = [None] * 32

    def mlp_back(ex, co, gain, normed, pre, hidden, stream, up):
        up, d_low, d_pre, d_gain, d_bias = mlp_backward(up, stream, vec[gain], pre, full[ex], full[co])
        grads[co], grads[ex] = (hidden, d_low), (normed, d_pre)
        grads[gain], grads[gain + 1] = d_gain[0], d_bias[0]
        return up

    up = jnp.where(live, cotangent.astype(F32), 0.0)
    up = mlp_back(30, 31, 28, dec_mlp_normed, dec_pre, dec_hidden, stream5, up)
    d_low = up.astype(BF)
    grads[27] = (cross_mixed, d_low)
    d_mixed = mm_t(d_low, co_w, BF)
    d_mixed, lse_all = unpack(lax.all_gather(pack(d_mixed, cross_lse.T), "seq", axis=0, tiled=True))
    lse_all = lse_all.T
    dxq, dmk, dmv = cross_back(xq, mk, mv, d_mixed, lse_all)
    dxq = (low(dxq) * SCALE).astype(BF)
    grads[24] = (own(cross_normed), dxq)
    back, grads[22], grads[23] = norm_back(stream4, vec[22], mm_t(dxq, cq_w))
    up = up + back
    d_low = up.astype(BF)
    grads[21] = (own(dec_mixed), d_low)
    d_mixed = mm_t(d_low, do_w, BF)
    dsq, dsk, dsv = clip_rows_back(sq, sk, sv, d_mixed, dec_lse, token_counts)

    def inputs_back(first, gain, normed, stream, dq, dk, dv, up):
        dq = (dq.astype(F32) * SCALE).astype(BF)
        total = 0.0
        for i, g in enumerate((dq, dk, dv)):
            grads[first + i] = (normed, g)
            total = total + mm_t(g, full[first + i])
        back, grads[gain], grads[gain + 1] = norm_back(stream, vec[gain], total)
        return up + back

    up = inputs_back(18, 16, own(dec_normed), own(embedded), own(dsq), own(dsk), own(dsv), up)

    cols = exchange_columns(up.astype(BF))

    grads[25] = (memory, dmk)
    grads[26] = (memory, dmv)
    up, grads[12], grads[13] = norm_back(stream2, vec[12], mm_t(dmk, ck_w) + mm_t(dmv, cv_w))
    up = mlp_back(10, 11, 8, enc_mlp_normed, enc_pre, enc_hidden, stream1, up)
    d_low = up.astype(BF)
    grads[7] = (enc_mixed, d_low)
    d_mixed = mm_t(d_low, eo, BF)
    dq, dk, dv = clip_attend_back(q, k_all, v_all, d_mixed, enc_lse)
    up = inputs_back(4, 2, enc_normed, stream0, dq, dk, dv, up)

    d_second = (gelu_slope(second_pre) * up).astype(BF)
    grads[1] = ([even0, odd0, even1], d_second)
    rim = extended(d_second, 1)
    padded = even_pre.shape[0]
    rim = jnp.pad(rim, ((0, padded + 1 - rim.shape[0]), (0, 0)))
    row = jnp.arange(padded)[:, None]
    even_keep = ((row > 0) | (me > 0)) & (row < n)
    odd_keep = (row < n - 1) | ((me < seqs - 1) & (row < n))
    d_even = mm_t(rim[1:], conv2[0]) + mm_t(rim[:padded], conv2[2])
    d_odd = mm_t(rim[1:], conv2[1])
    d_even = jnp.where(even_keep, gelu_slope(even_pre) * low(d_even), 0.0).astype(BF)
    d_odd = jnp.where(odd_keep, gelu_slope(odd_pre) * low(d_odd), 0.0).astype(BF)
    grads[0] = (outer(odd_in[:frames], d_odd[:frames], F32) + outer(even_in[1:], d_even[1:n], F32)).reshape(
        3, mels, D
    )
    me_g, mo_g = mm_t(d_even, conv1), mm_t(d_odd, conv1)
    mel_grad = jnp.concatenate(
        [
            me_g[1:n, :mels] + me_g[: n - 1, 2 * mels :] + mo_g[: n - 1, mels : 2 * mels],
            me_g[1:n, mels : 2 * mels] + mo_g[1:n, :mels] + mo_g[: n - 1, 2 * mels :],
        ],
        axis=1,
    ).reshape(1, 2 * frames, mels)

    every = lax.all_gather(cols, "dp", axis=0, tiled=True)
    done = (reduce_grads if fast else reduce_plain)(grads, shards)
    done[14] = dot(one_hot(ids, table), every, 0, 0)
    per_clip = every.reshape(dps, dps, -1, D // seqs)
    done[15] = jnp.sum(
        lax.dynamic_index_in_dim(per_clip, lax.axis_index("dp"), 1, False).astype(F32), axis=0
    )
    return tuple([decoded[None], mel_grad] + done)


def exchange_columns(v):
    n = lax.axis_size("seq")
    wide = v.shape[1] // n
    v = v.reshape(v.shape[0], n, wide).transpose(1, 0, 2)
    return lax.all_to_all(v, "seq", split_axis=0, concat_axis=0, tiled=True).reshape(-1, wide)


def solution(mesh):
    place = {
        "1": P(None, "seq", "dp"),
        "2": P(None, "dp", "seq"),
        "v": P(BOTH),
        "m": P("dp", "seq"),
        "t": P("dp", "seq"),
    }
    rows = P("dp", "seq", None)
    weights = tuple(place[k] for k in KINDS)
    return jax.shard_map(
        body,
        mesh=mesh,
        in_specs=(rows, P("dp", "seq"), P("dp")) + weights + (rows,),
        out_specs=(rows, rows) + weights,
        check_vma=False,
    )
```
